32 devices in a mesh: batch: 16 (over z, y, x), heads: 2 (over core).
Axes of the slice: x: 2, y: 2, z: 4, core: 2. Of those that a mesh axis runs over, the one named last changes fastest.
Arguments:
- text_states: bfloat16 [64, 128, 768], P(('batch', 'heads')), may hold values from -6 to 6
- image_states: bfloat16 [64, 104, 1024], P(('batch', 'heads')), may hold values from -6 to 6
- caption_lengths: int32 [64], P('batch'), may hold values from 16 to 128, as said below
- region_counts: int32 [64], P('batch'), may hold values from 20 to 101, as said below
- text_query: bfloat16 [768, 1024], replicated, may hold values from -0.21875 to 0.21875
- text_key: bfloat16 [768, 1024], replicated, may hold values from -0.21875 to 0.21875
- text_value: bfloat16 [768, 1024], replicated, may hold values from -0.21875 to 0.21875
- text_output: bfloat16 [1024, 768], replicated, may hold values from -0.75 to 0.75
- text_up: bfloat16 [768, 3072], replicated, may hold values from -0.21875 to 0.21875
- text_down: bfloat16 [3072, 768], replicated, may hold values from -0.109375 to 0.109375
- text_gains: float32 [2, 768], replicated, may hold values from 0.25 to 1.75
- text_shifts: float32 [2, 768], replicated, may hold values from -1 to 1
- image_query: bfloat16 [1024, 1024], replicated, may hold values from -0.1875 to 0.1875
- image_key: bfloat16 [1024, 1024], replicated, may hold values from -0.1875 to 0.1875
- image_value: bfloat16 [1024, 1024], replicated, may hold values from -0.1875 to 0.1875
- image_output: bfloat16 [1024, 1024], replicated, may hold values from -0.75 to 0.75
- image_up: bfloat16 [1024, 1024], replicated, may hold values from -0.1875 to 0.1875
- image_down: bfloat16 [1024, 1024], replicated, may hold values from -0.1875 to 0.1875
- image_gains: float32 [2, 1024], replicated, may hold values from 0.25 to 1.75
- image_shifts: float32 [2, 1024], replicated, may hold values from -1 to 1
- text_upstream: bfloat16 [64, 128, 768], P(('batch', 'heads')), may hold values from -6 to 6
- image_upstream: bfloat16 [64, 104, 1024], P(('batch', 'heads')), may hold values from -6 to 6
Outputs:
- text_result: bfloat16 [64, 128, 768], P(('batch', 'heads'))
- image_result: bfloat16 [64, 104, 1024], P(('batch', 'heads'))
- text_states_grad: bfloat16 [64, 128, 768], P(('batch', 'heads'))
- image_states_grad: bfloat16 [64, 104, 1024], P(('batch', 'heads'))
- text_query_grad: float32 [768, 1024], P(('batch', 'heads'))
- text_key_grad: float32 [768, 1024], P(('batch', 'heads'))
- text_value_grad: float32 [768, 1024], P(('batch', 'heads'))
- text_output_grad: float32 [1024, 768], P(None, ('batch', 'heads'))
- text_up_grad: float32 [768, 3072], P(('batch', 'heads'))
- text_down_grad: float32 [3072, 768], P(None, ('batch', 'heads'))
- text_gains_grad: float32 [2, 768], P(None, ('batch', 'heads'))
- text_shifts_grad: float32 [2, 768], P(None, ('batch', 'heads'))
- image_query_grad: float32 [1024, 1024], P(('batch', 'heads'))
- image_key_grad: float32 [1024, 1024], P(('batch', 'heads'))
- image_value_grad: float32 [1024, 1024], P(('batch', 'heads'))
- image_output_grad: float32 [1024, 1024], P(None, ('batch', 'heads'))
- image_up_grad: float32 [1024, 1024], P(('batch', 'heads'))
- image_down_grad: float32 [1024, 1024], P(None, ('batch', 'heads'))
- image_gains_grad: float32 [2, 1024], P(None, ('batch', 'heads'))
- image_shifts_grad: float32 [2, 1024], P(None, ('batch', 'heads'))
The draws below stay inside these ranges and needn't reach their ends.
Inputs may be any that keep to these rules, and one draw needn't show every extreme that they name: `caption_lengths`: some pair has exactly 128 caption tokens. `region_counts`: some pair has exactly 101 regions; region slots from a pair's count up to 104 are padding.
All inputs are finite; a program needn't handle non-finite values.
Results may differ from the reference program's by a relative error of at most 0.013.
Values may be sent and summed in bfloat16 or wider, within the bound.
A program may use at most 256 MiB of HBM per device.

```python
import math
import jax
import jax.numpy as jnp
from jax import lax

TEXT_DIM = 768
TEXT_FF = 3072
IMAGE_DIM = 1024
IMAGE_FF = 1024
CO_HEADS = 8
HEAD_DIM = 128
CAP_SLOTS = 128
REGION_MOST = 101
INNER = 1024
REGION_SLOTS = 104
PAIRS = 64


def draw_caption_lengths(key, part):
    subkeys = jax.random.split(jax.random.fold_in(key, 11), 2)
    low_end = max(2, CAP_SLOTS // 8)
    values = jax.random.randint(subkeys[0], (PAIRS,), low_end, CAP_SLOTS + 1)
    chosen = jax.random.randint(subkeys[1], (), 0, PAIRS)
    return values.at[chosen].set(CAP_SLOTS).astype(jnp.int32)


def draw_region_counts(key, part):
    subkeys = jax.random.split(jax.random.fold_in(key, 23), 4)
    floor_count = REGION_MOST // 5
    middle = REGION_MOST * 5 // 7
    common = jax.random.randint(subkeys[0], (PAIRS,), floor_count, middle)
    heavy_tail = jax.random.randint(subkeys[1], (PAIRS,), middle, REGION_MOST + 1)
    choose_heavy = jax.random.randint(subkeys[2], (PAIRS,), 0, 4)
    values = jnp.where(choose_heavy == 0, heavy_tail, common)
    chosen = jax.random.randint(subkeys[3], (), 0, PAIRS)
    return values.at[chosen].set(REGION_MOST).astype(jnp.int32)


def strengthened(result, key, source, target, blocks, factor):
    owner, partner = [(jnp.arange(result.shape[axis_at]) // (result.shape[axis_at] // blocks)).reshape([-1 if axis == axis_at else 1 for axis in range(result.ndim)]) for axis_at in (source, target)]
    chosen = jax.random.permutation(key, blocks)[partner]
    strong = (owner == chosen) | (owner == (partner + blocks // 2) % blocks)
    return jnp.where(strong, factor * result, result)


def levels(key, extent, shards, least, largest):
    loudness, own = 1.0, jax.random.fold_in(key, 6)
    for axis_at, parts in shards:
        steps = jnp.exp(jax.random.uniform(jax.random.fold_in(own, axis_at), (parts,), jnp.float32, least / len(shards), largest / len(shards)))
        loudness = loudness * jnp.repeat(steps, extent[axis_at] // parts).reshape([-1 if axis == axis_at else 1 for axis in range(len(extent))])
    return loudness


def normal_values(key, shape, scale, limit, cuts=(), dtype=jnp.bfloat16):
    values = jax.random.normal(key, shape, jnp.float32) * scale
    if len(cuts) > 0:
        values = levels(key, shape, cuts, -0.22, 0.18) * values
    return jnp.clip(values, min=-limit, max=limit).astype(dtype)


def gaussian_with(own_key, dims, width, bound, cuts, heavy, dtype=jnp.bfloat16):
    values = width * jax.random.normal(own_key, dims, jnp.float32)
    if cuts:
        values = values * levels(own_key, dims, cuts, -0.22, 0.18)
    return jnp.clip(strengthened(values, jax.random.fold_in(own_key, 3), *heavy), -bound, bound).astype(dtype)


def setup_inputs(seed: int = 0) -> dict:
    arg_keys = jax.random.split(jax.random.key(seed), 23)
    return {
        "text_states": normal_values(arg_keys[0], (PAIRS, CAP_SLOTS, TEXT_DIM), 1.0, 6.0, ((0, 32),)),
        "image_states": normal_values(arg_keys[1], (PAIRS, REGION_SLOTS, IMAGE_DIM), 1.0, 6.0, ((0, 32),)),
        "caption_lengths": draw_caption_lengths(jax.random.fold_in(arg_keys[22], 71), 0),
        "region_counts": draw_region_counts(jax.random.fold_in(arg_keys[22], 71), 0),
        "text_query": normal_values(arg_keys[4], (TEXT_DIM, INNER), TEXT_DIM ** -0.5, 0.21875),
        "text_key": normal_values(arg_keys[5], (TEXT_DIM, INNER), TEXT_DIM ** -0.5, 0.21875),
        "text_value": normal_values(arg_keys[6], (TEXT_DIM, INNER), TEXT_DIM ** -0.5, 0.21875),
        "text_output": normal_values(arg_keys[7], (INNER, TEXT_DIM), (INNER // 16) ** -0.5, 0.75),
        "text_up": normal_values(arg_keys[8], (TEXT_DIM, TEXT_FF), TEXT_DIM ** -0.5, 0.21875),
        "text_down": normal_values(arg_keys[9], (TEXT_FF, TEXT_DIM), TEXT_FF ** -0.5, 0.109375),
        "text_gains": jnp.clip(1.0 + 0.15 * jax.random.normal(arg_keys[10], (2, TEXT_DIM), jnp.float32), 0.25, 1.75),
        "text_shifts": normal_values(arg_keys[11], (2, TEXT_DIM), 0.2, 1.0, (), jnp.float32),
        "image_query": normal_values(arg_keys[12], (IMAGE_DIM, INNER), IMAGE_DIM ** -0.5, 0.1875),
        "image_key": normal_values(arg_keys[13], (IMAGE_DIM, INNER), IMAGE_DIM ** -0.5, 0.1875),
        "image_value": normal_values(arg_keys[14], (IMAGE_DIM, INNER), IMAGE_DIM ** -0.5, 0.1875),
        "image_output": normal_values(arg_keys[15], (INNER, IMAGE_DIM), (INNER // 16) ** -0.5, 0.75),
        "image_up": normal_values(arg_keys[16], (IMAGE_DIM, IMAGE_FF), IMAGE_DIM ** -0.5, 0.1875),
        "image_down": normal_values(arg_keys[17], (IMAGE_FF, IMAGE_DIM), IMAGE_FF ** -0.5, 0.1875),
        "image_gains": jnp.clip(1.0 + 0.15 * jax.random.normal(arg_keys[18], (2, IMAGE_DIM), jnp.float32), 0.25, 1.75),
        "image_shifts": normal_values(arg_keys[19], (2, IMAGE_DIM), 0.2, 1.0, (), jnp.float32),
        "text_upstream": gaussian_with(arg_keys[20], (PAIRS, CAP_SLOTS, TEXT_DIM), 1.0, 6.0, ((0, 32),), (0, 2, 32, 2.75)),
        "image_upstream": gaussian_with(arg_keys[21], (PAIRS, REGION_SLOTS, IMAGE_DIM), 1.0, 6.0, ((0, 32),), (0, 2, 32, 2.75)),
    }


@jax.custom_vjp
def low(v):
    return lax.optimization_barrier(v.astype(jnp.bfloat16)).astype(jnp.float32)

@jax.custom_vjp
def low_back(v):
    return v

def low_keep(v):
    return (low(v), None)

def low_pass(kept, grad):
    return (grad,)

def back_keep(v):
    return (v, None)

def back_low(kept, grad):
    return (low(grad),)
low.defvjp(low_keep, low_pass)
low_back.defvjp(back_keep, back_low)
EPS = 1e-05
NEG = -1000000000.0
PRECISE = lax.Precision.HIGHEST

def matmul_high(left, right):
    return jnp.dot(left, right, precision=PRECISE)

def layer_norm(values, gain, shift):
    row_mean = lax.optimization_barrier(jnp.mean(values, axis=-1, keepdims=True))
    centred = values - row_mean
    spread = lax.optimization_barrier(jnp.mean(centred * centred, axis=-1, keepdims=True))
    return centred * lax.rsqrt(spread + EPS) * gain + shift

def gelu_value(values):
    return 0.5 * values * (1.0 + jax.scipy.special.erf(values / math.sqrt(2.0)))

def cross_attend(queries, key_rows, value_rows, lengths):
    score_scale = 1.0 / math.sqrt(queries.shape[-1])
    scores = low_back(jnp.einsum('bqhd,bkhd->bhqk', queries, key_rows, precision=PRECISE) * score_scale)
    live_mask = lax.broadcasted_iota(jnp.int32, scores.shape, 3) < lengths.astype(jnp.int32)[:, None, None, None]
    scores = jnp.where(live_mask, scores, NEG)
    row_top = lax.optimization_barrier(jnp.max(scores, axis=-1, keepdims=True))
    weights = jnp.exp(scores - row_top)
    probability = weights / lax.optimization_barrier(jnp.sum(weights, axis=-1, keepdims=True))
    context = jnp.einsum('bhqk,bkhd->bqhd', low(probability), value_rows, precision=PRECISE)
    return low_back(low(context))

def split_heads(row_values, weight, pair_count):
    return low_back(low(matmul_high(row_values, weight))).reshape(pair_count, -1, CO_HEADS, HEAD_DIM)

def finish_stream(row_values, context, out_weight, up_weight, down_weight, gains, shifts):
    attended = low_back(matmul_high(context, out_weight))
    normed = layer_norm(row_values + attended, gains[0], shifts[0])
    active = gelu_value(low_back(matmul_high(low(normed), up_weight)))
    branch = low_back(matmul_high(low(active), down_weight))
    return layer_norm(normed + branch, gains[1], shifts[1])

def block_forward(text_block, image_block, caption, regions, params):
    w_tq, w_tk, w_tv, w_to, w_tu, w_td, text_gain, text_shift, w_iq, w_ik, w_iv, w_io, w_iu, w_id, image_gain, image_shift = params
    pair_count = text_block.shape[0]
    text_rows = text_block.reshape(-1, TEXT_DIM)
    image_rows = image_block.reshape(-1, IMAGE_DIM)
    text_context = cross_attend(split_heads(text_rows, w_tq, pair_count), split_heads(image_rows, w_ik, pair_count), split_heads(image_rows, w_iv, pair_count), regions)
    image_context = cross_attend(split_heads(image_rows, w_iq, pair_count), split_heads(text_rows, w_tk, pair_count), split_heads(text_rows, w_tv, pair_count), caption)
    text_out = finish_stream(text_rows, text_context.reshape(text_rows.shape[0], INNER), w_to, w_tu, w_td, text_gain, text_shift)
    image_out = finish_stream(image_rows, image_context.reshape(image_rows.shape[0], INNER), w_io, w_iu, w_id, image_gain, image_shift)
    return (text_out.reshape(text_block.shape), image_out.reshape(image_block.shape))

def reference(text_states, image_states, caption_lengths, region_counts, text_query, text_key, text_value, text_output, text_up, text_down, text_gains, text_shifts, image_query, image_key, image_value, image_output, image_up, image_down, image_gains, image_shifts, text_upstream, image_upstream):
    pair_block = 16
    block_count = text_states.shape[0] // pair_block
    caption = caption_lengths.astype(jnp.int32).reshape(block_count, pair_block)
    regions = region_counts.astype(jnp.int32).reshape(block_count, pair_block)

    def forward(text_in, image_in, *params):

        def one_block(block):
            text_block, image_block, caption_block, region_block = block
            return block_forward(text_block, image_block, caption_block, region_block, params)
        text_out, image_out = lax.map(jax.checkpoint(one_block), (text_in.reshape(block_count, pair_block, CAP_SLOTS, TEXT_DIM), image_in.reshape(block_count, pair_block, REGION_SLOTS, IMAGE_DIM), caption, regions))
        return (text_out.reshape(text_in.shape), image_out.reshape(image_in.shape))
    floats = tuple((array.astype(jnp.float32) for array in (text_states, image_states, text_query, text_key, text_value, text_output, text_up, text_down, text_gains, text_shifts, image_query, image_key, image_value, image_output, image_up, image_down, image_gains, image_shifts)))
    results, pullback = jax.vjp(forward, *floats)
    gradients = pullback((text_upstream.astype(jnp.float32), image_upstream.astype(jnp.float32)))
    text_in_grad, image_in_grad, g_tq, g_tk, g_tv, g_to, g_tu, g_td, g_tg, g_ts, g_iq, g_ik, g_iv, g_io, g_iu, g_id, g_ig, g_is = gradients
    return (results[0].astype(jnp.bfloat16), results[1].astype(jnp.bfloat16), text_in_grad.astype(jnp.bfloat16), image_in_grad.astype(jnp.bfloat16), g_tq, g_tk, g_tv, g_to, g_tu, g_td, g_tg, g_ts, g_iq, g_ik, g_iv, g_io, g_iu, g_id, g_ig, g_is)
```

```python
import functools
import math

import jax
import jax.numpy as jnp
from jax import lax
from jax.experimental import pallas as pl
from jax.experimental.pallas import tpu as pltpu
from jax.sharding import PartitionSpec as P

MESH_ID = pl.DeviceIdType.MESH
F32 = jnp.float32
BF16 = jnp.bfloat16


def plan(cw, t_cols, i_cols):
    text = [(w, o) for w, n in enumerate(t_cols) for o in range(0, n // 2, cw)]
    image = [(w, o) for w, n in enumerate(i_cols) for o in range(0, n // 2, cw)]
    return text, image


def grad_kernel(cfg, *refs):
    (nz, ny, nx, cw, t_left, i_left, t_cols, i_cols, order) = cfg
    n_t, n_i = len(t_cols), len(i_cols)
    n_tl, n_il = cfg_lefts(t_left), cfg_lefts(i_left)
    refs = list(refs)

    def take(n):
        got = refs[:n]
        del refs[:n]
        return got

    tl, tr, il, ir = take(n_tl), take(n_t), take(n_il), take(n_i)
    (small_ref,) = take(1)
    out_t, out_i, out_s = take(3)
    lt2, li2, ltt, lit = take(4)
    rt, ri = take(n_t), take(n_i)
    gt, gi, r1t, r1i, r2t, r2i, rut, rui, rdt, rdi, fint, fini = take(12)
    sv, sr = take(2)
    loc_sem, ex_s, ex_r, st_s, st_r, sm_s, sm_r = take(7)
    assert not refs

    b = lax.axis_index("batch")
    h = lax.axis_index("heads")
    x = lax.rem(b, nx)
    y = lax.rem(lax.div(b, nx), ny)
    z = lax.div(b, nx * ny)

    def dev(zz, yy, xx):
        return ((zz * ny + yy) * nx + xx, h)

    partner = (b, 1 - h)
    nbr_x, nbr_y = dev(z, y, 1 - x), dev(z, 1 - y, x)

    barrier = pltpu.get_barrier_semaphore()
    for who in (partner, nbr_x, nbr_y):
        pl.semaphore_signal(barrier, inc=1, device_id=who, device_id_type=MESH_ID)
    for off in range(1, nz):
        pl.semaphore_signal(
            barrier, inc=1, device_id=dev(lax.rem(z + off, nz), y, x), device_id_type=MESH_ID
        )
    pl.semaphore_wait(barrier, 3 + nz - 1)

    def remote(src, dst, ssem, rsem, who):
        return pltpu.make_async_remote_copy(
            src_ref=src, dst_ref=dst, send_sem=ssem, recv_sem=rsem, device_id=who, device_id_type=MESH_ID
        )

    t_rows, i_rows = tl[0].shape[0], il[0].shape[0]
    ex, k = [], 0
    lefts = [(tl[i], lt2.at[i], t_rows) for i in range(n_tl)] + [(il[i], li2.at[i], i_rows) for i in range(n_il)]
    ex_left, ex_right = {}, {}
    for idx, (src, dst, rows) in enumerate(lefts):
        here = pltpu.make_async_copy(src, dst.at[pl.ds(0, rows)], loc_sem.at[k])
        there = remote(src, dst.at[pl.ds(rows, rows)], ex_s.at[k], ex_r.at[k], partner)
        ex_left[idx] = (here, there)
        k += 1
    rights = [(tr[i], rt[i], t_rows, t_cols[i] // 2) for i in range(n_t)] + [
        (ir[i], ri[i], i_rows, i_cols[i] // 2) for i in range(n_i)
    ]
    for idx, (src, dst, rows, half) in enumerate(rights):
        mine = pl.ds(pl.multiple_of(h * half, 128), half)
        other = pl.ds(pl.multiple_of((1 - h) * half, 128), half)
        here = pltpu.make_async_copy(src.at[:, mine], dst.at[pl.ds(0, rows)], loc_sem.at[k])
        there = remote(src.at[:, other], dst.at[pl.ds(rows, rows)], ex_s.at[k], ex_r.at[k], partner)
        ex_right[idx] = (here, there)
        k += 1
    started = []
    done_left, done_right = set(), set()
    text_plan, image_plan = plan(cw, t_cols, i_cols)
    chunks = []
    for stream, idx, way in order:
        w, o = (text_plan if stream == 0 else image_plan)[idx]
        left = t_left[w] if stream == 0 else n_tl + i_left[w]
        right = w if stream == 0 else n_t + w
        chunks.append((stream, idx, left, right, o, way))
    for stream, idx, left, right, o, way in chunks:
        for key, table in ((left, ex_left), (right, ex_right)):
            if (key, id(table)) not in started:
                started.append((key, id(table)))
                table[key][0].start()
                table[key][1].start()

    small_copies = []

    def small_start(src, dst, i, who):
        c = remote(src, dst, sm_s.at[i], sm_r.at[i], who)
        c.start()
        small_copies.append(c)

    small_start(small_ref, sr.at[0], 0, partner)

    def small_step(step):
        if step == 0:
            small_copies[0].wait_recv()
            sv[0] = small_ref[...] + sr[0]
            small_start(sv.at[0], sr.at[1], 1, nbr_x)
        elif step == 1:
            small_copies[1].wait_recv()
            sv[1] = sv[0] + sr[1]
            small_start(sv.at[1], sr.at[2], 2, nbr_y)
        elif step == 2:
            small_copies[2].wait_recv()
            sv[2] = sv[1] + sr[2]
            for off in range(1, nz):
                small_start(sv.at[2], sr.at[2 + off], 2 + off, dev(lax.rem(z + off, nz), y, x))
        elif step == 3:
            total = sv[2]
            for off in range(1, nz):
                small_copies[2 + off].wait_recv()
                total = total + sr[2 + off]
            out_s[...] = total

    def bufs(c):
        stream, idx = chunks[c][0], chunks[c][1]
        if stream == 0:
            return gt.at[idx], r1t.at[idx], r2t.at[idx], rut.at[idx], rdt.at[idx], fint.at[idx], out_t
        return gi.at[idx], r1i.at[idx], r2i.at[idx], rui.at[idx], rdi.at[idx], fini.at[idx], out_i

    def need(key, table, done, transposed, src):
        if key in done:
            return
        done.add(key)
        table[key][0].wait()
        table[key][1].wait_recv()
        if transposed is not None:
            rows, cols = src.shape

            def body(j, carry):
                s = pl.ds(pl.multiple_of(j * 256, 256), 256)
                transposed[s, :] = src[:, s].T
                return carry

            lax.fori_loop(0, cols // 256, body, 0)

    def compute(c):
        stream, idx, left, right, o, way = chunks[c]
        if left < n_tl:
            lref, traw = ltt.at[left], lt2.at[left]
        else:
            lref, traw = lit.at[left - n_tl], li2.at[left - n_tl]
        need(left, ex_left, done_left, lref, traw)
        need(right, ex_right, done_right, None, None)
        rref = rt[right] if stream == 0 else ri[right - n_t]
        g = bufs(c)[0]
        blk = g.shape[-2]
        step = ny * nx * blk

        def body(i, carry):
            rows = lref[pl.ds(pl.multiple_of(i * step, 16), step), :]
            res = jnp.dot(rows, rref[:, pl.ds(o, cw)], preferred_element_type=F32)
            g[i] = res.astype(BF16).reshape(ny, nx, blk, cw)
            return carry

        lax.fori_loop(0, nz, body, 0)

    def add(dst, *srcs):
        total = dst[...].astype(F32)
        for s in srcs:
            total = total + s[...].astype(F32)
        dst[...] = total.astype(BF16)

    n = len(chunks)

    def s1(c):
        g, r1 = bufs(c)[:2]
        if chunks[c][5] == "x":
            return remote(g.at[:, :, 1 - x], r1, st_s.at[0, c], st_r.at[0, c], nbr_x)
        return remote(g.at[:, 1 - y], r1, st_s.at[0, c], st_r.at[0, c], nbr_y)

    def s2(c):
        g, _, r2 = bufs(c)[:3]
        if chunks[c][5] == "x":
            return remote(g.at[:, 1 - y, x], r2, st_s.at[1, c], st_r.at[1, c], nbr_y)
        return remote(g.at[:, y, 1 - x], r2, st_s.at[1, c], st_r.at[1, c], nbr_x)

    def up(c, k):
        g, ru = bufs(c)[0], bufs(c)[3]
        return remote(
            g.at[pl.ds(k + 1, nz - 1 - k), y, x], ru.at[pl.ds(k + 1, nz - 1 - k)],
            st_s.at[2, c], st_r.at[2, c], dev(k + 1, y, x),
        )

    def down(c, k):
        g, rd = bufs(c)[0], bufs(c)[4]
        return remote(
            g.at[pl.ds(0, k), y, x], rd.at[pl.ds(0, k)], st_s.at[3, c], st_r.at[3, c], dev(k - 1, y, x)
        )

    def fin(c):
        stream, idx = chunks[c][0], chunks[c][1]
        f, out = bufs(c)[5], bufs(c)[6]
        r = out.shape[1]
        return remote(
            f.at[pl.ds(pl.multiple_of((1 - h) * r, 8), r)], out.at[h * (out.shape[0] // 2) + idx],
            st_s.at[4, c], st_r.at[4, c], partner,
        )

    def stage1(c):
        s1(c).start()

    def stage2(c):
        s1(c).wait_recv()
        g, r1 = bufs(c)[:2]

        def body(i, carry):
            if chunks[c][5] == "x":
                for j in range(ny):
                    add(g.at[i, j, x], r1.at[i, j])
            else:
                for j in range(nx):
                    add(g.at[i, y, j], r1.at[i, j])
            return carry

        lax.fori_loop(0, nz, body, 0)
        s2(c).start()

    def stage3(c):
        s2(c).wait_recv()
        g, _, r2 = bufs(c)[:3]

        def body(i, carry):
            add(g.at[i, y, x], r2.at[i])
            return carry

        lax.fori_loop(0, nz, body, 0)

        @pl.when(z == 0)
        def _():
            up(c, 0).start()

        @pl.when(z == nz - 1)
        def _():
            down(c, nz - 1).start()

    def hop(c, d):
        g, _, _, ru, rd = bufs(c)[:5]

        @pl.when(z == d)
        def _():
            up(c, d - 1).wait_recv()
            for t in range(d + 1, nz):
                add(g.at[t, y, x], ru.at[t])
            up(c, d).start()

        @pl.when(z == nz - 1 - d)
        def _():
            down(c, nz - d).wait_recv()
            for t in range(0, nz - 1 - d):
                add(g.at[t, y, x], rd.at[t])
            down(c, nz - 1 - d).start()

    def finish(c):
        g, _, _, ru, rd, f, out = bufs(c)
        for k in range(nz):

            @pl.when(z == k)
            def _(k=k):
                if k == nz - 1:
                    up(c, k - 1).wait_recv()
                if k == 0:
                    down(c, 1).wait_recv()
                total = g[k, y, x].astype(F32)
                if k > 0:
                    total = total + ru[k].astype(F32)
                if k < nz - 1:
                    total = total + rd[k].astype(F32)
                f[...] = total

        r = out.shape[1]
        half = out.shape[0] // 2
        out[h * half + chunks[c][1]] = f[pl.ds(pl.multiple_of(h * r, 8), r), :]
        fin(c).start()

    pairs = n // 2
    lag = {"s1": 0, "s2": 1, "s3": 2, "h1": 3, "h2": 4, "fin": 5}
    for t in range(pairs + 6):
        def each(stage, fn):
            p = t - lag[stage]
            if 0 <= p < pairs:
                fn(2 * p)
                fn(2 * p + 1)

        if t == 0:
            for c in (0, 1):
                compute(c)
                stage1(c)
        if t + 1 < pairs:
            for c in (2 * t + 2, 2 * t + 3):
                compute(c)
                stage1(c)
        each("s2", stage2) if False else None
        p = t
        if p < pairs:
            stage2(2 * p)
            stage2(2 * p + 1)
        p = t - 1
        if 0 <= p < pairs:
            stage3(2 * p)
            stage3(2 * p + 1)
        for d in range(1, nz - 1):
            p = t - 1 - d
            if 0 <= p < pairs:
                hop(2 * p, d)
                hop(2 * p + 1, d)
        p = t - nz + 0
        if 0 <= p < pairs:
            finish(2 * p)
            finish(2 * p + 1)
        if t < 4:
            small_step(t)

    for c in range(n):
        fin(c).wait_recv()
        s1(c).wait_send()
        s2(c).wait_send()
        fin(c).wait_send()
        for k in range(nz):

            @pl.when(z == k)
            def _(k=k):
                if k < nz - 1:
                    up(c, k).wait_send()
                if k > 0:
                    down(c, k).wait_send()
    for table in (ex_left, ex_right):
        for key in table:
            table[key][1].wait_send()
    for c in small_copies:
        c.wait_send()


def cfg_lefts(lefts):
    return max(lefts) + 1


def reduce_grads(mesh_dims, cw, t_left, i_left, order, tl, tr, il, ir, small):
    nz, ny, nx = mesh_dims
    chips = nz * ny * nx
    t_cols, i_cols = tuple(a.shape[1] for a in tr), tuple(a.shape[1] for a in ir)
    t_rows, i_rows = tl[0].shape[0], il[0].shape[0]
    t_dim, i_dim = tl[0].shape[1], il[0].shape[1]
    tb, ib = t_dim // chips, i_dim // chips
    text_plan, image_plan = plan(cw, t_cols, i_cols)
    ct, ci = len(text_plan), len(image_plan)
    assert len(order) == ct + ci and len(order) % 2 == 0
    n = ct + ci
    cfg = (nz, ny, nx, cw, t_left, i_left, t_cols, i_cols, order)
    n_ex = len(tl) + len(tr) + len(il) + len(ir)
    V, DMA = pltpu.VMEM, pltpu.SemaphoreType.DMA
    scratch = [
        V((len(tl), 2 * t_rows, t_dim), BF16),
        V((len(il), 2 * i_rows, i_dim), BF16),
        V((len(tl), t_dim, 2 * t_rows), BF16),
        V((len(il), i_dim, 2 * i_rows), BF16),
        *[V((2 * t_rows, c // 2), BF16) for c in t_cols],
        *[V((2 * i_rows, c // 2), BF16) for c in i_cols],
        V((ct, nz, ny, nx, tb, cw), BF16),
        V((ci, nz, ny, nx, ib, cw), BF16),
        V((ct, nz, 2, tb, cw), BF16),
        V((ci, nz, 2, ib, cw), BF16),
        V((ct, nz, tb, cw), BF16),
        V((ci, nz, ib, cw), BF16),
        V((ct, nz, tb, cw), BF16),
        V((ci, nz, ib, cw), BF16),
        V((ct, nz, tb, cw), BF16),
        V((ci, nz, ib, cw), BF16),
        V((ct, tb, cw), F32),
        V((ci, ib, cw), F32),
        V((3, *small.shape), F32),
        V((2 + nz, *small.shape), F32),
        DMA((n_ex,)),
        DMA((n_ex,)),
        DMA((n_ex,)),
        DMA((5, n)),
        DMA((5, n)),
        DMA((2 + nz,)),
        DMA((2 + nz,)),
    ]
    hbm = pl.BlockSpec(memory_space=pl.ANY)
    vm = pl.BlockSpec(memory_space=pltpu.VMEM)
    return pl.pallas_call(
        functools.partial(grad_kernel, cfg),
        out_shape=(
            jax.ShapeDtypeStruct((2 * ct, tb // 2, cw), F32),
            jax.ShapeDtypeStruct((2 * ci, ib // 2, cw), F32),
            jax.ShapeDtypeStruct(small.shape, F32),
        ),
        in_specs=[hbm] * n_ex + [vm],
        out_specs=(vm, vm, vm),
        scratch_shapes=scratch,
        compiler_params=pltpu.CompilerParams(
            collective_id=0, has_side_effects=True, vmem_limit_bytes=67000000
        ),
        name="grad_reduce",
    )(*tl, *tr, *il, *ir, small)


CO_HEADS = 8
HEAD_DIM = 128
EPS = 1e-05
NEG = -1000000000.0
CW = 512
LEFTS = (0, 1, 2, 3, 3, 3)


def chunk_order(n_text, n_image):
    order = [(0, i) for i in range(n_text)]
    lead = n_text - n_image
    image = [(1, i) for i in range(n_image)]
    mixed = order[:lead]
    rest = order[lead:]
    while rest or image:
        mixed += image[:2] + rest[:2]
        image, rest = image[2:], rest[2:]
    return tuple((s, i, "xy"[k % 2]) for k, (s, i) in enumerate(mixed))


def project(row_values, weight):
    return jnp.dot(row_values, weight, preferred_element_type=F32)


def project_back(gradient, weight):
    return lax.dot_general(gradient, weight, (((1,), (1,)), ((), ())), preferred_element_type=F32)


def outer_sum(row_values, gradient):
    return lax.dot_general(row_values, gradient, (((0,), (0,)), ((), ())), preferred_element_type=F32)


def layer_norm(values, gain, shift):
    row_mean = jnp.mean(values, axis=-1, keepdims=True)
    centred = values - row_mean
    spread = jnp.mean(centred * centred, axis=-1, keepdims=True)
    inverse = lax.rsqrt(spread + EPS)
    normed = centred * inverse
    return (normed * gain + shift, normed, inverse)


def norm_back(gradient, normed, inverse, gain):
    scaled = gradient * gain
    first_mean = jnp.mean(scaled, axis=-1, keepdims=True)
    second_mean = jnp.mean(scaled * normed, axis=-1, keepdims=True)
    into = inverse * (scaled - first_mean - normed * second_mean)
    return (into, jnp.sum(gradient * normed, axis=0), jnp.sum(gradient, axis=0))


def gelu_value(values):
    return 0.5 * values * (1.0 + jax.scipy.special.erf(values / math.sqrt(2.0)))


def gelu_slope(values):
    return 0.5 * (1.0 + jax.scipy.special.erf(values / math.sqrt(2.0))) + values * jnp.exp(
        -0.5 * values * values
    ) / math.sqrt(2.0 * math.pi)


def attend(queries, key_rows, value_rows, lengths):
    score_scale = 1.0 / math.sqrt(queries.shape[-1])
    scores = jnp.einsum("bqhd,bkhd->bhqk", queries, key_rows, preferred_element_type=F32) * score_scale
    live_mask = lax.broadcasted_iota(jnp.int32, scores.shape, 3) < lengths[:, None, None, None]
    scores = jnp.where(live_mask, scores, NEG)
    weights = jnp.exp(scores - jnp.max(scores, axis=-1, keepdims=True))
    probability = weights / jnp.sum(weights, axis=-1, keepdims=True)
    context = jnp.einsum("bhqk,bkhd->bqhd", probability.astype(BF16), value_rows, preferred_element_type=F32)
    return context.astype(BF16), probability


def attend_back(queries, key_rows, value_rows, probability, context_grad):
    score_scale = 1.0 / math.sqrt(queries.shape[-1])
    value_grad = jnp.einsum(
        "bhqk,bqhd->bkhd", probability.astype(BF16), context_grad, preferred_element_type=F32
    )
    prob_grad = jnp.einsum("bqhd,bkhd->bhqk", context_grad, value_rows, preferred_element_type=F32)
    row_inner = jnp.sum(probability * prob_grad, axis=-1, keepdims=True)
    score_grad = (probability * (prob_grad - row_inner)).astype(BF16)
    query_grad = jnp.einsum("bhqk,bkhd->bqhd", score_grad, key_rows, preferred_element_type=F32) * score_scale
    key_grad = jnp.einsum("bhqk,bqhd->bkhd", score_grad, queries, preferred_element_type=F32) * score_scale
    return (query_grad.astype(BF16), key_grad.astype(BF16), value_grad.astype(BF16))


def stream_forward(row_values, context, out_weight, up_weight, down_weight, gains, shifts):
    attended = project(context, out_weight)
    first_out, normed_one, inverse_one = layer_norm(row_values.astype(F32) + attended, gains[0], shifts[0])
    first_low = first_out.astype(BF16)
    before = project(first_low, up_weight)
    active = gelu_value(before).astype(BF16)
    second_out, normed_two, inverse_two = layer_norm(
        first_out + project(active, down_weight), gains[1], shifts[1]
    )
    kept_state = (normed_one, inverse_one, first_low, before, active, normed_two, inverse_two)
    return (second_out.astype(BF16), kept_state)


def stream_back(upstream, kept_state, out_weight, up_weight, down_weight, gains):
    normed_one, inverse_one, first_low, before, active, normed_two, inverse_two = kept_state
    branch_grad, gain_two, shift_two = norm_back(upstream.astype(F32), normed_two, inverse_two, gains[1])
    branch_low = branch_grad.astype(BF16)
    active_grad = project_back(branch_low, down_weight)
    before_grad = (active_grad * gelu_slope(before)).astype(BF16)
    first_grad = project_back(before_grad, up_weight) + branch_grad
    sum_grad, gain_one, shift_one = norm_back(first_grad, normed_one, inverse_one, gains[0])
    sum_low = sum_grad.astype(BF16)
    context_grad = project_back(sum_low, out_weight).astype(BF16)
    return sum_grad, context_grad, branch_low, before_grad, sum_low, (gain_one, gain_two, shift_one, shift_two)


def make_local(mesh):
    devices = mesh.shape["batch"] * mesh.shape["heads"]
    fast = mesh.shape["batch"] == 16 and mesh.shape["heads"] == 2

    def local(
        text_states, image_states, caption_lengths, region_counts,
        text_query, text_key, text_value, text_output, text_up, text_down, text_gains, text_shifts,
        image_query, image_key, image_value, image_output, image_up, image_down, image_gains, image_shifts,
        text_upstream, image_upstream,
    ):
        pair_count, cap_len, text_width = text_states.shape
        region_len, image_width = image_states.shape[1:]
        text_rows = text_states.reshape(pair_count * cap_len, text_width)
        image_rows = image_states.reshape(pair_count * region_len, image_width)
        core = lax.axis_index("heads")
        captions = lax.dynamic_slice(caption_lengths, (core * pair_count,), (pair_count,))
        regions = lax.dynamic_slice(region_counts, (core * pair_count,), (pair_count,))

        def heads_of(row_values, weight, length):
            return project(row_values, weight).astype(BF16).reshape(pair_count, length, CO_HEADS, HEAD_DIM)

        tq, tk, tv = (heads_of(text_rows, w, cap_len) for w in (text_query, text_key, text_value))
        iq, ik, iv = (heads_of(image_rows, w, region_len) for w in (image_query, image_key, image_value))
        text_context, text_prob = attend(tq, ik, iv, regions)
        image_context, image_prob = attend(iq, tk, tv, captions)
        flat = lambda v: v.reshape(v.shape[0] * v.shape[1], -1)
        text_result, text_kept = stream_forward(
            text_rows, flat(text_context), text_output, text_up, text_down, text_gains, text_shifts
        )
        image_result, image_kept = stream_forward(
            image_rows, flat(image_context), image_output, image_up, image_down, image_gains, image_shifts
        )
        t_sum, t_cgrad, t_branch, t_zgrad, t_slow, t_small = stream_back(
            text_upstream.reshape(text_rows.shape), text_kept, text_output, text_up, text_down, text_gains
        )
        i_sum, i_cgrad, i_branch, i_zgrad, i_slow, i_small = stream_back(
            image_upstream.reshape(image_rows.shape), image_kept, image_output, image_up, image_down, image_gains
        )
        g_tq, g_ik, g_iv = attend_back(tq, ik, iv, text_prob, t_cgrad.reshape(tq.shape))
        g_iq, g_tk, g_tv = attend_back(iq, tk, tv, image_prob, i_cgrad.reshape(iq.shape))
        g_tq, g_tk, g_tv, g_iq, g_ik, g_iv = (flat(v) for v in (g_tq, g_tk, g_tv, g_iq, g_ik, g_iv))
        text_in = t_sum + project_back(g_tq, text_query) + project_back(g_tk, text_key) + project_back(g_tv, text_value)
        image_in = (
            i_sum + project_back(g_iq, image_query) + project_back(g_ik, image_key) + project_back(g_iv, image_value)
        )
        tl = (t_branch, text_kept[2], t_slow, text_rows)
        tr = (text_kept[4], t_zgrad, flat(text_context), g_tq, g_tk, g_tv)
        il = (i_branch, image_kept[2], i_slow, image_rows)
        ir = (image_kept[4], i_zgrad, flat(image_context), g_iq, g_ik, g_iv)
        wide = max(text_width, image_width)
        small = jnp.stack([jnp.pad(v, (0, wide - v.shape[0])) for v in t_small + i_small])
        me = lax.axis_index("batch") * mesh.shape["heads"] + core

        def parts(grads, width):
            down, up, out, query, key, value = grads
            return query, key, value, out.T, up, down.T

        if fast:
            text_plan, image_plan = plan(CW, tuple(v.shape[1] for v in tr), tuple(v.shape[1] for v in ir))
            got_t, got_i, total = reduce_grads(
                (4, 2, 2), CW, LEFTS, LEFTS, chunk_order(len(text_plan), len(image_plan)), tl, tr, il, ir, small
            )

            def weights(got, chunks):
                half = got.shape[0] // 2
                return [
                    jnp.concatenate(
                        [got[c * half + i] for c in range(2) for i, (v, _) in enumerate(chunks) if v == w], axis=1
                    )
                    for w in range(6)
                ]

            text_grads = weights(got_t, text_plan)
            image_grads = weights(got_i, image_plan)
        else:
            scatter = lambda v: lax.psum_scatter(v, ("batch", "heads"), scatter_dimension=0, tiled=True)
            text_grads = [scatter(outer_sum(tl[l], r)) for l, r in zip(LEFTS, tr)]
            image_grads = [scatter(outer_sum(il[l], r)) for l, r in zip(LEFTS, ir)]
            total = lax.psum(small, ("batch", "heads"))
        t_own, i_own = text_width // devices, image_width // devices
        t_norm = lax.dynamic_slice(total, (0, me * t_own), (4, t_own))
        i_norm = lax.dynamic_slice(total, (4, me * i_own), (4, i_own))
        return (
            text_result.reshape(text_states.shape),
            image_result.reshape(image_states.shape),
            text_in.astype(BF16).reshape(text_states.shape),
            image_in.astype(BF16).reshape(image_states.shape),
            *parts(text_grads, text_width), t_norm[:2], t_norm[2:],
            *parts(image_grads, image_width), i_norm[:2], i_norm[2:],
        )

    return local


def solution(mesh):
    rows = P(("batch", "heads"), None, None)
    first, second = P(("batch", "heads"), None), P(None, ("batch", "heads"))
    grads = (first, first, first, second, first, second, second, second)
    return jax.shard_map(
        make_local(mesh),
        mesh=mesh,
        in_specs=(rows, rows, P("batch"), P("batch"), *[P()] * 16, rows, rows),
        out_specs=(rows, rows, rows, rows, *grads, *grads),
        check_vma=False,
    )
```

```python
import functools
import math

import jax
import jax.numpy as jnp
from jax import lax
from jax.experimental import pallas as pl
from jax.experimental.pallas import tpu as pltpu
from jax.sharding import PartitionSpec as P

MESH_ID = pl.DeviceIdType.MESH
F32 = jnp.float32
BF16 = jnp.bfloat16
EPS = 1e-05
NEG = -1000000000.0
HEADS = 8
HEAD = 128
SCALE = 1.0 / math.sqrt(HEAD)
TILE = 256
CW = 256
LEFTS = (0, 1, 2, 3, 3, 3)
NT_DIMS = (((1,), (1,)), ((), ()))
TN_DIMS = (((0,), (0,)), ((), ()))
SLOTS = 6
G_RING, R_RING, Z_RING = 12, 12, 16
PRODUCED = ((1, 0), (1, 1), (1, 2), (0, 0), (0, 1), (0, 2), (1, 3), (0, 4), (0, 5), (0, 3), (1, 4), (1, 5))
SEQUENCE = (
    "i_qkv", "i_attend", "i_out", "i_ffn", "i_norm", "i_slope", "A0", "i_branch", "A1", "i_context", "t_q", "t_kv",
    "A2", "T0", "t_attend", "t_out", "T1", "t_ffn0", "t_ffn1", "t_ffn2", "T2", "t_norm", "A3", "t_slope0", "A4", "T3",
    "t_slope1", "A5", "T4", "t_slope2", "t_branch", "A6", "T5", "A7", "T6", "i_back", "A8", "T7", "t_context", "A9",
    "T8", "A10", "T9", "t_back", "A11", "T10", "A12", "T11", "A13", "T12", "i_final", "A14", "T13", "t_final", "A15",
    "T14", "T15", "T16", "T17", "T18", "T19",
)


def dot(a, b):
    return jnp.dot(a, b, preferred_element_type=F32)


def dot_nt(a, b):
    return lax.dot_general(a, b, NT_DIMS, preferred_element_type=F32)


def dot_tn(a, b):
    return lax.dot_general(a, b, TN_DIMS, preferred_element_type=F32)


def loop(n, body):
    def step(i, carry):
        body(i)
        return carry

    lax.fori_loop(0, n, step, 0)


def at(i, size):
    return pl.ds(pl.multiple_of(i * size, size), size)


def layer_kernel(dims, *refs):
    nz, ny, nx = dims
    refs = list(refs)

    def take(n):
        got = refs[:n]
        del refs[:n]
        return got

    cap_ref, reg_ref, xt_in, xi_in, ut_in, ui_in = take(6)
    w_in = [take(6), take(6)]
    gain_ref, shift_ref = take(2), take(2)
    res_t, res_i, sg_t, sg_i = take(4)
    w_out = [take(6), take(6)]
    norm_out = take(4)
    wbuf, x_t, x_i, raw_i, u_t, u_i = take(6)
    q_b, k_b, v_b = take(2), take(2), take(2)
    n1, inv, low, slope, acc, dctx, sums = take(2), take(2), take(2), take(2), take(2), take(2), take(2)
    lt = take(2)
    r_own, r_far = [take(6), take(6)], [take(6), take(6)]
    g_b, r1_b, r2_b, ru_b, rd_b = take(5)
    f_b = take(2)
    small, sv, sr = take(3)
    in_sem, w_sem, ex_s, ex_r, st_s, st_r, sm_s, sm_r = take(8)
    assert not refs

    b, h = lax.axis_index("batch"), lax.axis_index("heads")
    x, y, z = lax.rem(b, nx), lax.rem(lax.div(b, nx), ny), lax.div(b, nx * ny)

    def dev(zz, yy, xx):
        return ((zz * ny + yy) * nx + xx, h)

    partner, nbr_x, nbr_y = (b, 1 - h), dev(z, y, 1 - x), dev(z, 1 - y, x)
    barrier = pltpu.get_barrier_semaphore()
    for who in (partner, nbr_x, nbr_y):
        pl.semaphore_signal(barrier, inc=1, device_id=who, device_id_type=MESH_ID)
    for off in range(1, nz):
        pl.semaphore_signal(barrier, inc=1, device_id=dev(lax.rem(z + off, nz), y, x), device_id_type=MESH_ID)

    def remote(src, dst, ssem, rsem, who):
        return pltpu.make_async_remote_copy(
            src_ref=src, dst_ref=dst, send_sem=ssem, recv_sem=rsem, device_id=who, device_id_type=MESH_ID
        )

    T, I = 0, 1
    pieces = []

    def piece(name, ref, rows, cols):
        pieces.append((name, ref, rows, cols))

    td, ti = x_t.shape[1], x_i.shape[1]
    inner = q_b[0].shape[1]
    parts = w_in[T][1].shape[1] // 1024
    whole = lambda s, w: w_in[s][w]
    tu = lambda j: w_in[T][1].at[:, pl.ds(j * 1024, 1024)]
    tw = lambda j: w_in[T][0].at[pl.ds(j * 1024, 1024), :]
    piece("tk", whole(T, 4), td, inner)
    piece("tv", whole(T, 5), td, inner)
    piece("iq", whole(I, 3), ti, inner)
    piece("io", whole(I, 2), inner, ti)
    piece("iu", whole(I, 1), ti, ti)
    piece("id", whole(I, 0), ti, ti)
    piece("tq", whole(T, 3), td, inner)
    piece("ik", whole(I, 4), ti, inner)
    piece("iv", whole(I, 5), ti, inner)
    piece("to", whole(T, 2), inner, td)
    for j in range(parts):
        piece("tu%d" % j, tu(j), td, 1024)
        piece("td%d" % j, tw(j), 1024, td)
    piece("to", whole(T, 2), inner, td)
    for name, s, w in (("iq", I, 3), ("tk", T, 4), ("tv", T, 5), ("tq", T, 3), ("ik", I, 4), ("iv", I, 5)):
        rows = td if s == T else ti
        piece(name, whole(s, w), rows, inner)
    issued = [0]
    held = {}

    def weight_copy(k, slot):
        name, ref, rows, cols = pieces[k]
        return pltpu.make_async_copy(ref, wbuf.at[slot, pl.ds(0, rows), pl.ds(0, cols)], w_sem.at[slot])

    def issue(slot):
        if issued[0] < len(pieces):
            k = issued[0]
            issued[0] += 1
            weight_copy(k, slot).start()
            assert pieces[k][0] not in held
            held[pieces[k][0]] = [k, slot, False]

    def weight(name):
        k, slot, ready = held[name]
        if not ready:
            weight_copy(k, slot).wait()
            held[name][2] = True
        _, _, rows, cols = pieces[k]
        return wbuf.at[slot, pl.ds(0, rows), pl.ds(0, cols)]

    def release(name):
        k, slot, ready = held.pop(name)
        issue(slot)

    in_copies = [
        pltpu.make_async_copy(s, d, in_sem.at[i])
        for i, (s, d) in enumerate(((xt_in, x_t), (xi_in, raw_i.at[0]), (ut_in, u_t), (ui_in, raw_i.at[1])))
    ]
    in_copies[0].start()
    issue(0)
    in_copies[1].start()
    issue(1)
    issue(2)
    in_copies[3].start()
    in_copies[2].start()
    for slot in range(3, SLOTS):
        issue(slot)

    pairs_n, regions = raw_i.shape[1], raw_i.shape[2]
    cap = x_t.shape[0] // pairs_n
    pad = 112
    m_i, m_t = pairs_n * pad, x_t.shape[0]
    m_of, d_of = (m_t, m_i), (td, ti)
    x_of = (x_t, x_i)

    tail = pl.ds(m_i, x_i.shape[0] - m_i)
    for ref in (x_i, low[I], *r_own[I]):
        ref[tail, :] = jnp.zeros((x_i.shape[0] - m_i, ref.shape[1]), BF16)
    for ref in (*sums,):
        ref[...] = jnp.zeros(ref.shape, F32)

    def spread(src, dst):
        for p in range(pairs_n):
            dst[pl.ds(p * pad, regions), :] = src[p]
            dst[pl.ds(p * pad + regions, pad - regions), :] = jnp.zeros((pad - regions, dst.shape[1]), BF16)

    lengths = {
        T: [reg_ref[h * pairs_n + p] for p in range(pairs_n)],
        I: [cap_ref[h * pairs_n + p] for p in range(pairs_n)],
    }

    ex_left, ex_right = {}, {}
    n_left = max(LEFTS) + 1
    for s in (T, I):
        for l in range(n_left):
            k = s * n_left + l
            ex_left[s, l] = remote(
                lt[s].at[l, :, pl.ds(0, 256)], lt[s].at[l, :, pl.ds(256, 256)], ex_s.at[k], ex_r.at[k], partner
            )
        for w in range(6):
            k = 2 * n_left + s * 6 + w
            half = r_far[s][w].shape[1]
            ex_right[s, w] = remote(
                r_own[s][w].at[:, pl.ds(pl.multiple_of((1 - h) * half, 128), half)], r_far[s][w],
                ex_s.at[k], ex_r.at[k], partner,
            )
    arrived = set()
    entered = []

    def enter():
        if not entered:
            entered.append(1)
            pl.semaphore_wait(barrier, 3 + nz - 1)

    def send_left(s, l, src):
        def body(j):
            lt[s][l, at(j, TILE), pl.ds(0, 256)] = src[:, at(j, TILE)].T

        loop(d_of[s] // TILE, body)
        enter()
        ex_left[s, l].start()

    def send_right(s, w):
        enter()
        ex_right[s, w].start()

    def project(src, rows, w, dst):
        def body(j):
            dst[pl.ds(0, rows), at(j, TILE)] = dot(src[pl.ds(0, rows), :], w[:, at(j, TILE)]).astype(BF16)

        loop(w.shape[1] // TILE, body)

    def softmax(q, k, live):
        s = dot_nt(q, k) * SCALE
        mask = lax.broadcasted_iota(jnp.int32, s.shape, 1) < live
        s = jnp.where(mask, s, NEG)
        e = jnp.exp(s - jnp.max(s, axis=-1, keepdims=True))
        return e / jnp.sum(e, axis=-1, keepdims=True)

    span = (cap, pad)

    def rows_of(s, p):
        return pl.ds(p * span[s], span[s])

    def attend(s):
        o = 1 - s

        def body(i):
            cols = at(i, HEAD)
            for p in range(pairs_n):
                q, k = q_b[s][rows_of(s, p), cols], k_b[o][rows_of(o, p), cols]
                prob = softmax(q, k, lengths[s][p]).astype(BF16)
                r_own[s][2][rows_of(s, p), cols] = dot(prob, v_b[o][rows_of(o, p), cols]).astype(BF16)

        loop(HEADS, body)
        send_right(s, 2)

    def attend_back(s):
        o = 1 - s

        def body(i):
            cols = at(i, HEAD)
            for p in range(pairs_n):
                rq, rk = rows_of(s, p), rows_of(o, p)
                q, k, v, dc = q_b[s][rq, cols], k_b[o][rk, cols], v_b[o][rk, cols], dctx[s][rq, cols]
                prob = softmax(q, k, lengths[s][p])
                dp = dot_nt(dc, v)
                ds = (prob * (dp - jnp.sum(prob * dp, axis=-1, keepdims=True))).astype(BF16)
                r_own[s][3][rq, cols] = (dot(ds, k) * SCALE).astype(BF16)
                r_own[o][4][rk, cols] = (dot_tn(ds, q) * SCALE).astype(BF16)
                r_own[o][5][rk, cols] = dot_tn(prob.astype(BF16), dc).astype(BF16)

        loop(HEADS, body)
        send_right(s, 3)
        send_right(o, 4)
        send_right(o, 5)

    RB = 32

    def mean(v):
        return jnp.mean(v, axis=-1, keepdims=True)

    def sum8(v):
        return jnp.sum(v.reshape(v.shape[0] // 8, 8, v.shape[1]), axis=0)

    def norm_one(s):
        gain, shift = gain_ref[s][0:1, :], shift_ref[s][0:1, :]

        def body(i):
            r = at(i, RB)
            v = x_of[s][r, :].astype(F32) + acc[s][r, :]
            c = v - mean(v)
            iv = lax.rsqrt(mean(c * c) + EPS)
            n = c * iv
            n1[s][r, :] = n
            inv[s][r, :] = jnp.broadcast_to(iv, (RB, 128))
            low[s][r, :] = (n * gain + shift).astype(BF16)

        loop(m_of[s] // RB, body)
        send_left(s, 1, low[s])

    def norm_two(s, up_ref, res_ref):
        gain0, shift0 = gain_ref[s][0:1, :], shift_ref[s][0:1, :]
        gain, shift = gain_ref[s][1:2, :], shift_ref[s][1:2, :]

        def body(i):
            r = at(i, RB)
            v = n1[s][r, :] * gain0 + shift0 + acc[s][r, :]
            c = v - mean(v)
            iv = lax.rsqrt(mean(c * c) + EPS)
            n = c * iv
            up = up_ref[r, :].astype(F32)
            res_ref[r, :] = (n * gain + shift).astype(BF16)
            un = up * n
            sums[s][1] = sums[s][1] + sum8(un)
            sums[s][3] = sums[s][3] + sum8(up)
            u = up * gain
            d = iv * (u - mean(u) - n * mean(un * gain))
            acc[s][r, :] = d
            low[s][r, :] = d.astype(BF16)

        loop(m_of[s] // RB, body)
        send_left(s, 0, low[s])

    def norm_one_back(s):
        gain = gain_ref[s][0:1, :]

        def body(i):
            r = at(i, RB)
            g, n = acc[s][r, :], n1[s][r, :]
            gn = g * n
            sums[s][0] = sums[s][0] + sum8(gn)
            sums[s][2] = sums[s][2] + sum8(g)
            u = g * gain
            d = inv[s][r, 0:1] * (u - mean(u) - n * mean(gn * gain))
            acc[s][r, :] = d
            low[s][r, :] = d.astype(BF16)

        loop(m_of[s] // RB, body)
        send_left(s, 2, low[s])

    def out_project(s, w):
        m = m_of[s]

        def body(j):
            acc[s][pl.ds(0, m), at(j, TILE)] = dot(r_own[s][2][pl.ds(0, m), :], w[:, at(j, TILE)])

        loop(d_of[s] // TILE, body)

    def ffn(s, j, up_w, down_w):
        m, base = m_of[s], j * 1024

        def hidden(i):
            c = pl.ds(pl.multiple_of(base + i * TILE, TILE), TILE)
            v = dot(low[s][pl.ds(0, m), :], up_w[:, at(i, TILE)])
            half = 0.5 * (1.0 + lax.erf(v * (1.0 / math.sqrt(2.0))))
            r_own[s][0][pl.ds(0, m), c] = (v * half).astype(BF16)
            slope[s][pl.ds(0, m), c] = (half + v * jnp.exp(-0.5 * v * v) * (1.0 / math.sqrt(2.0 * math.pi))).astype(BF16)

        loop(1024 // TILE, hidden)

        def second(i):
            part = dot(r_own[s][0][pl.ds(0, m), pl.ds(base, 1024)], down_w[:, at(i, TILE)])
            if j == 0:
                acc[s][pl.ds(0, m), at(i, TILE)] = part
            else:
                acc[s][pl.ds(0, m), at(i, TILE)] += part

        loop(d_of[s] // TILE, second)

    def slope_back(s, j, down_w):
        m, base = m_of[s], j * 1024

        def body(i):
            c = pl.ds(pl.multiple_of(base + i * TILE, TILE), TILE)
            g = dot_nt(low[s][pl.ds(0, m), :], down_w[at(i, TILE), :])
            r_own[s][1][pl.ds(0, m), c] = (g * slope[s][pl.ds(0, m), c].astype(F32)).astype(BF16)

        loop(1024 // TILE, body)

    def back_add(s, src, cols, w):
        m = m_of[s]

        def body(i):
            acc[s][pl.ds(0, m), at(i, TILE)] += dot_nt(src[pl.ds(0, m), cols], w[at(i, TILE), :])

        loop(d_of[s] // TILE, body)

    def context_back(s, w):
        m = m_of[s]

        def body(i):
            dctx[s][pl.ds(0, m), at(i, TILE)] = dot_nt(low[s][pl.ds(0, m), :], w[at(i, TILE), :]).astype(BF16)

        loop(inner // TILE, body)

    def final(s, dst):
        def body(i):
            dst[at(i, RB), :] = acc[s][at(i, RB), :].astype(BF16)

        loop(m_of[s] // RB, body)

    def gather_rows(src, dst):
        for p in range(pairs_n):
            dst[p] = src[pl.ds(p * pad, regions), :]

    all_cols = pl.ds(0, 1024)

    def step(name):
        if name == "i_qkv":
            in_copies[0].wait()
            project(x_t, m_t, weight("tk"), k_b[T])
            release("tk")
            project(x_t, m_t, weight("tv"), v_b[T])
            release("tv")
            in_copies[1].wait()
            spread(raw_i.at[0], x_i)
            project(x_i, m_i, weight("iq"), q_b[I])
            release("iq")
        elif name == "i_attend":
            attend(I)
        elif name == "i_out":
            out_project(I, weight("io"))
            norm_one(I)
        elif name == "i_ffn":
            ffn(I, 0, weight("iu"), weight("id"))
            send_right(I, 0)
        elif name == "i_norm":
            in_copies[3].wait()
            spread(raw_i.at[1], u_i)
            norm_two(I, u_i, u_i)
            gather_rows(u_i, res_i)
        elif name == "i_slope":
            slope_back(I, 0, weight("id"))
            send_right(I, 1)
            release("id")
        elif name == "i_branch":
            back_add(I, r_own[I][1], all_cols, weight("iu"))
            release("iu")
            norm_one_back(I)
        elif name == "i_context":
            context_back(I, weight("io"))
            release("io")
            send_left(I, 3, x_i)
        elif name == "t_q":
            project(x_t, m_t, weight("tq"), q_b[T])
            release("tq")
            send_left(T, 3, x_t)
        elif name == "t_kv":
            project(x_i, m_i, weight("ik"), k_b[I])
            release("ik")
            project(x_i, m_i, weight("iv"), v_b[I])
            release("iv")
        elif name == "t_attend":
            attend(T)
        elif name == "t_out":
            out_project(T, weight("to"))
            release("to")
            norm_one(T)
        elif name.startswith("t_ffn"):
            j = int(name[-1])
            ffn(T, j, weight("tu%d" % j), weight("td%d" % j))
            if j == parts - 1:
                send_right(T, 0)
        elif name == "t_norm":
            in_copies[2].wait()
            norm_two(T, u_t, res_t)
        elif name.startswith("t_slope"):
            j = int(name[-1])
            slope_back(T, j, weight("td%d" % j))
            release("td%d" % j)
            if j == parts - 1:
                send_right(T, 1)
        elif name == "t_branch":
            for j in range(parts):
                back_add(T, r_own[T][1], pl.ds(j * 1024, 1024), weight("tu%d" % j))
                release("tu%d" % j)
            norm_one_back(T)
            small_fill()
        elif name == "t_context":
            context_back(T, weight("to"))
            release("to")
        elif name == "i_back":
            attend_back(I)
            back_add(I, r_own[I][3], all_cols, weight("iq"))
            release("iq")
            back_add(T, r_own[T][4], all_cols, weight("tk"))
            release("tk")
            back_add(T, r_own[T][5], all_cols, weight("tv"))
            release("tv")
        elif name == "t_back":
            attend_back(T)
        elif name == "i_final":
            back_add(I, r_own[I][4], all_cols, weight("ik"))
            release("ik")
            back_add(I, r_own[I][5], all_cols, weight("iv"))
            release("iv")
            final(I, u_i)
            gather_rows(u_i, sg_i)
        elif name == "t_final":
            back_add(T, r_own[T][3], all_cols, weight("tq"))
            release("tq")
            final(T, sg_t)
        elif name[0] == "A":
            for c in (2 * int(name[1:]), 2 * int(name[1:]) + 1):
                compute(c)
                s1(c).start()
        else:
            tick(int(name[1:]))

    small_copies = []

    def small_start(src, dst, i, who):
        c = remote(src, dst, sm_s.at[i], sm_r.at[i], who)
        c.start()
        small_copies.append(c)

    def small_fill():
        small[...] = jnp.zeros(small.shape, F32)
        for s in (T, I):
            for k in range(4):
                small[pl.ds(4 * s + k, 1), pl.ds(0, d_of[s])] = jnp.sum(sums[s][k], axis=0, keepdims=True)

    def small_step(i):
        if i == 0:
            small_start(small, sr.at[0], 0, partner)
        elif i == 1:
            small_copies[0].wait_recv()
            sv[0] = small[...] + sr[0]
            small_start(sv.at[0], sr.at[1], 1, nbr_x)
        elif i == 2:
            small_copies[1].wait_recv()
            sv[1] = sv[0] + sr[1]
            small_start(sv.at[1], sr.at[2], 2, nbr_y)
        elif i == 3:
            small_copies[2].wait_recv()
            sv[2] = sv[1] + sr[2]
            for off in range(1, nz):
                small_start(sv.at[2], sr.at[2 + off], 2 + off, dev(lax.rem(z + off, nz), y, x))
        elif i == 4:
            total = sv[2]
            for off in range(1, nz):
                small_copies[2 + off].wait_recv()
                total = total + sr[2 + off]
            wide = total.shape[1]
            me = b * 2 + h
            for s in (T, I):
                own = norm_out[2 * s].shape[1]
                mine = pltpu.roll(total, lax.rem(wide - me * own, wide), 1)
                norm_out[2 * s][...] = mine[4 * s : 4 * s + 2, :own]
                norm_out[2 * s + 1][...] = mine[4 * s + 2 : 4 * s + 4, :own]

    chunks = []
    for s, w in PRODUCED:
        for o in range(0, r_far[s][w].shape[1], CW):
            chunks.append((s, w, o, "xy"[len(chunks) % 2], len([1 for c in chunks if c[0] == s])))
    n = len(chunks)

    def bufs(c):
        rows = pl.ds(0, d_of[chunks[c][0]] // (nz * ny * nx))
        return (
            g_b.at[c % G_RING, :, :, :, rows], r1_b.at[c % R_RING, :, :, rows], r2_b.at[c % R_RING, :, rows],
            ru_b.at[c % Z_RING, :, rows], rd_b.at[c % Z_RING, :, rows],
        )

    def compute(c):
        s, w, o, way, _ = chunks[c]
        for copy, key in ((ex_left[s, LEFTS[w]], (0, s, LEFTS[w])), (ex_right[s, w], (1, s, w))):
            if key not in arrived:
                arrived.add(key)
                copy.wait_recv()
        blk = d_of[s] // (nz * ny * nx)
        size = ny * nx * blk
        half = r_far[s][w].shape[1]
        mine = pl.ds(pl.multiple_of(h * half + o, 128), CW)
        g = g_b.at[c % G_RING]

        def body(i):
            r = pl.ds(pl.multiple_of(i * size, 64), size)
            l = LEFTS[w]
            res = dot(lt[s][l, r, pl.ds(0, 256)], r_own[s][w][:, mine]) + dot(
                lt[s][l, r, pl.ds(256, 256)], r_far[s][w][:, pl.ds(o, CW)]
            )
            g[i, :, :, pl.ds(0, blk)] = res.astype(BF16).reshape(ny, nx, blk, CW)

        loop(nz, body)

    def add(dst, src):
        dst[...] = (dst[...].astype(F32) + src[...].astype(F32)).astype(BF16)

    def s1(c):
        g, r1 = bufs(c)[:2]
        if chunks[c][3] == "x":
            return remote(g.at[:, :, 1 - x], r1, st_s.at[0, c], st_r.at[0, c], nbr_x)
        return remote(g.at[:, 1 - y], r1, st_s.at[0, c], st_r.at[0, c], nbr_y)

    def s2(c):
        g, _, r2 = bufs(c)[:3]
        if chunks[c][3] == "x":
            return remote(g.at[:, 1 - y, x], r2, st_s.at[1, c], st_r.at[1, c], nbr_y)
        return remote(g.at[:, y, 1 - x], r2, st_s.at[1, c], st_r.at[1, c], nbr_x)

    def up(c, k):
        g, ru = bufs(c)[0], bufs(c)[3]
        rest = pl.ds(k + 1, nz - 1 - k)
        return remote(g.at[rest, y, x], ru.at[rest], st_s.at[2, c], st_r.at[2, c], dev(k + 1, y, x))

    def down(c, k):
        g, rd = bufs(c)[0], bufs(c)[4]
        rest = pl.ds(0, k)
        return remote(g.at[rest, y, x], rd.at[rest], st_s.at[3, c], st_r.at[3, c], dev(k - 1, y, x))

    def swap(c):
        s, w, o, _, k = chunks[c]
        out = w_out[s][w]
        half = out.shape[1] // 2
        return remote(
            f_b[s].at[k], out.at[:, pl.ds(pl.multiple_of(h * half + o, 128), CW)],
            st_s.at[4, c], st_r.at[4, c], partner,
        )

    def stage2(c):
        s1(c).wait_recv()
        g, r1 = bufs(c)[:2]

        def body(i):
            for j in range(2):
                add(g.at[i, j, x] if chunks[c][3] == "x" else g.at[i, y, j], r1.at[i, j])

        loop(nz, body)
        s2(c).start()

    def stage3(c):
        s2(c).wait_recv()
        g, _, r2 = bufs(c)[:3]
        loop(nz, lambda i: add(g.at[i, y, x], r2.at[i]))

        @pl.when(z == 0)
        def _():
            up(c, 0).start()

        @pl.when(z == nz - 1)
        def _():
            down(c, nz - 1).start()

    def hop(c, d):
        g, _, _, ru, rd = bufs(c)

        @pl.when(z == d)
        def _():
            up(c, d - 1).wait_recv()
            for t in range(d + 1, nz):
                add(g.at[t, y, x], ru.at[t])
            up(c, d).start()

        @pl.when(z == nz - 1 - d)
        def _():
            down(c, nz - d).wait_recv()
            for t in range(0, nz - 1 - d):
                add(g.at[t, y, x], rd.at[t])
            down(c, nz - 1 - d).start()

    def finish(c):
        g, _, _, ru, rd = bufs(c)
        s, w, o, _, idx = chunks[c]
        out = w_out[s][w]
        r, half = out.shape[0], out.shape[1] // 2
        cols = pl.ds(pl.multiple_of(h * half + o, 128), CW)
        for k in range(nz):

            @pl.when(z == k)
            def _(k=k):
                if k == nz - 1:
                    up(c, k - 1).wait_recv()
                if k == 0:
                    down(c, 1).wait_recv()
                total = g[k, y, x].astype(F32)
                if k > 0:
                    total = total + ru[k].astype(F32)
                if k < nz - 1:
                    total = total + rd[k].astype(F32)
                first, second = total[:r], total[r:]
                out[:, cols] = jnp.where(h == 0, first, second)
                f_b[s][idx] = jnp.where(h == 0, second, first)

        swap(c).start()
        s1(c).wait_send()
        s2(c).wait_send()
        for k in range(nz):

            @pl.when(z == k)
            def _(k=k):
                if k < nz - 1:
                    up(c, k).wait_send()
                if k > 0:
                    down(c, k).wait_send()

    pairs = n // 2
    small_from = 6

    def tick(t):
        for lag, stage in (
            (0, stage2), (1, stage3), *[(1 + d, functools.partial(hop, d=d)) for d in range(1, nz - 1)], (nz, finish)
        ):
            p = t - lag
            if 0 <= p < pairs:
                stage(2 * p)
                stage(2 * p + 1)
        if small_from <= t < small_from + 5:
            small_step(t - small_from)

    for name in SEQUENCE:
        step(name)

    for c in range(n):
        swap(c).wait_recv()
        swap(c).wait_send()
    for copy in (*ex_left.values(), *ex_right.values()):
        copy.wait_send()
    for copy in small_copies:
        copy.wait_send()


def layer(dims, lengths, states, upstream, weights, gains, shifts):
    nz, ny, nx = dims
    chips = nz * ny * nx
    xt, xi = states
    pairs, cap, td = xt.shape
    regions, ti = xi.shape[1:]
    xt, ut = xt.reshape(pairs * cap, td), upstream[0].reshape(pairs * cap, td)
    mt = pairs * cap
    fixed = 256
    inner = weights[0][3].shape[1]
    d_of = (td, ti)
    cols = [[w.shape[0], weights[s][1].shape[1], inner, inner, inner, inner] for s, w in ((0, weights[0][0]), (1, weights[1][0]))]
    V, DMA = pltpu.VMEM, pltpu.SemaphoreType.DMA
    rows_of = (mt, fixed)
    ti_blk = ti // chips
    counts = [sum(c // 2 // CW for c in cols[s]) for s in range(2)]
    n = sum(counts)
    act = lambda dt, width: [V((rows_of[s], width[s]), dt) for s in range(2)]
    scratch = [
        V((SLOTS, 1024, 1024), BF16),
        V((mt, td), BF16), V((fixed, ti), BF16), V((2, pairs, regions, ti), BF16), V((mt, td), BF16), V((fixed, ti), BF16),
        *act(BF16, (inner, inner)), *act(BF16, (inner, inner)), *act(BF16, (inner, inner)),
        *act(F32, d_of), *act(F32, (128, 128)), *act(BF16, d_of), *act(BF16, (cols[0][1], cols[1][1])),
        *act(F32, d_of), *act(BF16, (inner, inner)),
        *[V((4, 8, d), F32) for d in d_of],
        *[V((4, d, 512), BF16) for d in d_of],
        *[V((rows_of[s], c), BF16) for s in range(2) for c in cols[s]],
        *[V((rows_of[s], c // 2), BF16) for s in range(2) for c in cols[s]],
        V((G_RING, nz, ny, nx, ti_blk, CW), BF16),
        V((R_RING, nz, 2, ti_blk, CW), BF16),
        V((R_RING, nz, ti_blk, CW), BF16),
        V((Z_RING, nz, ti_blk, CW), BF16),
        V((Z_RING, nz, ti_blk, CW), BF16),
        *[V((counts[s], d_of[s] // chips // 2, CW), F32) for s in range(2)],
        V((8, max(d_of)), F32), V((3, 8, max(d_of)), F32), V((2 + nz, 8, max(d_of)), F32),
        DMA((4,)), DMA((SLOTS,)), DMA((20,)), DMA((20,)), DMA((5, n)), DMA((5, n)), DMA((2 + nz,)), DMA((2 + nz,)),
    ]
    hbm = pl.BlockSpec(memory_space=pl.ANY)
    vm = pl.BlockSpec(memory_space=pltpu.VMEM)
    smem = pl.BlockSpec(memory_space=pltpu.SMEM)
    sds = jax.ShapeDtypeStruct
    outs = [
        sds((mt, td), BF16), sds((pairs, regions, ti), BF16), sds((mt, td), BF16), sds((pairs, regions, ti), BF16),
        *[sds((d_of[s] // chips // 2, c), F32) for s in range(2) for c in cols[s]],
        *[sds((2, d_of[s] // chips // 2), F32) for s in range(2) for _ in range(2)],
    ]
    got = pl.pallas_call(
        functools.partial(layer_kernel, dims),
        out_shape=outs,
        in_specs=[smem, smem, *[hbm] * 4, *[hbm] * 12, *[vm] * 4],
        out_specs=[vm] * len(outs),
        scratch_shapes=scratch,
        compiler_params=pltpu.CompilerParams(
            collective_id=0, has_side_effects=True, vmem_limit_bytes=67043328
        ),
        name="co_layer",
    )(*lengths, xt, xi, ut, upstream[1], *weights[0], *weights[1], *gains, *shifts)
    return got


def matmul(row_values, weight):
    return jnp.dot(row_values, weight, preferred_element_type=F32)


def project_back(gradient, weight):
    return lax.dot_general(gradient, weight, (((1,), (1,)), ((), ())), preferred_element_type=F32)


def outer_sum(row_values, gradient):
    return lax.dot_general(row_values, gradient, (((0,), (0,)), ((), ())), preferred_element_type=F32)


def layer_norm(values, gain, shift):
    row_mean = jnp.mean(values, axis=-1, keepdims=True)
    centred = values - row_mean
    spread = jnp.mean(centred * centred, axis=-1, keepdims=True)
    inverse = lax.rsqrt(spread + EPS)
    normed = centred * inverse
    return (normed * gain + shift, normed, inverse)


def norm_back(gradient, normed, inverse, gain):
    scaled = gradient * gain
    first_mean = jnp.mean(scaled, axis=-1, keepdims=True)
    second_mean = jnp.mean(scaled * normed, axis=-1, keepdims=True)
    into = inverse * (scaled - first_mean - normed * second_mean)
    return (into, jnp.sum(gradient * normed, axis=0), jnp.sum(gradient, axis=0))


def gelu_value(values):
    return 0.5 * values * (1.0 + jax.scipy.special.erf(values / math.sqrt(2.0)))


def gelu_slope(values):
    return 0.5 * (1.0 + jax.scipy.special.erf(values / math.sqrt(2.0))) + values * jnp.exp(
        -0.5 * values * values
    ) / math.sqrt(2.0 * math.pi)


def attend(queries, key_rows, value_rows, lengths):
    score_scale = 1.0 / math.sqrt(queries.shape[-1])
    scores = jnp.einsum("bqhd,bkhd->bhqk", queries, key_rows, preferred_element_type=F32) * score_scale
    live_mask = lax.broadcasted_iota(jnp.int32, scores.shape, 3) < lengths[:, None, None, None]
    scores = jnp.where(live_mask, scores, NEG)
    weights = jnp.exp(scores - jnp.max(scores, axis=-1, keepdims=True))
    probability = weights / jnp.sum(weights, axis=-1, keepdims=True)
    context = jnp.einsum("bhqk,bkhd->bqhd", probability.astype(BF16), value_rows, preferred_element_type=F32)
    return context.astype(BF16), probability


def attend_back(queries, key_rows, value_rows, probability, context_grad):
    score_scale = 1.0 / math.sqrt(queries.shape[-1])
    value_grad = jnp.einsum(
        "bhqk,bqhd->bkhd", probability.astype(BF16), context_grad, preferred_element_type=F32
    )
    prob_grad = jnp.einsum("bqhd,bkhd->bhqk", context_grad, value_rows, preferred_element_type=F32)
    row_inner = jnp.sum(probability * prob_grad, axis=-1, keepdims=True)
    score_grad = (probability * (prob_grad - row_inner)).astype(BF16)
    query_grad = jnp.einsum("bhqk,bkhd->bqhd", score_grad, key_rows, preferred_element_type=F32) * score_scale
    key_grad = jnp.einsum("bhqk,bqhd->bkhd", score_grad, queries, preferred_element_type=F32) * score_scale
    return (query_grad.astype(BF16), key_grad.astype(BF16), value_grad.astype(BF16))


def stream_forward(row_values, context, out_weight, up_weight, down_weight, gains, shifts):
    attended = matmul(context, out_weight)
    first_out, normed_one, inverse_one = layer_norm(row_values.astype(F32) + attended, gains[0], shifts[0])
    first_low = first_out.astype(BF16)
    before = matmul(first_low, up_weight)
    active = gelu_value(before).astype(BF16)
    second_out, normed_two, inverse_two = layer_norm(
        first_out + matmul(active, down_weight), gains[1], shifts[1]
    )
    kept_state = (normed_one, inverse_one, first_low, before, active, normed_two, inverse_two)
    return (second_out.astype(BF16), kept_state)


def stream_back(upstream, kept_state, out_weight, up_weight, down_weight, gains):
    normed_one, inverse_one, first_low, before, active, normed_two, inverse_two = kept_state
    branch_grad, gain_two, shift_two = norm_back(upstream.astype(F32), normed_two, inverse_two, gains[1])
    branch_low = branch_grad.astype(BF16)
    active_grad = project_back(branch_low, down_weight)
    before_grad = (active_grad * gelu_slope(before)).astype(BF16)
    first_grad = project_back(before_grad, up_weight) + branch_grad
    sum_grad, gain_one, shift_one = norm_back(first_grad, normed_one, inverse_one, gains[0])
    sum_low = sum_grad.astype(BF16)
    context_grad = project_back(sum_low, out_weight).astype(BF16)
    return sum_grad, context_grad, branch_low, before_grad, sum_low, (gain_one, gain_two, shift_one, shift_two)


def make_local(mesh):
    devices = mesh.shape["batch"] * mesh.shape["heads"]

    def local(
        text_states, image_states, caption_lengths, region_counts,
        text_query, text_key, text_value, text_output, text_up, text_down, text_gains, text_shifts,
        image_query, image_key, image_value, image_output, image_up, image_down, image_gains, image_shifts,
        text_upstream, image_upstream,
    ):
        def parts(grads):
            down, up, out, query, key, value = grads
            return query, key, value, out.T, up, down.T

        if mesh.shape["batch"] == 16 and mesh.shape["heads"] == 2:
            text_weights = (text_down, text_up, text_output, text_query, text_key, text_value)
            image_weights = (image_down, image_up, image_output, image_query, image_key, image_value)
            got = layer(
                (4, 2, 2), (caption_lengths, region_counts), (text_states, image_states), (text_upstream, image_upstream),
                (text_weights, image_weights), (text_gains, image_gains), (text_shifts, image_shifts),
            )
            return (
                got[0].reshape(text_states.shape), got[1], got[2].reshape(text_states.shape), got[3],
                *parts(got[4:10]), got[16], got[17], *parts(got[10:16]), got[18], got[19],
            )
        pair_count, cap_len, text_width = text_states.shape
        region_len, image_width = image_states.shape[1:]
        text_rows = text_states.reshape(pair_count * cap_len, text_width)
        image_rows = image_states.reshape(pair_count * region_len, image_width)
        core = lax.axis_index("heads")
        captions = lax.dynamic_slice(caption_lengths, (core * pair_count,), (pair_count,))
        regions = lax.dynamic_slice(region_counts, (core * pair_count,), (pair_count,))

        def heads_of(row_values, weight, length):
            return matmul(row_values, weight).astype(BF16).reshape(pair_count, length, HEADS, HEAD)

        tq, tk, tv = (heads_of(text_rows, w, cap_len) for w in (text_query, text_key, text_value))
        iq, ik, iv = (heads_of(image_rows, w, region_len) for w in (image_query, image_key, image_value))
        text_context, text_prob = attend(tq, ik, iv, regions)
        image_context, image_prob = attend(iq, tk, tv, captions)
        flat = lambda v: v.reshape(v.shape[0] * v.shape[1], -1)
        text_result, text_kept = stream_forward(
            text_rows, flat(text_context), text_output, text_up, text_down, text_gains, text_shifts
        )
        image_result, image_kept = stream_forward(
            image_rows, flat(image_context), image_output, image_up, image_down, image_gains, image_shifts
        )
        t_sum, t_cgrad, t_branch, t_zgrad, t_slow, t_small = stream_back(
            text_upstream.reshape(text_rows.shape), text_kept, text_output, text_up, text_down, text_gains
        )
        i_sum, i_cgrad, i_branch, i_zgrad, i_slow, i_small = stream_back(
            image_upstream.reshape(image_rows.shape), image_kept, image_output, image_up, image_down, image_gains
        )
        g_tq, g_ik, g_iv = attend_back(tq, ik, iv, text_prob, t_cgrad.reshape(tq.shape))
        g_iq, g_tk, g_tv = attend_back(iq, tk, tv, image_prob, i_cgrad.reshape(iq.shape))
        g_tq, g_tk, g_tv, g_iq, g_ik, g_iv = (flat(v) for v in (g_tq, g_tk, g_tv, g_iq, g_ik, g_iv))
        text_in = t_sum + project_back(g_tq, text_query) + project_back(g_tk, text_key) + project_back(g_tv, text_value)
        image_in = (
            i_sum + project_back(g_iq, image_query) + project_back(g_ik, image_key) + project_back(g_iv, image_value)
        )
        tl = (t_branch, text_kept[2], t_slow, text_rows)
        tr = (text_kept[4], t_zgrad, flat(text_context), g_tq, g_tk, g_tv)
        il = (i_branch, image_kept[2], i_slow, image_rows)
        ir = (image_kept[4], i_zgrad, flat(image_context), g_iq, g_ik, g_iv)
        wide = max(text_width, image_width)
        small = jnp.stack([jnp.pad(v, (0, wide - v.shape[0])) for v in t_small + i_small])
        me = lax.axis_index("batch") * mesh.shape["heads"] + core

        scatter = lambda v: lax.psum_scatter(v, ("batch", "heads"), scatter_dimension=0, tiled=True)
        text_grads = [scatter(outer_sum(tl[l], r)) for l, r in zip(LEFTS, tr)]
        image_grads = [scatter(outer_sum(il[l], r)) for l, r in zip(LEFTS, ir)]
        total = lax.psum(small, ("batch", "heads"))
        t_own, i_own = text_width // devices, image_width // devices
        t_norm = lax.dynamic_slice(total, (0, me * t_own), (4, t_own))
        i_norm = lax.dynamic_slice(total, (4, me * i_own), (4, i_own))
        return (
            text_result.reshape(text_states.shape),
            image_result.reshape(image_states.shape),
            text_in.astype(BF16).reshape(text_states.shape),
            image_in.astype(BF16).reshape(image_states.shape),
            *parts(text_grads), t_norm[:2], t_norm[2:],
            *parts(image_grads), i_norm[:2], i_norm[2:],
        )

    return local


def solution(mesh):
    rows = P(("batch", "heads"), None, None)
    first, second = P(("batch", "heads"), None), P(None, ("batch", "heads"))
    grads = (first, first, first, second, first, second, second, second)
    return jax.shard_map(
        make_local(mesh),
        mesh=mesh,
        in_specs=(rows, rows, P("batch"), P("batch"), *[P()] * 16, rows, rows),
        out_specs=(rows, rows, rows, rows, *grads, *grads),
        check_vma=False,
    )
```

```python
import functools
import math

import jax
import jax.numpy as jnp
from jax import lax
from jax.experimental import pallas as pl
from jax.experimental.pallas import tpu as pltpu
from jax.sharding import PartitionSpec as P

MESH_ID = pl.DeviceIdType.MESH
F32 = jnp.float32
BF16 = jnp.bfloat16
EPS = 1e-05
NEG = -1000000000.0
HEADS = 8
HEAD = 128
SCALE = 1.0 / math.sqrt(HEAD)
TILE = 256
CW = 256
LEFTS = (0, 1, 2, 3, 3, 3)
NT_DIMS = (((1,), (1,)), ((), ()))
TN_DIMS = (((0,), (0,)), ((), ()))
SLOTS = 6
G_RING, R_RING, Z_RING = 12, 12, 16
PRODUCED = ((1, 0), (1, 1), (1, 2), (0, 0), (0, 1), (0, 2), (1, 3), (0, 4), (0, 5), (0, 3), (1, 4), (1, 5))
SEQUENCE = (
    "i_qkv", "i_attend", "i_out", "i_ffn", "i_norm", "i_slope", "A0", "i_branch", "A1", "i_context", "t_q", "t_kv",
    "A2", "T0", "t_attend", "t_out", "T1", "t_ffn0", "t_ffn1", "t_ffn2", "T2", "t_norm", "A3", "t_slope0", "A4", "T3",
    "t_slope1", "A5", "T4", "t_slope2", "t_branch", "A6", "T5", "A7", "T6", "i_back", "A8", "T7", "t_context", "A9",
    "T8", "A10", "T9", "t_back", "A11", "T10", "A12", "T11", "A13", "T12", "i_final", "A14", "T13", "t_final", "A15",
    "T14", "T15", "T16", "T17", "T18", "T19",
)


def dot(a, b):
    return jnp.dot(a, b, preferred_element_type=F32)


def dot_nt(a, b):
    return lax.dot_general(a, b, NT_DIMS, preferred_element_type=F32)


def dot_tn(a, b):
    return lax.dot_general(a, b, TN_DIMS, preferred_element_type=F32)


def loop(n, body):
    def step(i, carry):
        body(i)
        return carry

    lax.fori_loop(0, n, step, 0)


def at(i, size):
    return pl.ds(pl.multiple_of(i * size, size), size)


def layer_kernel(dims, *refs):
    nz, ny, nx = dims
    refs = list(refs)

    def take(n):
        got = refs[:n]
        del refs[:n]
        return got

    cap_ref, reg_ref, xt_in, xi_in, ut_in, ui_in = take(6)
    w_in = [take(6), take(6)]
    gain_ref, shift_ref = take(2), take(2)
    res_t, res_i, sg_t, sg_i = take(4)
    w_out = [take(6), take(6)]
    norm_out = take(4)
    wbuf, x_t, x_i, raw_i, u_t, u_i = take(6)
    q_b, k_b, v_b = take(2), take(2), take(2)
    n1, inv, low, slope, acc, dctx, sums = take(2), take(2), take(2), take(2), take(2), take(2), take(2)
    lt = take(2)
    r_own, r_far = [take(6), take(6)], [take(6), take(6)]
    g_b, r1_b, r2_b, ru_b, rd_b = take(5)
    f_b = take(2)
    small, sv, sr = take(3)
    in_sem, w_sem, ex_s, ex_r, st_s, st_r, sm_s, sm_r = take(8)
    assert not refs

    b, h = lax.axis_index("batch"), lax.axis_index("heads")
    x, y, z = lax.rem(b, nx), lax.rem(lax.div(b, nx), ny), lax.div(b, nx * ny)

    def dev(zz, yy, xx):
        return ((zz * ny + yy) * nx + xx, h)

    partner, nbr_x, nbr_y = (b, 1 - h), dev(z, y, 1 - x), dev(z, 1 - y, x)
    barrier = pltpu.get_barrier_semaphore()
    for who in (partner, nbr_x, nbr_y):
        pl.semaphore_signal(barrier, inc=1, device_id=who, device_id_type=MESH_ID)
    for off in range(1, nz):
        pl.semaphore_signal(barrier, inc=1, device_id=dev(lax.rem(z + off, nz), y, x), device_id_type=MESH_ID)

    def remote(src, dst, ssem, rsem, who):
        return pltpu.make_async_remote_copy(
            src_ref=src, dst_ref=dst, send_sem=ssem, recv_sem=rsem, device_id=who, device_id_type=MESH_ID
        )

    T, I = 0, 1
    pieces = []

    def piece(name, ref, rows, cols):
        pieces.append((name, ref, rows, cols))

    td, ti = x_t.shape[1], x_i.shape[1]
    inner = q_b[0].shape[1]
    parts = w_in[T][1].shape[1] // 1024
    whole = lambda s, w: w_in[s][w]
    tu = lambda j: w_in[T][1].at[:, pl.ds(j * 1024, 1024)]
    tw = lambda j: w_in[T][0].at[pl.ds(j * 1024, 1024), :]
    piece("tk", whole(T, 4), td, inner)
    piece("tv", whole(T, 5), td, inner)
    piece("iq", whole(I, 3), ti, inner)
    piece("io", whole(I, 2), inner, ti)
    piece("iu", whole(I, 1), ti, ti)
    piece("id", whole(I, 0), ti, ti)
    piece("tq", whole(T, 3), td, inner)
    piece("ik", whole(I, 4), ti, inner)
    piece("iv", whole(I, 5), ti, inner)
    piece("to", whole(T, 2), inner, td)
    for j in range(parts):
        piece("tu%d" % j, tu(j), td, 1024)
        piece("td%d" % j, tw(j), 1024, td)
    piece("to", whole(T, 2), inner, td)
    for name, s, w in (("iq", I, 3), ("tk", T, 4), ("tv", T, 5), ("tq", T, 3), ("ik", I, 4), ("iv", I, 5)):
        rows = td if s == T else ti
        piece(name, whole(s, w), rows, inner)
    issued = [0]
    held = {}

    def weight_copy(k, slot):
        name, ref, rows, cols = pieces[k]
        return pltpu.make_async_copy(ref, wbuf.at[slot, pl.ds(0, rows), pl.ds(0, cols)], w_sem.at[slot])

    def issue(slot):
        if issued[0] < len(pieces):
            k = issued[0]
            issued[0] += 1
            weight_copy(k, slot).start()
            assert pieces[k][0] not in held
            held[pieces[k][0]] = [k, slot, False]

    def weight(name):
        k, slot, ready = held[name]
        if not ready:
            weight_copy(k, slot).wait()
            held[name][2] = True
        _, _, rows, cols = pieces[k]
        return wbuf.at[slot, pl.ds(0, rows), pl.ds(0, cols)]

    def release(name):
        k, slot, ready = held.pop(name)
        issue(slot)

    in_copies = [
        pltpu.make_async_copy(s, d, in_sem.at[i])
        for i, (s, d) in enumerate(((xt_in, x_t), (xi_in, raw_i.at[0]), (ut_in, u_t), (ui_in, raw_i.at[1])))
    ]
    in_copies[0].start()
    issue(0)
    in_copies[1].start()
    issue(1)
    issue(2)
    in_copies[3].start()
    in_copies[2].start()
    for slot in range(3, SLOTS):
        issue(slot)

    pairs_n, regions = raw_i.shape[1], raw_i.shape[2]
    cap = x_t.shape[0] // pairs_n
    pad = 112
    m_i, m_t = pairs_n * pad, x_t.shape[0]
    m_of, d_of = (m_t, m_i), (td, ti)
    x_of = (x_t, x_i)

    tail = pl.ds(m_i, x_i.shape[0] - m_i)
    for ref in (x_i, low[I], *r_own[I]):
        ref[tail, :] = jnp.zeros((x_i.shape[0] - m_i, ref.shape[1]), BF16)
    for ref in (*sums,):
        ref[...] = jnp.zeros(ref.shape, F32)

    def spread(src, dst):
        for p in range(pairs_n):
            dst[pl.ds(p * pad, regions), :] = src[p]
            dst[pl.ds(p * pad + regions, pad - regions), :] = jnp.zeros((pad - regions, dst.shape[1]), BF16)

    lengths = {
        T: [reg_ref[h * pairs_n + p] for p in range(pairs_n)],
        I: [cap_ref[h * pairs_n + p] for p in range(pairs_n)],
    }

    ex_left, ex_right = {}, {}
    n_left = max(LEFTS) + 1
    for s in (T, I):
        for l in range(n_left):
            k = s * n_left + l
            ex_left[s, l] = remote(
                lt[s].at[l, :, pl.ds(0, 256)], lt[s].at[l, :, pl.ds(256, 256)], ex_s.at[k], ex_r.at[k], partner
            )
        for w in range(6):
            k = 2 * n_left + s * 6 + w
            half = r_far[s][w].shape[1]
            ex_right[s, w] = remote(
                r_own[s][w].at[:, pl.ds(pl.multiple_of((1 - h) * half, 128), half)], r_far[s][w],
                ex_s.at[k], ex_r.at[k], partner,
            )
    arrived = set()
    entered = []

    def enter():
        if not entered:
            entered.append(1)
            pl.semaphore_wait(barrier, 3 + nz - 1)

    def send_left(s, l, src):
        def body(j):
            lt[s][l, at(j, TILE), pl.ds(0, 256)] = src[:, at(j, TILE)].T

        loop(d_of[s] // TILE, body)
        enter()
        ex_left[s, l].start()

    def send_right(s, w):
        enter()
        ex_right[s, w].start()

    def project(src, rows, w, dst):
        def body(j):
            dst[pl.ds(0, rows), at(j, TILE)] = dot(src[pl.ds(0, rows), :], w[:, at(j, TILE)]).astype(BF16)

        loop(w.shape[1] // TILE, body)

    def softmax(q, k, live):
        s = dot_nt(q, k) * SCALE
        mask = lax.broadcasted_iota(jnp.int32, s.shape, 1) < live
        s = jnp.where(mask, s, NEG)
        e = jnp.exp(s - jnp.max(s, axis=-1, keepdims=True))
        return e / jnp.sum(e, axis=-1, keepdims=True)

    span = (cap, pad)

    def rows_of(s, p):
        return pl.ds(p * span[s], span[s])

    def attend(s):
        o = 1 - s

        def body(i):
            cols = at(i, HEAD)
            for p in range(pairs_n):
                q, k = q_b[s][rows_of(s, p), cols], k_b[o][rows_of(o, p), cols]
                prob = softmax(q, k, lengths[s][p]).astype(BF16)
                r_own[s][2][rows_of(s, p), cols] = dot(prob, v_b[o][rows_of(o, p), cols]).astype(BF16)

        loop(HEADS, body)
        send_right(s, 2)

    def attend_back(s):
        o = 1 - s

        def body(i):
            cols = at(i, HEAD)
            for p in range(pairs_n):
                rq, rk = rows_of(s, p), rows_of(o, p)
                q, k, v, dc = q_b[s][rq, cols], k_b[o][rk, cols], v_b[o][rk, cols], dctx[s][rq, cols]
                prob = softmax(q, k, lengths[s][p])
                dp = dot_nt(dc, v)
                ds = (prob * (dp - jnp.sum(prob * dp, axis=-1, keepdims=True))).astype(BF16)
                r_own[s][3][rq, cols] = (dot(ds, k) * SCALE).astype(BF16)
                r_own[o][4][rk, cols] = (dot_tn(ds, q) * SCALE).astype(BF16)
                r_own[o][5][rk, cols] = dot_tn(prob.astype(BF16), dc).astype(BF16)

        loop(HEADS, body)
        send_right(s, 3)
        send_right(o, 4)
        send_right(o, 5)

    RB = 32

    def mean(v):
        return jnp.mean(v, axis=-1, keepdims=True)

    def sum8(v):
        return jnp.sum(v.reshape(v.shape[0] // 8, 8, v.shape[1]), axis=0)

    def norm_one(s):
        gain, shift = gain_ref[s][0:1, :], shift_ref[s][0:1, :]

        def body(i):
            r = at(i, RB)
            v = x_of[s][r, :].astype(F32) + acc[s][r, :]
            c = v - mean(v)
            iv = lax.rsqrt(mean(c * c) + EPS)
            n = c * iv
            n1[s][r, :] = n
            inv[s][r, :] = jnp.broadcast_to(iv, (RB, 128))
            low[s][r, :] = (n * gain + shift).astype(BF16)

        loop(m_of[s] // RB, body)
        send_left(s, 1, low[s])

    def norm_two(s, up_ref, res_ref):
        gain0, shift0 = gain_ref[s][0:1, :], shift_ref[s][0:1, :]
        gain, shift = gain_ref[s][1:2, :], shift_ref[s][1:2, :]

        def body(i):
            r = at(i, RB)
            v = n1[s][r, :] * gain0 + shift0 + acc[s][r, :]
            c = v - mean(v)
            iv = lax.rsqrt(mean(c * c) + EPS)
            n = c * iv
            up = up_ref[r, :].astype(F32)
            res_ref[r, :] = (n * gain + shift).astype(BF16)
            un = up * n
            sums[s][1] = sums[s][1] + sum8(un)
            sums[s][3] = sums[s][3] + sum8(up)
            u = up * gain
            d = iv * (u - mean(u) - n * mean(un * gain))
            acc[s][r, :] = d
            low[s][r, :] = d.astype(BF16)

        loop(m_of[s] // RB, body)
        send_left(s, 0, low[s])

    def norm_one_back(s):
        gain = gain_ref[s][0:1, :]

        def body(i):
            r = at(i, RB)
            g, n = acc[s][r, :], n1[s][r, :]
            gn = g * n
            sums[s][0] = sums[s][0] + sum8(gn)
            sums[s][2] = sums[s][2] + sum8(g)
            u = g * gain
            d = inv[s][r, 0:1] * (u - mean(u) - n * mean(gn * gain))
            acc[s][r, :] = d
            low[s][r, :] = d.astype(BF16)

        loop(m_of[s] // RB, body)
        send_left(s, 2, low[s])

    def out_project(s, w):
        m = m_of[s]

        def body(j):
            acc[s][pl.ds(0, m), at(j, TILE)] = dot(r_own[s][2][pl.ds(0, m), :], w[:, at(j, TILE)])

        loop(d_of[s] // TILE, body)

    def ffn(s, j, up_w, down_w):
        m, base = m_of[s], j * 1024

        def hidden(i):
            c = pl.ds(pl.multiple_of(base + i * TILE, TILE), TILE)
            v = dot(low[s][pl.ds(0, m), :], up_w[:, at(i, TILE)])
            half = 0.5 * (1.0 + lax.erf(v * (1.0 / math.sqrt(2.0))))
            r_own[s][0][pl.ds(0, m), c] = (v * half).astype(BF16)
            slope[s][pl.ds(0, m), c] = (half + v * jnp.exp(-0.5 * v * v) * (1.0 / math.sqrt(2.0 * math.pi))).astype(BF16)

        loop(1024 // TILE, hidden)

        def second(i):
            part = dot(r_own[s][0][pl.ds(0, m), pl.ds(base, 1024)], down_w[:, at(i, TILE)])
            if j == 0:
                acc[s][pl.ds(0, m), at(i, TILE)] = part
            else:
                acc[s][pl.ds(0, m), at(i, TILE)] += part

        loop(d_of[s] // TILE, second)

    def slope_back(s, j, down_w):
        m, base = m_of[s], j * 1024

        def body(i):
            c = pl.ds(pl.multiple_of(base + i * TILE, TILE), TILE)
            g = dot_nt(low[s][pl.ds(0, m), :], down_w[at(i, TILE), :])
            r_own[s][1][pl.ds(0, m), c] = (g * slope[s][pl.ds(0, m), c].astype(F32)).astype(BF16)

        loop(1024 // TILE, body)

    def back_add(s, src, cols, w):
        m = m_of[s]

        def body(i):
            acc[s][pl.ds(0, m), at(i, TILE)] += dot_nt(src[pl.ds(0, m), cols], w[at(i, TILE), :])

        loop(d_of[s] // TILE, body)

    def context_back(s, w):
        m = m_of[s]

        def body(i):
            dctx[s][pl.ds(0, m), at(i, TILE)] = dot_nt(low[s][pl.ds(0, m), :], w[at(i, TILE), :]).astype(BF16)

        loop(inner // TILE, body)

    def final(s, dst):
        def body(i):
            dst[at(i, RB), :] = acc[s][at(i, RB), :].astype(BF16)

        loop(m_of[s] // RB, body)

    def gather_rows(src, dst):
        for p in range(pairs_n):
            dst[p] = src[pl.ds(p * pad, regions), :]

    all_cols = pl.ds(0, 1024)

    def step(name):
        if name == "i_qkv":
            in_copies[0].wait()
            project(x_t, m_t, weight("tk"), k_b[T])
            release("tk")
            project(x_t, m_t, weight("tv"), v_b[T])
            release("tv")
            in_copies[1].wait()
            spread(raw_i.at[0], x_i)
            project(x_i, m_i, weight("iq"), q_b[I])
            release("iq")
        elif name == "i_attend":
            attend(I)
        elif name == "i_out":
            out_project(I, weight("io"))
            norm_one(I)
        elif name == "i_ffn":
            ffn(I, 0, weight("iu"), weight("id"))
            send_right(I, 0)
        elif name == "i_norm":
            in_copies[3].wait()
            spread(raw_i.at[1], u_i)
            norm_two(I, u_i, u_i)
            gather_rows(u_i, res_i)
        elif name == "i_slope":
            slope_back(I, 0, weight("id"))
            send_right(I, 1)
            release("id")
        elif name == "i_branch":
            back_add(I, r_own[I][1], all_cols, weight("iu"))
            release("iu")
            norm_one_back(I)
        elif name == "i_context":
            context_back(I, weight("io"))
            release("io")
            send_left(I, 3, x_i)
        elif name == "t_q":
            project(x_t, m_t, weight("tq"), q_b[T])
            release("tq")
            send_left(T, 3, x_t)
        elif name == "t_kv":
            project(x_i, m_i, weight("ik"), k_b[I])
            release("ik")
            project(x_i, m_i, weight("iv"), v_b[I])
            release("iv")
        elif name == "t_attend":
            attend(T)
        elif name == "t_out":
            out_project(T, weight("to"))
            release("to")
            norm_one(T)
        elif name.startswith("t_ffn"):
            j = int(name[-1])
            ffn(T, j, weight("tu%d" % j), weight("td%d" % j))
            if j == parts - 1:
                send_right(T, 0)
        elif name == "t_norm":
            in_copies[2].wait()
            norm_two(T, u_t, res_t)
        elif name.startswith("t_slope"):
            j = int(name[-1])
            slope_back(T, j, weight("td%d" % j))
            release("td%d" % j)
            if j == parts - 1:
                send_right(T, 1)
        elif name == "t_branch":
            for j in range(parts):
                back_add(T, r_own[T][1], pl.ds(j * 1024, 1024), weight("tu%d" % j))
                release("tu%d" % j)
            norm_one_back(T)
            small_fill()
        elif name == "t_context":
            context_back(T, weight("to"))
            release("to")
        elif name == "i_back":
            attend_back(I)
            back_add(I, r_own[I][3], all_cols, weight("iq"))
            release("iq")
            back_add(T, r_own[T][4], all_cols, weight("tk"))
            release("tk")
            back_add(T, r_own[T][5], all_cols, weight("tv"))
            release("tv")
        elif name == "t_back":
            attend_back(T)
        elif name == "i_final":
            back_add(I, r_own[I][4], all_cols, weight("ik"))
            release("ik")
            back_add(I, r_own[I][5], all_cols, weight("iv"))
            release("iv")
            final(I, u_i)
            gather_rows(u_i, sg_i)
        elif name == "t_final":
            back_add(T, r_own[T][3], all_cols, weight("tq"))
            release("tq")
            final(T, sg_t)
        elif name[0] == "A":
            for c in (2 * int(name[1:]), 2 * int(name[1:]) + 1):
                compute(c)
                s1(c).start()
        else:
            tick(int(name[1:]))

    small_copies = []

    def small_start(src, dst, i, who):
        c = remote(src, dst, sm_s.at[i], sm_r.at[i], who)
        c.start()
        small_copies.append(c)

    def small_fill():
        small[...] = jnp.zeros(small.shape, F32)
        for s in (T, I):
            for k in range(4):
                small[pl.ds(4 * s + k, 1), pl.ds(0, d_of[s])] = jnp.sum(sums[s][k], axis=0, keepdims=True)

    def small_step(i):
        if i == 0:
            small_start(small, sr.at[0], 0, partner)
        elif i == 1:
            small_copies[0].wait_recv()
            sv[0] = small[...] + sr[0]
            small_start(sv.at[0], sr.at[1], 1, nbr_x)
        elif i == 2:
            small_copies[1].wait_recv()
            sv[1] = sv[0] + sr[1]
            small_start(sv.at[1], sr.at[2], 2, nbr_y)
        elif i == 3:
            small_copies[2].wait_recv()
            sv[2] = sv[1] + sr[2]
            for off in range(1, nz):
                small_start(sv.at[2], sr.at[2 + off], 2 + off, dev(lax.rem(z + off, nz), y, x))
        elif i == 4:
            total = sv[2]
            for off in range(1, nz):
                small_copies[2 + off].wait_recv()
                total = total + sr[2 + off]
            wide = total.shape[1]
            me = b * 2 + h
            for s in (T, I):
                own = norm_out[2 * s].shape[1]
                mine = pltpu.roll(total, lax.rem(wide - me * own, wide), 1)
                norm_out[2 * s][...] = mine[4 * s : 4 * s + 2, :own]
                norm_out[2 * s + 1][...] = mine[4 * s + 2 : 4 * s + 4, :own]

    chunks = []
    for s, w in PRODUCED:
        for o in range(0, r_far[s][w].shape[1], CW):
            chunks.append((s, w, o, "xy"[len(chunks) % 2], len([1 for c in chunks if c[0] == s])))
    n = len(chunks)

    def bufs(c):
        rows = pl.ds(0, d_of[chunks[c][0]] // (nz * ny * nx))
        return (
            g_b.at[c % G_RING, :, :, :, rows], r1_b.at[c % R_RING, :, :, rows], r2_b.at[c % R_RING, :, rows],
            ru_b.at[c % Z_RING, :, rows], rd_b.at[c % Z_RING, :, rows],
        )

    def compute(c):
        s, w, o, way, _ = chunks[c]
        for copy, key in ((ex_left[s, LEFTS[w]], (0, s, LEFTS[w])), (ex_right[s, w], (1, s, w))):
            if key not in arrived:
                arrived.add(key)
                copy.wait_recv()
        blk = d_of[s] // (nz * ny * nx)
        size = ny * nx * blk
        half = r_far[s][w].shape[1]
        mine = pl.ds(pl.multiple_of(h * half + o, 128), CW)
        g = g_b.at[c % G_RING]

        def body(i):
            r = pl.ds(pl.multiple_of(i * size, 64), size)
            l = LEFTS[w]
            res = dot(lt[s][l, r, pl.ds(0, 256)], r_own[s][w][:, mine]) + dot(
                lt[s][l, r, pl.ds(256, 256)], r_far[s][w][:, pl.ds(o, CW)]
            )
            g[i, :, :, pl.ds(0, blk)] = res.astype(BF16).reshape(ny, nx, blk, CW)

        loop(nz, body)

    def add(dst, src):
        dst[...] = (dst[...].astype(F32) + src[...].astype(F32)).astype(BF16)

    def s1(c):
        g, r1 = bufs(c)[:2]
        if chunks[c][3] == "x":
            return remote(g.at[:, :, 1 - x], r1, st_s.at[0, c], st_r.at[0, c], nbr_x)
        return remote(g.at[:, 1 - y], r1, st_s.at[0, c], st_r.at[0, c], nbr_y)

    def s2(c):
        g, _, r2 = bufs(c)[:3]
        if chunks[c][3] == "x":
            return remote(g.at[:, 1 - y, x], r2, st_s.at[1, c], st_r.at[1, c], nbr_y)
        return remote(g.at[:, y, 1 - x], r2, st_s.at[1, c], st_r.at[1, c], nbr_x)

    def up(c, k):
        g, ru = bufs(c)[0], bufs(c)[3]
        rest = pl.ds(k + 1, nz - 1 - k)
        return remote(g.at[rest, y, x], ru.at[rest], st_s.at[2, c], st_r.at[2, c], dev(k + 1, y, x))

    def down(c, k):
        g, rd = bufs(c)[0], bufs(c)[4]
        rest = pl.ds(0, k)
        return remote(g.at[rest, y, x], rd.at[rest], st_s.at[3, c], st_r.at[3, c], dev(k - 1, y, x))

    def swap(c):
        s, w, o, _, k = chunks[c]
        out = w_out[s][w]
        half = out.shape[1] // 2
        return remote(
            f_b[s].at[k], out.at[:, pl.ds(pl.multiple_of(h * half + o, 128), CW)],
            st_s.at[4, c], st_r.at[4, c], partner,
        )

    def stage2(c):
        s1(c).wait_recv()
        g, r1 = bufs(c)[:2]

        def body(i):
            for j in range(2):
                add(g.at[i, j, x] if chunks[c][3] == "x" else g.at[i, y, j], r1.at[i, j])

        loop(nz, body)
        s2(c).start()

    def stage3(c):
        s2(c).wait_recv()
        g, _, r2 = bufs(c)[:3]
        loop(nz, lambda i: add(g.at[i, y, x], r2.at[i]))

        @pl.when(z == 0)
        def _():
            up(c, 0).start()

        @pl.when(z == nz - 1)
        def _():
            down(c, nz - 1).start()

    def hop(c, d):
        g, _, _, ru, rd = bufs(c)

        @pl.when(z == d)
        def _():
            up(c, d - 1).wait_recv()
            for t in range(d + 1, nz):
                add(g.at[t, y, x], ru.at[t])
            up(c, d).start()

        @pl.when(z == nz - 1 - d)
        def _():
            down(c, nz - d).wait_recv()
            for t in range(0, nz - 1 - d):
                add(g.at[t, y, x], rd.at[t])
            down(c, nz - 1 - d).start()

    def finish(c):
        g, _, _, ru, rd = bufs(c)
        s, w, o, _, idx = chunks[c]
        out = w_out[s][w]
        r, half = out.shape[0], out.shape[1] // 2
        cols = pl.ds(pl.multiple_of(h * half + o, 128), CW)
        for k in range(nz):

            @pl.when(z == k)
            def _(k=k):
                if k == nz - 1:
                    up(c, k - 1).wait_recv()
                if k == 0:
                    down(c, 1).wait_recv()
                total = g[k, y, x].astype(F32)
                if k > 0:
                    total = total + ru[k].astype(F32)
                if k < nz - 1:
                    total = total + rd[k].astype(F32)
                first, second = total[:r], total[r:]
                out[:, cols] = jnp.where(h == 0, first, second)
                f_b[s][idx] = jnp.where(h == 0, second, first)

        swap(c).start()
        s1(c).wait_send()
        s2(c).wait_send()
        for k in range(nz):

            @pl.when(z == k)
            def _(k=k):
                if k < nz - 1:
                    up(c, k).wait_send()
                if k > 0:
                    down(c, k).wait_send()

    pairs = n // 2
    small_from = 6

    def tick(t):
        for lag, stage in (
            (0, stage2), (1, stage3), *[(1 + d, functools.partial(hop, d=d)) for d in range(1, nz - 1)], (nz, finish)
        ):
            p = t - lag
            if 0 <= p < pairs:
                stage(2 * p)
                stage(2 * p + 1)
        if small_from <= t < small_from + 5:
            small_step(t - small_from)

    for name in SEQUENCE:
        step(name)

    for c in range(n):
        swap(c).wait_recv()
        swap(c).wait_send()
    for copy in (*ex_left.values(), *ex_right.values()):
        copy.wait_send()
    for copy in small_copies:
        copy.wait_send()


def hand_over(turned, *refs):
    n = (len(refs) - 1 - len(turned)) // 2
    ins, outs, scratch, sem = refs[:n], refs[n : 2 * n], refs[2 * n : -1], refs[-1]
    copies = []

    def send(i, src):
        copies.append(pltpu.make_async_copy(src, outs[i], sem.at[i]))
        copies[-1].start()

    for i in range(n):
        if i not in turned:
            send(i, ins[i])
    for i, ref in zip(turned, scratch):
        ref[...] = ins[i][...].T
        send(i, ref)
    for c in copies:
        c.wait()


def layer(dims, lengths, states, upstream, weights, gains, shifts):
    nz, ny, nx = dims
    chips = nz * ny * nx
    xt, xi = states
    pairs, cap, td = xt.shape
    regions, ti = xi.shape[1:]
    xt, ut = xt.reshape(pairs * cap, td), upstream[0].reshape(pairs * cap, td)
    mt = pairs * cap
    fixed = 256
    inner = weights[0][3].shape[1]
    d_of = (td, ti)
    cols = [[w.shape[0], weights[s][1].shape[1], inner, inner, inner, inner] for s, w in ((0, weights[0][0]), (1, weights[1][0]))]
    V, DMA = pltpu.VMEM, pltpu.SemaphoreType.DMA
    rows_of = (mt, fixed)
    ti_blk = ti // chips
    counts = [sum(c // 2 // CW for c in cols[s]) for s in range(2)]
    n = sum(counts)
    act = lambda dt, width: [V((rows_of[s], width[s]), dt) for s in range(2)]
    scratch = [
        V((SLOTS, 1024, 1024), BF16),
        V((mt, td), BF16), V((fixed, ti), BF16), V((2, pairs, regions, ti), BF16), V((mt, td), BF16), V((fixed, ti), BF16),
        *act(BF16, (inner, inner)), *act(BF16, (inner, inner)), *act(BF16, (inner, inner)),
        *act(F32, d_of), *act(F32, (128, 128)), *act(BF16, d_of), *act(BF16, (cols[0][1], cols[1][1])),
        *act(F32, d_of), *act(BF16, (inner, inner)),
        *[V((4, 8, d), F32) for d in d_of],
        *[V((4, d, 512), BF16) for d in d_of],
        *[V((rows_of[s], c), BF16) for s in range(2) for c in cols[s]],
        *[V((rows_of[s], c // 2), BF16) for s in range(2) for c in cols[s]],
        V((G_RING, nz, ny, nx, ti_blk, CW), BF16),
        V((R_RING, nz, 2, ti_blk, CW), BF16),
        V((R_RING, nz, ti_blk, CW), BF16),
        V((Z_RING, nz, ti_blk, CW), BF16),
        V((Z_RING, nz, ti_blk, CW), BF16),
        *[V((counts[s], d_of[s] // chips // 2, CW), F32) for s in range(2)],
        V((8, max(d_of)), F32), V((3, 8, max(d_of)), F32), V((2 + nz, 8, max(d_of)), F32),
        DMA((4,)), DMA((SLOTS,)), DMA((20,)), DMA((20,)), DMA((5, n)), DMA((5, n)), DMA((2 + nz,)), DMA((2 + nz,)),
    ]
    hbm = pl.BlockSpec(memory_space=pl.ANY)
    vm = pl.BlockSpec(memory_space=pltpu.VMEM)
    smem = pl.BlockSpec(memory_space=pltpu.SMEM)
    sds = jax.ShapeDtypeStruct
    outs = [
        sds((mt, td), BF16), sds((pairs, regions, ti), BF16), sds((mt, td), BF16), sds((pairs, regions, ti), BF16),
        *[sds((d_of[s] // chips // 2, c), F32) for s in range(2) for c in cols[s]],
        *[sds((2, d_of[s] // chips // 2), F32) for s in range(2) for _ in range(2)],
    ]
    turned = (4, 6, 10, 12)
    got = pl.pallas_call(
        functools.partial(layer_kernel, dims),
        out_shape=outs,
        in_specs=[smem, smem, *[hbm] * 4, *[hbm] * 12, *[vm] * 4],
        out_specs=[vm] * len(outs),
        scratch_shapes=scratch,
        compiler_params=pltpu.CompilerParams(
            collective_id=0, has_side_effects=True, vmem_limit_bytes=67043328
        ),
        name="co_layer",
    )(*lengths, xt, xi, ut, upstream[1], *weights[0], *weights[1], *gains, *shifts)
    n = len(got)
    return pl.pallas_call(
        functools.partial(hand_over, turned),
        out_shape=[sds(v.shape[::-1] if i in turned else v.shape, v.dtype) for i, v in enumerate(outs)],
        in_specs=[vm] * n,
        out_specs=[hbm] * n,
        scratch_shapes=[*[V(outs[i].shape[::-1], F32) for i in turned], DMA((n,))],
        name="hand_over",
    )(*got)


def matmul(row_values, weight):
    return jnp.dot(row_values, weight, preferred_element_type=F32)


def project_back(gradient, weight):
    return lax.dot_general(gradient, weight, (((1,), (1,)), ((), ())), preferred_element_type=F32)


def outer_sum(row_values, gradient):
    return lax.dot_general(row_values, gradient, (((0,), (0,)), ((), ())), preferred_element_type=F32)


def layer_norm(values, gain, shift):
    row_mean = jnp.mean(values, axis=-1, keepdims=True)
    centred = values - row_mean
    spread = jnp.mean(centred * centred, axis=-1, keepdims=True)
    inverse = lax.rsqrt(spread + EPS)
    normed = centred * inverse
    return (normed * gain + shift, normed, inverse)


def norm_back(gradient, normed, inverse, gain):
    scaled = gradient * gain
    first_mean = jnp.mean(scaled, axis=-1, keepdims=True)
    second_mean = jnp.mean(scaled * normed, axis=-1, keepdims=True)
    into = inverse * (scaled - first_mean - normed * second_mean)
    return (into, jnp.sum(gradient * normed, axis=0), jnp.sum(gradient, axis=0))


def gelu_value(values):
    return 0.5 * values * (1.0 + jax.scipy.special.erf(values / math.sqrt(2.0)))


def gelu_slope(values):
    return 0.5 * (1.0 + jax.scipy.special.erf(values / math.sqrt(2.0))) + values * jnp.exp(
        -0.5 * values * values
    ) / math.sqrt(2.0 * math.pi)


def attend(queries, key_rows, value_rows, lengths):
    score_scale = 1.0 / math.sqrt(queries.shape[-1])
    scores = jnp.einsum("bqhd,bkhd->bhqk", queries, key_rows, preferred_element_type=F32) * score_scale
    live_mask = lax.broadcasted_iota(jnp.int32, scores.shape, 3) < lengths[:, None, None, None]
    scores = jnp.where(live_mask, scores, NEG)
    weights = jnp.exp(scores - jnp.max(scores, axis=-1, keepdims=True))
    probability = weights / jnp.sum(weights, axis=-1, keepdims=True)
    context = jnp.einsum("bhqk,bkhd->bqhd", probability.astype(BF16), value_rows, preferred_element_type=F32)
    return context.astype(BF16), probability


def attend_back(queries, key_rows, value_rows, probability, context_grad):
    score_scale = 1.0 / math.sqrt(queries.shape[-1])
    value_grad = jnp.einsum(
        "bhqk,bqhd->bkhd", probability.astype(BF16), context_grad, preferred_element_type=F32
    )
    prob_grad = jnp.einsum("bqhd,bkhd->bhqk", context_grad, value_rows, preferred_element_type=F32)
    row_inner = jnp.sum(probability * prob_grad, axis=-1, keepdims=True)
    score_grad = (probability * (prob_grad - row_inner)).astype(BF16)
    query_grad = jnp.einsum("bhqk,bkhd->bqhd", score_grad, key_rows, preferred_element_type=F32) * score_scale
    key_grad = jnp.einsum("bhqk,bqhd->bkhd", score_grad, queries, preferred_element_type=F32) * score_scale
    return (query_grad.astype(BF16), key_grad.astype(BF16), value_grad.astype(BF16))


def stream_forward(row_values, context, out_weight, up_weight, down_weight, gains, shifts):
    attended = matmul(context, out_weight)
    first_out, normed_one, inverse_one = layer_norm(row_values.astype(F32) + attended, gains[0], shifts[0])
    first_low = first_out.astype(BF16)
    before = matmul(first_low, up_weight)
    active = gelu_value(before).astype(BF16)
    second_out, normed_two, inverse_two = layer_norm(
        first_out + matmul(active, down_weight), gains[1], shifts[1]
    )
    kept_state = (normed_one, inverse_one, first_low, before, active, normed_two, inverse_two)
    return (second_out.astype(BF16), kept_state)


def stream_back(upstream, kept_state, out_weight, up_weight, down_weight, gains):
    normed_one, inverse_one, first_low, before, active, normed_two, inverse_two = kept_state
    branch_grad, gain_two, shift_two = norm_back(upstream.astype(F32), normed_two, inverse_two, gains[1])
    branch_low = branch_grad.astype(BF16)
    active_grad = project_back(branch_low, down_weight)
    before_grad = (active_grad * gelu_slope(before)).astype(BF16)
    first_grad = project_back(before_grad, up_weight) + branch_grad
    sum_grad, gain_one, shift_one = norm_back(first_grad, normed_one, inverse_one, gains[0])
    sum_low = sum_grad.astype(BF16)
    context_grad = project_back(sum_low, out_weight).astype(BF16)
    return sum_grad, context_grad, branch_low, before_grad, sum_low, (gain_one, gain_two, shift_one, shift_two)


def make_local(mesh):
    devices = mesh.shape["batch"] * mesh.shape["heads"]

    def local(
        text_states, image_states, caption_lengths, region_counts,
        text_query, text_key, text_value, text_output, text_up, text_down, text_gains, text_shifts,
        image_query, image_key, image_value, image_output, image_up, image_down, image_gains, image_shifts,
        text_upstream, image_upstream,
    ):
        def named(grads):
            down, up, out, query, key, value = grads
            return query, key, value, out, up, down

        def parts(grads):
            down, up, out, query, key, value = grads
            return named((down.T, up, out.T, query, key, value))

        if mesh.shape["batch"] == 16 and mesh.shape["heads"] == 2:
            text_weights = (text_down, text_up, text_output, text_query, text_key, text_value)
            image_weights = (image_down, image_up, image_output, image_query, image_key, image_value)
            got = layer(
                (4, 2, 2), (caption_lengths, region_counts), (text_states, image_states), (text_upstream, image_upstream),
                (text_weights, image_weights), (text_gains, image_gains), (text_shifts, image_shifts),
            )
            return (
                got[0].reshape(text_states.shape), got[1], got[2].reshape(text_states.shape), got[3],
                *named(got[4:10]), got[16], got[17], *named(got[10:16]), got[18], got[19],
            )
        pair_count, cap_len, text_width = text_states.shape
        region_len, image_width = image_states.shape[1:]
        text_rows = text_states.reshape(pair_count * cap_len, text_width)
        image_rows = image_states.reshape(pair_count * region_len, image_width)
        core = lax.axis_index("heads")
        captions = lax.dynamic_slice(caption_lengths, (core * pair_count,), (pair_count,))
        regions = lax.dynamic_slice(region_counts, (core * pair_count,), (pair_count,))

        def heads_of(row_values, weight, length):
            return matmul(row_values, weight).astype(BF16).reshape(pair_count, length, HEADS, HEAD)

        tq, tk, tv = (heads_of(text_rows, w, cap_len) for w in (text_query, text_key, text_value))
        iq, ik, iv = (heads_of(image_rows, w, region_len) for w in (image_query, image_key, image_value))
        text_context, text_prob = attend(tq, ik, iv, regions)
        image_context, image_prob = attend(iq, tk, tv, captions)
        flat = lambda v: v.reshape(v.shape[0] * v.shape[1], -1)
        text_result, text_kept = stream_forward(
            text_rows, flat(text_context), text_output, text_up, text_down, text_gains, text_shifts
        )
        image_result, image_kept = stream_forward(
            image_rows, flat(image_context), image_output, image_up, image_down, image_gains, image_shifts
        )
        t_sum, t_cgrad, t_branch, t_zgrad, t_slow, t_small = stream_back(
            text_upstream.reshape(text_rows.shape), text_kept, text_output, text_up, text_down, text_gains
        )
        i_sum, i_cgrad, i_branch, i_zgrad, i_slow, i_small = stream_back(
            image_upstream.reshape(image_rows.shape), image_kept, image_output, image_up, image_down, image_gains
        )
        g_tq, g_ik, g_iv = attend_back(tq, ik, iv, text_prob, t_cgrad.reshape(tq.shape))
        g_iq, g_tk, g_tv = attend_back(iq, tk, tv, image_prob, i_cgrad.reshape(iq.shape))
        g_tq, g_tk, g_tv, g_iq, g_ik, g_iv = (flat(v) for v in (g_tq, g_tk, g_tv, g_iq, g_ik, g_iv))
        text_in = t_sum + project_back(g_tq, text_query) + project_back(g_tk, text_key) + project_back(g_tv, text_value)
        image_in = (
            i_sum + project_back(g_iq, image_query) + project_back(g_ik, image_key) + project_back(g_iv, image_value)
        )
        tl = (t_branch, text_kept[2], t_slow, text_rows)
        tr = (text_kept[4], t_zgrad, flat(text_context), g_tq, g_tk, g_tv)
        il = (i_branch, image_kept[2], i_slow, image_rows)
        ir = (image_kept[4], i_zgrad, flat(image_context), g_iq, g_ik, g_iv)
        wide = max(text_width, image_width)
        small = jnp.stack([jnp.pad(v, (0, wide - v.shape[0])) for v in t_small + i_small])
        me = lax.axis_index("batch") * mesh.shape["heads"] + core

        scatter = lambda v: lax.psum_scatter(v, ("batch", "heads"), scatter_dimension=0, tiled=True)
        text_grads = [scatter(outer_sum(tl[l], r)) for l, r in zip(LEFTS, tr)]
        image_grads = [scatter(outer_sum(il[l], r)) for l, r in zip(LEFTS, ir)]
        total = lax.psum(small, ("batch", "heads"))
        t_own, i_own = text_width // devices, image_width // devices
        t_norm = lax.dynamic_slice(total, (0, me * t_own), (4, t_own))
        i_norm = lax.dynamic_slice(total, (4, me * i_own), (4, i_own))
        return (
            text_result.reshape(text_states.shape),
            image_result.reshape(image_states.shape),
            text_in.astype(BF16).reshape(text_states.shape),
            image_in.astype(BF16).reshape(image_states.shape),
            *parts(text_grads), t_norm[:2], t_norm[2:],
            *parts(image_grads), i_norm[:2], i_norm[2:],
        )

    return local


def solution(mesh):
    rows = P(("batch", "heads"), None, None)
    first, second = P(("batch", "heads"), None), P(None, ("batch", "heads"))
    grads = (first, first, first, second, first, second, second, second)
    return jax.shard_map(
        make_local(mesh),
        mesh=mesh,
        in_specs=(rows, rows, P("batch"), P("batch"), *[P()] * 16, rows, rows),
        out_specs=(rows, rows, rows, rows, *grads, *grads),
        check_vma=False,
    )
```

```python
import functools
import math

import jax
import jax.numpy as jnp
from jax import lax
from jax.experimental import pallas as pl
from jax.experimental.pallas import tpu as pltpu
from jax.sharding import PartitionSpec as P

MESH_ID = pl.DeviceIdType.MESH
F32 = jnp.float32
BF16 = jnp.bfloat16
EPS = 1e-05
NEG = -1000000000.0
HEADS = 8
HEAD = 128
SCALE = 1.0 / math.sqrt(HEAD)
TILE = 256
CW = 256
LEFTS = (0, 1, 2, 3, 3, 3)
NT_DIMS = (((1,), (1,)), ((), ()))
TN_DIMS = (((0,), (0,)), ((), ()))
SLOTS = 6
UNROLL = 2
HEAD_GROUP = 2
G_RING, R_RING, Z_RING = 12, 12, 12
LATE = (1, 2, 5, 6, 8, 11, 13, 14, 16, 17, 19, 20, 23, 24, 25, 26, 28, 29)
PRODUCED = ((1, 0), (1, 1), (1, 2), (0, 0), (0, 1), (0, 2), (1, 3), (0, 4), (0, 5), (0, 3), (1, 4), (1, 5))
SEQUENCE = (
    "i_qkv", "i_attend", "i_out", "i_ffn", "i_norm", "A0", "i_slope", "i_branch", "i_context", "A1", "t_q", "t_kv",
    "t_attend", "T0", "A2", "t_out", "t_ffn0", "t_ffn1", "T1", "t_ffn2", "t_norm", "A3", "T2", "t_slope0", "A4", "T3",
    "A5", "t_slope1", "t_slope2", "T4", "A6", "t_branch", "T5", "A7", "T6", "A8", "i_back", "T7", "A9", "t_context",
    "T8", "A10", "t_back", "T9", "i_final", "A11", "t_final", "T10", "A12", "T11", "A13", "T12", "A14", "T13", "T14",
    "A15", "T15", "T16", "T17", "T18", "T19",
)


def dot(a, b):
    return jnp.dot(a, b, preferred_element_type=F32)


def dot_nt(a, b):
    return lax.dot_general(a, b, NT_DIMS, preferred_element_type=F32)


def dot_tn(a, b):
    return lax.dot_general(a, b, TN_DIMS, preferred_element_type=F32)


def loop(n, body, unroll=None):
    u = min(n, unroll or UNROLL)

    def step(i, carry):
        for k in range(u):
            body(i * u + k)
        return carry

    if n == u:
        step(0, 0)
    else:
        lax.fori_loop(0, n // u, step, 0)
        for k in range(n - n % u, n):
            body(k)


def at(i, size):
    return pl.ds(i * size if isinstance(i, int) else pl.multiple_of(i * size, size), size)


def layer_kernel(dims, *refs):
    nz, ny, nx = dims
    refs = list(refs)

    def take(n):
        got = refs[:n]
        del refs[:n]
        return got

    cap_ref, reg_ref, xt_in, xi_in, ut_in, ui_in = take(6)
    w_in = [take(6), take(6)]
    gain_ref, shift_ref = take(2), take(2)
    res_t, res_i, sg_t, sg_i = take(4)
    w_out = [take(6), take(6)]
    norm_out = take(4)
    wbuf, x_t, x_i = take(3)
    q_b, k_b, v_b = take(2), take(2), take(2)
    n1, inv, low, acc, dctx, sums = take(2), take(2), take(2), take(2), take(2), take(2)
    lt = take(2)
    r_own, r_far = [take(6), take(6)], [take(6), take(6)]
    g_b, r1_b, r2_b, ru_b, rd_b = take(5)
    f_b = take(2)
    small, sv, sr = take(3)
    in_sem, w_sem, ex_s, ex_r, st_s, st_r, sm_s, sm_r = take(8)
    assert not refs
    u_t, u_i = dctx[0].at[:, pl.ds(0, x_t.shape[1])], dctx[1]

    b, h = lax.axis_index("batch"), lax.axis_index("heads")
    x, y, z = lax.rem(b, nx), lax.rem(lax.div(b, nx), ny), lax.div(b, nx * ny)

    def dev(zz, yy, xx):
        return ((zz * ny + yy) * nx + xx, h)

    partner, nbr_x, nbr_y = (b, 1 - h), dev(z, y, 1 - x), dev(z, 1 - y, x)
    barrier = pltpu.get_barrier_semaphore()
    for who in (partner, nbr_x, nbr_y):
        pl.semaphore_signal(barrier, inc=1, device_id=who, device_id_type=MESH_ID)
    for off in range(1, nz):
        pl.semaphore_signal(barrier, inc=1, device_id=dev(lax.rem(z + off, nz), y, x), device_id_type=MESH_ID)

    def remote(src, dst, ssem, rsem, who):
        return pltpu.make_async_remote_copy(
            src_ref=src, dst_ref=dst, send_sem=ssem, recv_sem=rsem, device_id=who, device_id_type=MESH_ID
        )

    T, I = 0, 1
    pieces = []

    def piece(name, ref, rows, cols):
        pieces.append((name, ref, rows, cols))

    td, ti = x_t.shape[1], x_i.shape[1]
    inner = q_b[0].shape[1]
    parts = w_in[T][1].shape[1] // 1024
    whole = lambda s, w: w_in[s][w]
    tu = lambda j: w_in[T][1].at[:, pl.ds(j * 1024, 1024)]
    tw = lambda j: w_in[T][0].at[pl.ds(j * 1024, 1024), :]
    piece("tk", whole(T, 4), td, inner)
    piece("tv", whole(T, 5), td, inner)
    piece("iq", whole(I, 3), ti, inner)
    piece("io", whole(I, 2), inner, ti)
    piece("iu", whole(I, 1), ti, ti)
    piece("id", whole(I, 0), ti, ti)
    piece("tq", whole(T, 3), td, inner)
    piece("ik", whole(I, 4), ti, inner)
    piece("iv", whole(I, 5), ti, inner)
    piece("to", whole(T, 2), inner, td)
    for j in range(parts):
        piece("tu%d" % j, tu(j), td, 1024)
        piece("td%d" % j, tw(j), 1024, td)
    piece("to", whole(T, 2), inner, td)
    for name, s, w in (("iq", I, 3), ("tk", T, 4), ("tv", T, 5), ("tq", T, 3), ("ik", I, 4), ("iv", I, 5)):
        rows = td if s == T else ti
        piece(name, whole(s, w), rows, inner)
    issued = [0]
    held = {}

    def weight_copy(k, slot):
        name, ref, rows, cols = pieces[k]
        return pltpu.make_async_copy(ref, wbuf.at[slot, pl.ds(0, rows), pl.ds(0, cols)], w_sem.at[slot])

    def issue(slot):
        if issued[0] < len(pieces):
            k = issued[0]
            issued[0] += 1
            weight_copy(k, slot).start()
            assert pieces[k][0] not in held
            held[pieces[k][0]] = [k, slot, False]

    def weight(name):
        k, slot, ready = held[name]
        if not ready:
            weight_copy(k, slot).wait()
            held[name][2] = True
        _, _, rows, cols = pieces[k]
        return wbuf.at[slot, pl.ds(0, rows), pl.ds(0, cols)]

    def release(name):
        k, slot, ready = held.pop(name)
        issue(slot)

    pairs_n, regions = xi_in.shape[:2]
    pad = 112

    def image_rows(src, dst, k):
        return [
            pltpu.make_async_copy(src.at[p], dst.at[pl.ds(p * pad, regions), :], in_sem.at[k + p]) for p in range(pairs_n)
        ]

    def start(copies):
        for c in copies:
            c.start()

    def wait(copies):
        for c in copies:
            c.wait()

    in_copies = [
        [pltpu.make_async_copy(xt_in, x_t, in_sem.at[0])], image_rows(xi_in, x_i, 2),
        [pltpu.make_async_copy(ut_in, u_t, in_sem.at[1])], image_rows(ui_in, u_i, 2 + pairs_n),
    ]
    start(in_copies[0])
    issue(0)
    start(in_copies[1])
    issue(1)
    issue(2)
    start(in_copies[3])
    start(in_copies[2])
    for slot in range(3, SLOTS):
        issue(slot)

    cap = x_t.shape[0] // pairs_n
    m_i, m_t = pairs_n * pad, x_t.shape[0]
    m_of, d_of = (m_t, m_i), (td, ti)
    x_of = (x_t, x_i)

    tail = pl.ds(m_i, x_i.shape[0] - m_i)
    for ref in (x_i, low[I], *r_own[I]):
        ref[tail, :] = jnp.zeros((x_i.shape[0] - m_i, ref.shape[1]), BF16)
    for ref in (*sums,):
        ref[...] = jnp.zeros(ref.shape, F32)

    for ref in (x_i, u_i):
        for p in range(pairs_n):
            ref[pl.ds(p * pad + regions, pad - regions), :] = jnp.zeros((pad - regions, ref.shape[1]), BF16)

    lengths = {
        T: [reg_ref[h * pairs_n + p] for p in range(pairs_n)],
        I: [cap_ref[h * pairs_n + p] for p in range(pairs_n)],
    }

    ex_left, ex_right = {}, {}
    n_left = max(LEFTS) + 1
    for s in (T, I):
        for l in range(n_left):
            k = s * n_left + l
            ex_left[s, l] = remote(
                lt[s].at[l, :, pl.ds(0, 256)], lt[s].at[l, :, pl.ds(256, 256)], ex_s.at[k], ex_r.at[k], partner
            )
        for w in range(6):
            k = 2 * n_left + s * 6 + w
            half = r_far[s][w].shape[1]
            ex_right[s, w] = remote(
                r_own[s][w].at[:, pl.ds(pl.multiple_of((1 - h) * half, 128), half)], r_far[s][w],
                ex_s.at[k], ex_r.at[k], partner,
            )
    arrived = set()
    entered = []

    def enter():
        if not entered:
            entered.append(1)
            pl.semaphore_wait(barrier, 3 + nz - 1)

    def send_left(s, l, src):
        def body(j):
            lt[s][l, at(j, TILE), pl.ds(0, 256)] = src[:, at(j, TILE)].T

        loop(d_of[s] // TILE, body)
        enter()
        ex_left[s, l].start()

    def send_right(s, w):
        enter()
        ex_right[s, w].start()

    def project(src, rows, w, dst):
        def body(j):
            dst[pl.ds(0, rows), at(j, TILE)] = dot(src[pl.ds(0, rows), :], w[:, at(j, TILE)]).astype(BF16)

        loop(w.shape[1] // TILE, body)

    def softmaxes(parts_of):
        scores = [dot_nt(q, k) * SCALE for q, k, _ in parts_of]
        scores = [
            jnp.where(lax.broadcasted_iota(jnp.int32, v.shape, 1) < live, v, NEG)
            for v, (_, _, live) in zip(scores, parts_of)
        ]
        tops = [jnp.max(v, axis=-1, keepdims=True) for v in scores]
        exps = [jnp.exp(v - t) for v, t in zip(scores, tops)]
        totals = [jnp.sum(e, axis=-1, keepdims=True) for e in exps]
        return [e / t for e, t in zip(exps, totals)]

    span = (cap, pad)

    def rows_of(s, p):
        return pl.ds(p * span[s], span[s])

    def units(i):
        return [(at(i * HEAD_GROUP + k, HEAD), p) for k in range(HEAD_GROUP) for p in range(pairs_n)]

    def attend(s):
        o = 1 - s

        def body(i):
            group = units(i)
            probs = softmaxes(
                [(q_b[s][rows_of(s, p), c], k_b[o][rows_of(o, p), c], lengths[s][p]) for c, p in group]
            )
            got = [dot(prob.astype(BF16), v_b[o][rows_of(o, p), c]) for prob, (c, p) in zip(probs, group)]
            for g, (c, p) in zip(got, group):
                r_own[s][2][rows_of(s, p), c] = g.astype(BF16)

        loop(HEADS // HEAD_GROUP, body, 1)
        send_right(s, 2)

    def attend_back(s):
        o = 1 - s

        def body(i):
            group = units(i)
            qs = [q_b[s][rows_of(s, p), c] for c, p in group]
            ks = [k_b[o][rows_of(o, p), c] for c, p in group]
            dcs = [dctx[s][rows_of(s, p), c] for c, p in group]
            dps = [dot_nt(dc, v_b[o][rows_of(o, p), c]) for dc, (c, p) in zip(dcs, group)]
            probs = softmaxes([(q, k, lengths[s][p]) for q, k, (_, p) in zip(qs, ks, group)])
            dvs = [dot_tn(prob.astype(BF16), dc) for prob, dc in zip(probs, dcs)]
            inner_sums = [jnp.sum(prob * dp, axis=-1, keepdims=True) for prob, dp in zip(probs, dps)]
            dss = [(prob * (dp - t)).astype(BF16) for prob, dp, t in zip(probs, dps, inner_sums)]
            dqs = [dot(ds, k) * SCALE for ds, k in zip(dss, ks)]
            dks = [dot_tn(ds, q) * SCALE for ds, q in zip(dss, qs)]
            for (c, p), dq, dk, dv in zip(group, dqs, dks, dvs):
                rq, rk = rows_of(s, p), rows_of(o, p)
                r_own[s][3][rq, c] = dq.astype(BF16)
                r_own[o][4][rk, c] = dk.astype(BF16)
                r_own[o][5][rk, c] = dv.astype(BF16)

        loop(HEADS // HEAD_GROUP, body, 1)
        send_right(s, 3)
        send_right(o, 4)
        send_right(o, 5)

    RB = 32

    def mean(v):
        return jnp.mean(v, axis=-1, keepdims=True)

    def sum8(v):
        return jnp.sum(v.reshape(v.shape[0] // 8, 8, v.shape[1]), axis=0)

    def norm_one(s):
        gain, shift = gain_ref[s][0:1, :], shift_ref[s][0:1, :]

        def body(i):
            r = at(i, RB)
            v = x_of[s][r, :].astype(F32) + acc[s][r, :]
            c = v - mean(v)
            iv = lax.rsqrt(mean(c * c) + EPS)
            n = c * iv
            n1[s][r, :] = n
            inv[s][r, :] = jnp.broadcast_to(iv, (RB, 128))
            low[s][r, :] = (n * gain + shift).astype(BF16)

        loop(m_of[s] // RB, body)
        send_left(s, 1, low[s])

    def norm_two(s, up_ref, res_ref):
        gain0, shift0 = gain_ref[s][0:1, :], shift_ref[s][0:1, :]
        gain, shift = gain_ref[s][1:2, :], shift_ref[s][1:2, :]

        def body(i):
            r = at(i, RB)
            v = n1[s][r, :] * gain0 + shift0 + acc[s][r, :]
            c = v - mean(v)
            iv = lax.rsqrt(mean(c * c) + EPS)
            n = c * iv
            up = up_ref[r, :].astype(F32)
            res_ref[r, :] = (n * gain + shift).astype(BF16)
            un = up * n
            sums[s][1] = sums[s][1] + sum8(un)
            sums[s][3] = sums[s][3] + sum8(up)
            u = up * gain
            d = iv * (u - mean(u) - n * mean(un * gain))
            acc[s][r, :] = d
            low[s][r, :] = d.astype(BF16)

        loop(m_of[s] // RB, body)
        send_left(s, 0, low[s])

    def norm_one_back(s):
        gain = gain_ref[s][0:1, :]

        def body(i):
            r = at(i, RB)
            g, n = acc[s][r, :], n1[s][r, :]
            gn = g * n
            sums[s][0] = sums[s][0] + sum8(gn)
            sums[s][2] = sums[s][2] + sum8(g)
            u = g * gain
            d = inv[s][r, 0:1] * (u - mean(u) - n * mean(gn * gain))
            acc[s][r, :] = d
            low[s][r, :] = d.astype(BF16)

        loop(m_of[s] // RB, body)
        send_left(s, 2, low[s])

    def out_project(s, w):
        m = m_of[s]

        def body(j):
            acc[s][pl.ds(0, m), at(j, TILE)] = dot(r_own[s][2][pl.ds(0, m), :], w[:, at(j, TILE)])

        loop(d_of[s] // TILE, body)

    def ffn(s, j, up_w, down_w):
        m, base = m_of[s], j * 1024

        def hidden(i):
            c = pl.ds(pl.multiple_of(base + i * TILE, TILE), TILE)
            v = dot(low[s][pl.ds(0, m), :], up_w[:, at(i, TILE)])
            half = 0.5 * (1.0 + lax.erf(v * (1.0 / math.sqrt(2.0))))
            r_own[s][0][pl.ds(0, m), c] = (v * half).astype(BF16)
            r_own[s][1][pl.ds(0, m), c] = (half + v * jnp.exp(-0.5 * v * v) * (1.0 / math.sqrt(2.0 * math.pi))).astype(BF16)

        loop(1024 // TILE, hidden)

        def second(i):
            part = dot(r_own[s][0][pl.ds(0, m), pl.ds(base, 1024)], down_w[:, at(i, TILE)])
            if j == 0:
                acc[s][pl.ds(0, m), at(i, TILE)] = part
            else:
                acc[s][pl.ds(0, m), at(i, TILE)] += part

        loop(d_of[s] // TILE, second)

    def slope_back(s, j, down_w):
        m, base = m_of[s], j * 1024

        def body(i):
            c = pl.ds(pl.multiple_of(base + i * TILE, TILE), TILE)
            g = dot_nt(low[s][pl.ds(0, m), :], down_w[at(i, TILE), :])
            r_own[s][1][pl.ds(0, m), c] = (g * r_own[s][1][pl.ds(0, m), c].astype(F32)).astype(BF16)

        loop(1024 // TILE, body)

    def back_add(s, src, cols, w):
        m = m_of[s]

        def body(i):
            acc[s][pl.ds(0, m), at(i, TILE)] += dot_nt(src[pl.ds(0, m), cols], w[at(i, TILE), :])

        loop(d_of[s] // TILE, body)

    def context_back(s, w):
        m = m_of[s]

        def body(i):
            dctx[s][pl.ds(0, m), at(i, TILE)] = dot_nt(low[s][pl.ds(0, m), :], w[at(i, TILE), :]).astype(BF16)

        loop(inner // TILE, body)

    def final(s, dst):
        def body(i):
            dst[at(i, RB), :] = acc[s][at(i, RB), :].astype(BF16)

        loop(m_of[s] // RB, body)

    def gather_rows(src, dst):
        for p in range(pairs_n):
            dst[p] = src[pl.ds(p * pad, regions), :]

    all_cols = pl.ds(0, 1024)

    def step(name):
        if name == "i_qkv":
            wait(in_copies[0])
            project(x_t, m_t, weight("tk"), k_b[T])
            release("tk")
            project(x_t, m_t, weight("tv"), v_b[T])
            release("tv")
            wait(in_copies[1])
            project(x_i, m_i, weight("iq"), q_b[I])
            release("iq")
        elif name == "i_attend":
            attend(I)
        elif name == "i_out":
            out_project(I, weight("io"))
            norm_one(I)
        elif name == "i_ffn":
            ffn(I, 0, weight("iu"), weight("id"))
            send_right(I, 0)
        elif name == "i_norm":
            wait(in_copies[3])
            norm_two(I, u_i, u_i)
            gather_rows(u_i, res_i)
        elif name == "i_slope":
            slope_back(I, 0, weight("id"))
            send_right(I, 1)
            release("id")
        elif name == "i_branch":
            back_add(I, r_own[I][1], all_cols, weight("iu"))
            release("iu")
            norm_one_back(I)
        elif name == "i_context":
            context_back(I, weight("io"))
            release("io")
            send_left(I, 3, x_i)
        elif name == "t_q":
            project(x_t, m_t, weight("tq"), q_b[T])
            release("tq")
            send_left(T, 3, x_t)
        elif name == "t_kv":
            project(x_i, m_i, weight("ik"), k_b[I])
            release("ik")
            project(x_i, m_i, weight("iv"), v_b[I])
            release("iv")
        elif name == "t_attend":
            attend(T)
        elif name == "t_out":
            out_project(T, weight("to"))
            release("to")
            norm_one(T)
        elif name.startswith("t_ffn"):
            j = int(name[-1])
            ffn(T, j, weight("tu%d" % j), weight("td%d" % j))
            if j == parts - 1:
                send_right(T, 0)
        elif name == "t_norm":
            wait(in_copies[2])
            norm_two(T, u_t, res_t)
        elif name.startswith("t_slope"):
            j = int(name[-1])
            slope_back(T, j, weight("td%d" % j))
            release("td%d" % j)
            if j == parts - 1:
                send_right(T, 1)
        elif name == "t_branch":
            for j in range(parts):
                back_add(T, r_own[T][1], pl.ds(j * 1024, 1024), weight("tu%d" % j))
                release("tu%d" % j)
            norm_one_back(T)
            small_fill()
        elif name == "t_context":
            context_back(T, weight("to"))
            release("to")
        elif name == "i_back":
            attend_back(I)
            back_add(I, r_own[I][3], all_cols, weight("iq"))
            release("iq")
            back_add(T, r_own[T][4], all_cols, weight("tk"))
            release("tk")
            back_add(T, r_own[T][5], all_cols, weight("tv"))
            release("tv")
        elif name == "t_back":
            attend_back(T)
        elif name == "i_final":
            back_add(I, r_own[I][4], all_cols, weight("ik"))
            release("ik")
            back_add(I, r_own[I][5], all_cols, weight("iv"))
            release("iv")
            final(I, u_i)
            gather_rows(u_i, sg_i)
        elif name == "t_final":
            back_add(T, r_own[T][3], all_cols, weight("tq"))
            release("tq")
            final(T, sg_t)
        elif name[0] == "A":
            for c in (2 * int(name[1:]), 2 * int(name[1:]) + 1):
                compute(c)
                s1(c).start()
        else:
            tick(int(name[1:]))

    small_copies = []

    def small_start(src, dst, i, who):
        c = remote(src, dst, sm_s.at[i], sm_r.at[i], who)
        c.start()
        small_copies.append(c)

    def small_fill():
        small[...] = jnp.zeros(small.shape, F32)
        for s in (T, I):
            for k in range(4):
                small[pl.ds(4 * s + k, 1), pl.ds(0, d_of[s])] = jnp.sum(sums[s][k], axis=0, keepdims=True)

    def small_step(i):
        if i == 0:
            small_start(small, sr.at[0], 0, partner)
        elif i == 1:
            small_copies[0].wait_recv()
            sv[0] = small[...] + sr[0]
            small_start(sv.at[0], sr.at[1], 1, nbr_x)
        elif i == 2:
            small_copies[1].wait_recv()
            sv[1] = sv[0] + sr[1]
            small_start(sv.at[1], sr.at[2], 2, nbr_y)
        elif i == 3:
            small_copies[2].wait_recv()
            sv[2] = sv[1] + sr[2]
            for off in range(1, nz):
                small_start(sv.at[2], sr.at[2 + off], 2 + off, dev(lax.rem(z + off, nz), y, x))
        elif i == 4:
            total = sv[2]
            for off in range(1, nz):
                small_copies[2 + off].wait_recv()
                total = total + sr[2 + off]
            wide = total.shape[1]
            me = b * 2 + h
            for s in (T, I):
                own = norm_out[2 * s].shape[1]
                mine = pltpu.roll(total, lax.rem(wide - me * own, wide), 1)
                norm_out[2 * s][...] = mine[4 * s : 4 * s + 2, :own]
                norm_out[2 * s + 1][...] = mine[4 * s + 2 : 4 * s + 4, :own]

    chunks = []
    for s, w in PRODUCED:
        for o in range(0, r_far[s][w].shape[1], CW):
            late = len(chunks) in LATE
            chunks.append((s, w, o, "xy"[len(chunks) % 2], len([1 for c in chunks if c[0] == s]), late))
    n = len(chunks)

    def bufs(c):
        rows = pl.ds(0, d_of[chunks[c][0]] // (nz * ny * nx))
        return (
            g_b.at[c % G_RING, :, :, :, rows], r1_b.at[c % R_RING, :, :, rows], r2_b.at[c % R_RING, :, rows],
            ru_b.at[c % Z_RING, :, :, rows], rd_b.at[c % Z_RING, :, :, rows],
        )

    def compute(c):
        s, w, o, way, _, _ = chunks[c]
        for copy, key in ((ex_left[s, LEFTS[w]], (0, s, LEFTS[w])), (ex_right[s, w], (1, s, w))):
            if key not in arrived:
                arrived.add(key)
                copy.wait_recv()
        blk = d_of[s] // (nz * ny * nx)
        size = ny * nx * blk
        half = r_far[s][w].shape[1]
        mine = pl.ds(pl.multiple_of(h * half + o, 128), CW)
        g = g_b.at[c % G_RING]

        def body(i):
            r = pl.ds(pl.multiple_of(i * size, 64), size)
            l = LEFTS[w]
            res = dot(lt[s][l, r, pl.ds(0, 256)], r_own[s][w][:, mine]) + dot(
                lt[s][l, r, pl.ds(256, 256)], r_far[s][w][:, pl.ds(o, CW)]
            )
            g[i, :, :, pl.ds(0, blk)] = res.astype(BF16).reshape(ny, nx, blk, CW)

        loop(nz, body)

    def add(dst, src):
        dst[...] = (dst[...].astype(F32) + src[...].astype(F32)).astype(BF16)

    def s1(c):
        g, r1 = bufs(c)[:2]
        if chunks[c][3] == "x":
            return remote(g.at[:, :, 1 - x], r1, st_s.at[0, c], st_r.at[0, c], nbr_x)
        return remote(g.at[:, 1 - y], r1, st_s.at[0, c], st_r.at[0, c], nbr_y)

    def s2(c):
        g, _, r2 = bufs(c)[:3]
        first, late = chunks[c][3] == "x", chunks[c][5]
        far = (1 - y, x) if first else (y, 1 - x)
        src, dst = (g.at[z, far[0], far[1]], r2.at[0]) if late else (g.at[:, far[0], far[1]], r2)
        return remote(src, dst, st_s.at[1, c], st_r.at[1, c], nbr_y if first else nbr_x)

    def blocks(c, t):
        g, _, _, ru, rd = bufs(c)
        if not chunks[c][5]:
            return [(g.at[t, y, x], ru.at[t, 0], rd.at[t, 0])]
        here = (lambda j: g.at[t, j, x]) if chunks[c][3] == "x" else (lambda j: g.at[t, y, j])
        return [(here(j), ru.at[t, j], rd.at[t, j]) for j in range(2)]

    def along(c, rest, buf):
        g = bufs(c)[0]
        if not chunks[c][5]:
            return g.at[rest, y, x], buf.at[rest, 0]
        return (g.at[rest, :, x] if chunks[c][3] == "x" else g.at[rest, y]), buf.at[rest]

    def up(c, k):
        src, dst = along(c, pl.ds(k + 1, nz - 1 - k), bufs(c)[3])
        return remote(src, dst, st_s.at[2, c], st_r.at[2, c], dev(k + 1, y, x))

    def down(c, k):
        src, dst = along(c, pl.ds(0, k), bufs(c)[4])
        return remote(src, dst, st_s.at[3, c], st_r.at[3, c], dev(k - 1, y, x))

    def swap(c):
        s, w, o, _, k, _ = chunks[c]
        out = w_out[s][w]
        half = out.shape[1] // 2
        return remote(
            f_b[s].at[k], out.at[:, pl.ds(pl.multiple_of(h * half + o, 128), CW)],
            st_s.at[4, c], st_r.at[4, c], partner,
        )

    def ends(c):
        @pl.when(z == 0)
        def _():
            up(c, 0).start()

        @pl.when(z == nz - 1)
        def _():
            down(c, nz - 1).start()

    def stage2(pair):
        for c in pair:
            s1(c).wait_recv()
        for c in pair:
            g, r1 = bufs(c)[:2]

            def body(i):
                for j in range(2):
                    add(g.at[i, j, x] if chunks[c][3] == "x" else g.at[i, y, j], r1.at[i, j])

            loop(nz, body)
            if chunks[c][5]:
                ends(c)
            else:
                s2(c).start()

    def stage3(pair):
        for c in pair:
            s2(c).wait_recv()
        for c in pair:
            g, _, r2 = bufs(c)[:3]
            loop(nz, lambda i: add(g.at[i, y, x], r2.at[i]))
            ends(c)

    def hop(pair, d):
        for c in pair:

            @pl.when(z == d)
            def _(c=c):
                up(c, d - 1).wait_recv()
                for t in range(d + 1, nz):
                    for here, below, _ in blocks(c, t):
                        add(here, below)
                up(c, d).start()

            @pl.when(z == nz - 1 - d)
            def _(c=c):
                down(c, nz - d).wait_recv()
                for t in range(0, nz - 1 - d):
                    for here, _, above in blocks(c, t):
                        add(here, above)
                down(c, nz - 1 - d).start()

    def last_hops(c, k):
        if k == nz - 1:
            up(c, k - 1).wait_recv()
        if k == 0:
            down(c, 1).wait_recv()

    def z_total(c, k, j):
        g, _, _, ru, rd = bufs(c)
        late, first = chunks[c][5], chunks[c][3] == "x"
        lane = j if late else 0
        row, col = (j, x) if late and first else (y, j) if late else (y, x)
        total = g[k, row, col].astype(F32)
        if k > 0:
            total = total + ru[k, lane].astype(F32)
        if k < nz - 1:
            total = total + rd[k, lane].astype(F32)
        return total

    def fold(pair):
        for c in pair:
            far = 1 - y if chunks[c][3] == "x" else 1 - x
            for k in range(nz):

                @pl.when(z == k)
                def _(c=c, k=k, far=far):
                    last_hops(c, k)
                    got = z_total(c, k, far).astype(BF16)
                    g = bufs(c)[0]
                    if chunks[c][3] == "x":
                        g[k, far, x] = got
                    else:
                        g[k, y, far] = got

            s2(c).start()

    def finish(pair):
        for c in pair:
            s, w, o, way, idx, late = chunks[c]
            out = w_out[s][w]
            r, half = out.shape[0], out.shape[1] // 2
            cols = pl.ds(pl.multiple_of(h * half + o, 128), CW)
            if late:
                s2(c).wait_recv()
            for k in range(nz):

                @pl.when(z == k)
                def _(k=k):
                    if not late:
                        last_hops(c, k)
                    total = z_total(c, k, y if way == "x" else x)
                    if late:
                        total = total + bufs(c)[2][0].astype(F32)
                    first, second = total[:r], total[r:]
                    out[:, cols] = jnp.where(h == 0, first, second)
                    f_b[s][idx] = jnp.where(h == 0, second, first)

            swap(c).start()
            s1(c).wait_send()
            s2(c).wait_send()
            for k in range(nz):

                @pl.when(z == k)
                def _(k=k):
                    if k < nz - 1:
                        up(c, k).wait_send()
                    if k > 0:
                        down(c, k).wait_send()

    pairs = n // 2
    small_from = 9

    def stage(p, lag):
        pair = (2 * p, 2 * p + 1)
        if lag == 0:
            return stage2(pair)
        if lag == nz:
            return finish(pair)
        for late in (True, False):
            part = [c for c in pair if chunks[c][5] == late]
            if late and lag == nz - 1:
                fold(part)
            elif not late and lag == 1:
                stage3(part)
            else:
                hop(part, lag if late else lag - 1)

    def tick(t):
        for lag in range(nz, -1, -1):
            if 0 <= t - lag < pairs:
                stage(t - lag, lag)
        if small_from <= t < small_from + 5:
            small_step(t - small_from)

    for name in SEQUENCE:
        step(name)

    for c in range(n):
        swap(c).wait_recv()
        swap(c).wait_send()
    for copy in (*ex_left.values(), *ex_right.values()):
        copy.wait_send()
    for copy in small_copies:
        copy.wait_send()


def hand_over(*refs):
    n = len(refs) // 2
    copies = [pltpu.make_async_copy(refs[i], refs[n + i], refs[-1].at[i]) for i in range(n)]
    for c in copies:
        c.start()
    for c in copies:
        c.wait()


def layer(dims, lengths, states, upstream, weights, gains, shifts):
    nz, ny, nx = dims
    chips = nz * ny * nx
    xt, xi = states
    pairs, cap, td = xt.shape
    regions, ti = xi.shape[1:]
    xt, ut = xt.reshape(pairs * cap, td), upstream[0].reshape(pairs * cap, td)
    mt = pairs * cap
    fixed = 256
    inner = weights[0][3].shape[1]
    d_of = (td, ti)
    cols = [[w.shape[0], weights[s][1].shape[1], inner, inner, inner, inner] for s, w in ((0, weights[0][0]), (1, weights[1][0]))]
    V, DMA = pltpu.VMEM, pltpu.SemaphoreType.DMA
    rows_of = (mt, fixed)
    ti_blk = ti // chips
    counts = [sum(c // 2 // CW for c in cols[s]) for s in range(2)]
    n = sum(counts)
    act = lambda dt, width: [V((rows_of[s], width[s]), dt) for s in range(2)]
    scratch = [
        V((SLOTS, 1024, 1024), BF16),
        V((mt, td), BF16), V((fixed, ti), BF16),
        *act(BF16, (inner, inner)), *act(BF16, (inner, inner)), *act(BF16, (inner, inner)),
        *act(F32, d_of), *act(F32, (128, 128)), *act(BF16, d_of),
        *act(F32, d_of), *act(BF16, (inner, inner)),
        *[V((4, 8, d), F32) for d in d_of],
        *[V((4, d, 512), BF16) for d in d_of],
        *[V((rows_of[s], c), BF16) for s in range(2) for c in cols[s]],
        *[V((rows_of[s], c // 2), BF16) for s in range(2) for c in cols[s]],
        V((G_RING, nz, ny, nx, ti_blk, CW), BF16),
        V((R_RING, nz, 2, ti_blk, CW), BF16),
        V((R_RING, nz, ti_blk, CW), BF16),
        V((Z_RING, nz, 2, ti_blk, CW), BF16),
        V((Z_RING, nz, 2, ti_blk, CW), BF16),
        *[V((counts[s], d_of[s] // chips // 2, CW), F32) for s in range(2)],
        V((8, max(d_of)), F32), V((3, 8, max(d_of)), F32), V((2 + nz, 8, max(d_of)), F32),
        DMA((2 + 2 * pairs,)), DMA((SLOTS,)), DMA((20,)), DMA((20,)), DMA((5, n)), DMA((5, n)), DMA((2 + nz,)), DMA((2 + nz,)),
    ]
    hbm = pl.BlockSpec(memory_space=pl.ANY)
    vm = pl.BlockSpec(memory_space=pltpu.VMEM)
    smem = pl.BlockSpec(memory_space=pltpu.SMEM)
    sds = jax.ShapeDtypeStruct
    outs = [
        sds((mt, td), BF16), sds((pairs, regions, ti), BF16), sds((mt, td), BF16), sds((pairs, regions, ti), BF16),
        *[sds((d_of[s] // chips // 2, c), F32) for s in range(2) for c in cols[s]],
        *[sds((2, d_of[s] // chips // 2), F32) for s in range(2) for _ in range(2)],
    ]
    got = pl.pallas_call(
        functools.partial(layer_kernel, dims),
        out_shape=outs,
        in_specs=[smem, smem, *[hbm] * 4, *[hbm] * 12, *[vm] * 4],
        out_specs=[vm] * len(outs),
        scratch_shapes=scratch,
        compiler_params=pltpu.CompilerParams(
            collective_id=0, has_side_effects=True, vmem_limit_bytes=67043328
        ),
        name="co_layer",
    )(*lengths, xt, xi, ut, upstream[1], *weights[0], *weights[1], *gains, *shifts)
    n = len(got)
    return pl.pallas_call(
        hand_over,
        out_shape=outs,
        in_specs=[vm] * n,
        out_specs=[hbm] * n,
        scratch_shapes=[DMA((n,))],
        name="hand_over",
    )(*got)


def matmul(row_values, weight):
    return jnp.dot(row_values, weight, preferred_element_type=F32)


def project_back(gradient, weight):
    return lax.dot_general(gradient, weight, (((1,), (1,)), ((), ())), preferred_element_type=F32)


def outer_sum(row_values, gradient):
    return lax.dot_general(row_values, gradient, (((0,), (0,)), ((), ())), preferred_element_type=F32)


def layer_norm(values, gain, shift):
    row_mean = jnp.mean(values, axis=-1, keepdims=True)
    centred = values - row_mean
    spread = jnp.mean(centred * centred, axis=-1, keepdims=True)
    inverse = lax.rsqrt(spread + EPS)
    normed = centred * inverse
    return (normed * gain + shift, normed, inverse)


def norm_back(gradient, normed, inverse, gain):
    scaled = gradient * gain
    first_mean = jnp.mean(scaled, axis=-1, keepdims=True)
    second_mean = jnp.mean(scaled * normed, axis=-1, keepdims=True)
    into = inverse * (scaled - first_mean - normed * second_mean)
    return (into, jnp.sum(gradient * normed, axis=0), jnp.sum(gradient, axis=0))


def gelu_value(values):
    return 0.5 * values * (1.0 + jax.scipy.special.erf(values / math.sqrt(2.0)))


def gelu_slope(values):
    return 0.5 * (1.0 + jax.scipy.special.erf(values / math.sqrt(2.0))) + values * jnp.exp(
        -0.5 * values * values
    ) / math.sqrt(2.0 * math.pi)


def attend(queries, key_rows, value_rows, lengths):
    score_scale = 1.0 / math.sqrt(queries.shape[-1])
    scores = jnp.einsum("bqhd,bkhd->bhqk", queries, key_rows, preferred_element_type=F32) * score_scale
    live_mask = lax.broadcasted_iota(jnp.int32, scores.shape, 3) < lengths[:, None, None, None]
    scores = jnp.where(live_mask, scores, NEG)
    weights = jnp.exp(scores - jnp.max(scores, axis=-1, keepdims=True))
    probability = weights / jnp.sum(weights, axis=-1, keepdims=True)
    context = jnp.einsum("bhqk,bkhd->bqhd", probability.astype(BF16), value_rows, preferred_element_type=F32)
    return context.astype(BF16), probability


def attend_back(queries, key_rows, value_rows, probability, context_grad):
    score_scale = 1.0 / math.sqrt(queries.shape[-1])
    value_grad = jnp.einsum(
        "bhqk,bqhd->bkhd", probability.astype(BF16), context_grad, preferred_element_type=F32
    )
    prob_grad = jnp.einsum("bqhd,bkhd->bhqk", context_grad, value_rows, preferred_element_type=F32)
    row_inner = jnp.sum(probability * prob_grad, axis=-1, keepdims=True)
    score_grad = (probability * (prob_grad - row_inner)).astype(BF16)
    query_grad = jnp.einsum("bhqk,bkhd->bqhd", score_grad, key_rows, preferred_element_type=F32) * score_scale
    key_grad = jnp.einsum("bhqk,bqhd->bkhd", score_grad, queries, preferred_element_type=F32) * score_scale
    return (query_grad.astype(BF16), key_grad.astype(BF16), value_grad.astype(BF16))


def stream_forward(row_values, context, out_weight, up_weight, down_weight, gains, shifts):
    attended = matmul(context, out_weight)
    first_out, normed_one, inverse_one = layer_norm(row_values.astype(F32) + attended, gains[0], shifts[0])
    first_low = first_out.astype(BF16)
    before = matmul(first_low, up_weight)
    active = gelu_value(before).astype(BF16)
    second_out, normed_two, inverse_two = layer_norm(
        first_out + matmul(active, down_weight), gains[1], shifts[1]
    )
    kept_state = (normed_one, inverse_one, first_low, before, active, normed_two, inverse_two)
    return (second_out.astype(BF16), kept_state)


def stream_back(upstream, kept_state, out_weight, up_weight, down_weight, gains):
    normed_one, inverse_one, first_low, before, active, normed_two, inverse_two = kept_state
    branch_grad, gain_two, shift_two = norm_back(upstream.astype(F32), normed_two, inverse_two, gains[1])
    branch_low = branch_grad.astype(BF16)
    active_grad = project_back(branch_low, down_weight)
    before_grad = (active_grad * gelu_slope(before)).astype(BF16)
    first_grad = project_back(before_grad, up_weight) + branch_grad
    sum_grad, gain_one, shift_one = norm_back(first_grad, normed_one, inverse_one, gains[0])
    sum_low = sum_grad.astype(BF16)
    context_grad = project_back(sum_low, out_weight).astype(BF16)
    return sum_grad, context_grad, branch_low, before_grad, sum_low, (gain_one, gain_two, shift_one, shift_two)


def make_local(mesh):
    devices = mesh.shape["batch"] * mesh.shape["heads"]

    def local(
        text_states, image_states, caption_lengths, region_counts,
        text_query, text_key, text_value, text_output, text_up, text_down, text_gains, text_shifts,
        image_query, image_key, image_value, image_output, image_up, image_down, image_gains, image_shifts,
        text_upstream, image_upstream,
    ):
        def parts(grads):
            down, up, out, query, key, value = grads
            return query, key, value, out.T, up, down.T

        if mesh.shape["batch"] == 16 and mesh.shape["heads"] == 2:
            text_weights = (text_down, text_up, text_output, text_query, text_key, text_value)
            image_weights = (image_down, image_up, image_output, image_query, image_key, image_value)
            got = layer(
                (4, 2, 2), (caption_lengths, region_counts), (text_states, image_states), (text_upstream, image_upstream),
                (text_weights, image_weights), (text_gains, image_gains), (text_shifts, image_shifts),
            )
            return (
                got[0].reshape(text_states.shape), got[1], got[2].reshape(text_states.shape), got[3],
                *parts(got[4:10]), got[16], got[17], *parts(got[10:16]), got[18], got[19],
            )
        pair_count, cap_len, text_width = text_states.shape
        region_len, image_width = image_states.shape[1:]
        text_rows = text_states.reshape(pair_count * cap_len, text_width)
        image_rows = image_states.reshape(pair_count * region_len, image_width)
        core = lax.axis_index("heads")
        captions = lax.dynamic_slice(caption_lengths, (core * pair_count,), (pair_count,))
        regions = lax.dynamic_slice(region_counts, (core * pair_count,), (pair_count,))

        def heads_of(row_values, weight, length):
            return matmul(row_values, weight).astype(BF16).reshape(pair_count, length, HEADS, HEAD)

        tq, tk, tv = (heads_of(text_rows, w, cap_len) for w in (text_query, text_key, text_value))
        iq, ik, iv = (heads_of(image_rows, w, region_len) for w in (image_query, image_key, image_value))
        text_context, text_prob = attend(tq, ik, iv, regions)
        image_context, image_prob = attend(iq, tk, tv, captions)
        flat = lambda v: v.reshape(v.shape[0] * v.shape[1], -1)
        text_result, text_kept = stream_forward(
            text_rows, flat(text_context), text_output, text_up, text_down, text_gains, text_shifts
        )
        image_result, image_kept = stream_forward(
            image_rows, flat(image_context), image_output, image_up, image_down, image_gains, image_shifts
        )
        t_sum, t_cgrad, t_branch, t_zgrad, t_slow, t_small = stream_back(
            text_upstream.reshape(text_rows.shape), text_kept, text_output, text_up, text_down, text_gains
        )
        i_sum, i_cgrad, i_branch, i_zgrad, i_slow, i_small = stream_back(
            image_upstream.reshape(image_rows.shape), image_kept, image_output, image_up, image_down, image_gains
        )
        g_tq, g_ik, g_iv = attend_back(tq, ik, iv, text_prob, t_cgrad.reshape(tq.shape))
        g_iq, g_tk, g_tv = attend_back(iq, tk, tv, image_prob, i_cgrad.reshape(iq.shape))
        g_tq, g_tk, g_tv, g_iq, g_ik, g_iv = (flat(v) for v in (g_tq, g_tk, g_tv, g_iq, g_ik, g_iv))
        text_in = t_sum + project_back(g_tq, text_query) + project_back(g_tk, text_key) + project_back(g_tv, text_value)
        image_in = (
            i_sum + project_back(g_iq, image_query) + project_back(g_ik, image_key) + project_back(g_iv, image_value)
        )
        tl = (t_branch, text_kept[2], t_slow, text_rows)
        tr = (text_kept[4], t_zgrad, flat(text_context), g_tq, g_tk, g_tv)
        il = (i_branch, image_kept[2], i_slow, image_rows)
        ir = (image_kept[4], i_zgrad, flat(image_context), g_iq, g_ik, g_iv)
        wide = max(text_width, image_width)
        small = jnp.stack([jnp.pad(v, (0, wide - v.shape[0])) for v in t_small + i_small])
        me = lax.axis_index("batch") * mesh.shape["heads"] + core

        scatter = lambda v: lax.psum_scatter(v, ("batch", "heads"), scatter_dimension=0, tiled=True)
        text_grads = [scatter(outer_sum(tl[l], r)) for l, r in zip(LEFTS, tr)]
        image_grads = [scatter(outer_sum(il[l], r)) for l, r in zip(LEFTS, ir)]
        total = lax.psum(small, ("batch", "heads"))
        t_own, i_own = text_width // devices, image_width // devices
        t_norm = lax.dynamic_slice(total, (0, me * t_own), (4, t_own))
        i_norm = lax.dynamic_slice(total, (4, me * i_own), (4, i_own))
        return (
            text_result.reshape(text_states.shape),
            image_result.reshape(image_states.shape),
            text_in.astype(BF16).reshape(text_states.shape),
            image_in.astype(BF16).reshape(image_states.shape),
            *parts(text_grads), t_norm[:2], t_norm[2:],
            *parts(image_grads), i_norm[:2], i_norm[2:],
        )

    return local


def solution(mesh):
    rows = P(("batch", "heads"), None, None)
    first, second = P(("batch", "heads"), None), P(None, ("batch", "heads"))
    grads = (first, first, first, second, first, second, second, second)
    return jax.shard_map(
        make_local(mesh),
        mesh=mesh,
        in_specs=(rows, rows, P("batch"), P("batch"), *[P()] * 16, rows, rows),
        out_specs=(rows, rows, rows, rows, *grads, *grads),
        check_vma=False,
    )
```

```python
import functools
import math

import jax
import jax.numpy as jnp
from jax import lax
from jax.experimental import pallas as pl
from jax.experimental.pallas import tpu as pltpu
from jax.sharding import PartitionSpec as P

MESH_ID = pl.DeviceIdType.MESH
F32 = jnp.float32
BF16 = jnp.bfloat16
EPS = 1e-05
NEG = -1000000000.0
HEADS = 8
HEAD = 128
SCALE = 1.0 / math.sqrt(HEAD)
TILE = 256
CW = 256
LEFTS = (0, 1, 2, 3, 3, 3)
NT_DIMS = (((1,), (1,)), ((), ()))
TN_DIMS = (((0,), (0,)), ((), ()))
SLOTS = 6
UNROLL = 2
HEAD_GROUP = 2
G_RING, R_RING, Z_RING = 12, 12, 12
LATE = (0, 3, 6, 9, 10, 13, 15, 16, 19, 20, 23, 24, 25, 26, 29)
PRODUCED = ((1, 0), (1, 1), (1, 2), (0, 0), (0, 1), (0, 2), (1, 3), (0, 4), (0, 5), (1, 4), (1, 5), (0, 3))
SMALL_FROM = 5
STEPS = (
    "i_qkv", "i_attend", "i_out", "i_ffn", "i_norm", "i_slope", "i_branch", "i_context", "t_q", "t_kv", "t_attend",
    "t_out", "t_ffn0", "t_ffn1", "t_ffn2", "t_norm", "t_slope0", "t_slope1", "t_slope2", "t_branch", "i_back",
    "t_context", "t_back", "i_final", "t_final",
)
SEQUENCE = (
    -1, -1, -1, -1, -1, 0, -1, -1, 1, -1, 2, -1, -1, -1, -1, 100, -1, -1, 200, 300, -1, 101, -1, 3, 201, 4, -1, -1,
    102, 301, -1, 400, 202, 103, 5, 302, 500, 203, 104, 6, 401, -1, 600, 303, 204, 7, 402, 501, -1, 601, 403, 304,
    502, 700, 8, -1, 503, 602, 404, 800, 701, 9, 900, 603, 504, 10, 702, 801, 703, 901, 604, 11, 802, 1000, -1, 803,
    1100, -1, 902, 704, 12, 804, 1001, -1, 1101, 1200, 903, 13, 1002, 904, 1300, 1003, 14, 1102, 1004, 1201, 1400, 15,
    1103, 1301, 1202, 1500, 1401, 1302, 1203, 1600, 1501, 1402, 1601, 1303, 1502, 1602, 1104, 1403, 1503, 1204, 1603,
    1304, 1404, 1504, 1604,
)


def dot(a, b):
    return jnp.dot(a, b, preferred_element_type=F32)


def dot_nt(a, b):
    return lax.dot_general(a, b, NT_DIMS, preferred_element_type=F32)


def dot_tn(a, b):
    return lax.dot_general(a, b, TN_DIMS, preferred_element_type=F32)


def loop(n, body, unroll=None):
    u = min(n, unroll or UNROLL)

    def step(i, carry):
        for k in range(u):
            body(i * u + k)
        return carry

    if n == u:
        step(0, 0)
    else:
        lax.fori_loop(0, n // u, step, 0)
        for k in range(n - n % u, n):
            body(k)


def at(i, size):
    return pl.ds(i * size if isinstance(i, int) else pl.multiple_of(i * size, size), size)


def layer_kernel(dims, *refs):
    nz, ny, nx = dims
    refs = list(refs)

    def take(n):
        got = refs[:n]
        del refs[:n]
        return got

    cap_ref, reg_ref, xt_in, xi_in, ut_in, ui_in = take(6)
    w_in = [take(6), take(6)]
    gain_ref, shift_ref = take(2), take(2)
    res_t, res_i, sg_t, sg_i = take(4)
    w_out = [take(6), take(6)]
    norm_out = take(4)
    wbuf, x_t, x_i = take(3)
    q_b, k_b, v_b = take(2), take(2), take(2)
    n1, inv, low, acc, dctx, sums = take(2), take(2), take(2), take(2), take(2), take(2)
    lt = take(2)
    r_own, r_far = [take(6), take(6)], [take(6), take(6)]
    g_b, r1_b, r2_b, ru_b, rd_b = take(5)
    f_b = take(2)
    small, sv, sr = take(3)
    in_sem, w_sem, ex_s, ex_r, st_s, st_r, sw_s, sw_r, sm_s, sm_r = take(10)
    assert not refs
    u_t, u_i = dctx[0].at[:, pl.ds(0, x_t.shape[1])], dctx[1]

    b, h = lax.axis_index("batch"), lax.axis_index("heads")
    x, y, z = lax.rem(b, nx), lax.rem(lax.div(b, nx), ny), lax.div(b, nx * ny)

    def dev(zz, yy, xx):
        return ((zz * ny + yy) * nx + xx, h)

    partner, nbr_x, nbr_y = (b, 1 - h), dev(z, y, 1 - x), dev(z, 1 - y, x)
    barrier = pltpu.get_barrier_semaphore()
    for who in (partner, nbr_x, nbr_y):
        pl.semaphore_signal(barrier, inc=1, device_id=who, device_id_type=MESH_ID)
    for off in range(1, nz):
        pl.semaphore_signal(barrier, inc=1, device_id=dev(lax.rem(z + off, nz), y, x), device_id_type=MESH_ID)

    def remote(src, dst, ssem, rsem, who):
        return pltpu.make_async_remote_copy(
            src_ref=src, dst_ref=dst, send_sem=ssem, recv_sem=rsem, device_id=who, device_id_type=MESH_ID
        )

    T, I = 0, 1
    pieces = []

    def piece(name, ref, rows, cols):
        pieces.append((name, ref, rows, cols))

    td, ti = x_t.shape[1], x_i.shape[1]
    inner = q_b[0].shape[1]
    parts = w_in[T][1].shape[1] // 1024
    whole = lambda s, w: w_in[s][w]
    tu = lambda j: w_in[T][1].at[:, pl.ds(j * 1024, 1024)]
    tw = lambda j: w_in[T][0].at[pl.ds(j * 1024, 1024), :]
    piece("tk", whole(T, 4), td, inner)
    piece("tv", whole(T, 5), td, inner)
    piece("iq", whole(I, 3), ti, inner)
    piece("io", whole(I, 2), inner, ti)
    piece("iu", whole(I, 1), ti, ti)
    piece("id", whole(I, 0), ti, ti)
    piece("tq", whole(T, 3), td, inner)
    piece("ik", whole(I, 4), ti, inner)
    piece("iv", whole(I, 5), ti, inner)
    piece("to", whole(T, 2), inner, td)
    for j in range(parts):
        piece("tu%d" % j, tu(j), td, 1024)
        piece("td%d" % j, tw(j), 1024, td)
    piece("to", whole(T, 2), inner, td)
    for name, s, w in (("iq", I, 3), ("tk", T, 4), ("tv", T, 5), ("tq", T, 3), ("ik", I, 4), ("iv", I, 5)):
        rows = td if s == T else ti
        piece(name, whole(s, w), rows, inner)
    issued = [0]
    held = {}

    def weight_copy(k, slot):
        name, ref, rows, cols = pieces[k]
        return pltpu.make_async_copy(ref, wbuf.at[slot, pl.ds(0, rows), pl.ds(0, cols)], w_sem.at[slot])

    def issue(slot):
        if issued[0] < len(pieces):
            k = issued[0]
            issued[0] += 1
            weight_copy(k, slot).start()
            assert pieces[k][0] not in held
            held[pieces[k][0]] = [k, slot, False]

    def weight(name):
        k, slot, ready = held[name]
        if not ready:
            weight_copy(k, slot).wait()
            held[name][2] = True
        _, _, rows, cols = pieces[k]
        return wbuf.at[slot, pl.ds(0, rows), pl.ds(0, cols)]

    def release(name):
        k, slot, ready = held.pop(name)
        issue(slot)

    pairs_n, regions = xi_in.shape[:2]
    pad = 112

    def image_rows(src, dst, k):
        return [
            pltpu.make_async_copy(src.at[p], dst.at[pl.ds(p * pad, regions), :], in_sem.at[k + p]) for p in range(pairs_n)
        ]

    def start(copies):
        for c in copies:
            c.start()

    def wait(copies):
        for c in copies:
            c.wait()

    in_copies = [
        [pltpu.make_async_copy(xt_in, x_t, in_sem.at[0])], image_rows(xi_in, x_i, 2),
        [pltpu.make_async_copy(ut_in, u_t, in_sem.at[1])], image_rows(ui_in, u_i, 2 + pairs_n),
    ]
    start(in_copies[0])
    issue(0)
    start(in_copies[1])
    issue(1)
    issue(2)
    start(in_copies[3])
    start(in_copies[2])
    for slot in range(3, SLOTS):
        issue(slot)

    cap = x_t.shape[0] // pairs_n
    m_i, m_t = pairs_n * pad, x_t.shape[0]
    m_of, d_of = (m_t, m_i), (td, ti)
    x_of = (x_t, x_i)

    tail = pl.ds(m_i, x_i.shape[0] - m_i)
    for ref in (x_i, low[I], *r_own[I]):
        ref[tail, :] = jnp.zeros((x_i.shape[0] - m_i, ref.shape[1]), BF16)
    for ref in (*sums,):
        ref[...] = jnp.zeros(ref.shape, F32)

    for ref in (x_i, u_i):
        for p in range(pairs_n):
            ref[pl.ds(p * pad + regions, pad - regions), :] = jnp.zeros((pad - regions, ref.shape[1]), BF16)

    lengths = {
        T: [reg_ref[h * pairs_n + p] for p in range(pairs_n)],
        I: [cap_ref[h * pairs_n + p] for p in range(pairs_n)],
    }

    ex_left, ex_right = {}, {}
    n_left = max(LEFTS) + 1
    for s in (T, I):
        for l in range(n_left):
            k = s * n_left + l
            ex_left[s, l] = remote(
                lt[s].at[l, :, pl.ds(0, 256)], lt[s].at[l, :, pl.ds(256, 256)], ex_s.at[k], ex_r.at[k], partner
            )
        for w in range(6):
            k = 2 * n_left + s * 6 + w
            half = r_far[s][w].shape[1]
            ex_right[s, w] = remote(
                r_own[s][w].at[:, pl.ds(pl.multiple_of((1 - h) * half, 128), half)], r_far[s][w],
                ex_s.at[k], ex_r.at[k], partner,
            )
    arrived = set()
    entered = []

    def enter():
        if not entered:
            entered.append(1)
            pl.semaphore_wait(barrier, 3 + nz - 1)

    def send_left(s, l, src):
        def body(j):
            lt[s][l, at(j, TILE), pl.ds(0, 256)] = src[:, at(j, TILE)].T

        loop(d_of[s] // TILE, body)
        enter()
        ex_left[s, l].start()

    def send_right(s, w):
        enter()
        ex_right[s, w].start()

    def project(src, rows, w, dst):
        def body(j):
            dst[pl.ds(0, rows), at(j, TILE)] = dot(src[pl.ds(0, rows), :], w[:, at(j, TILE)]).astype(BF16)

        loop(w.shape[1] // TILE, body)

    def softmaxes(parts_of):
        scores = [dot_nt(q, k) * SCALE for q, k, _ in parts_of]
        scores = [
            jnp.where(lax.broadcasted_iota(jnp.int32, v.shape, 1) < live, v, NEG)
            for v, (_, _, live) in zip(scores, parts_of)
        ]
        tops = [jnp.max(v, axis=-1, keepdims=True) for v in scores]
        exps = [jnp.exp(v - t) for v, t in zip(scores, tops)]
        totals = [jnp.sum(e, axis=-1, keepdims=True) for e in exps]
        return [e / t for e, t in zip(exps, totals)]

    span = (cap, pad)

    def rows_of(s, p):
        return pl.ds(p * span[s], span[s])

    def units(i):
        return [(at(i * HEAD_GROUP + k, HEAD), p) for k in range(HEAD_GROUP) for p in range(pairs_n)]

    def attend(s):
        o = 1 - s

        def body(i):
            group = units(i)
            probs = softmaxes(
                [(q_b[s][rows_of(s, p), c], k_b[o][rows_of(o, p), c], lengths[s][p]) for c, p in group]
            )
            got = [dot(prob.astype(BF16), v_b[o][rows_of(o, p), c]) for prob, (c, p) in zip(probs, group)]
            for g, (c, p) in zip(got, group):
                r_own[s][2][rows_of(s, p), c] = g.astype(BF16)

        loop(HEADS // HEAD_GROUP, body, 1)
        send_right(s, 2)

    def attend_back(s):
        o = 1 - s

        def body(i):
            group = units(i)
            qs = [q_b[s][rows_of(s, p), c] for c, p in group]
            ks = [k_b[o][rows_of(o, p), c] for c, p in group]
            dcs = [dctx[s][rows_of(s, p), c] for c, p in group]
            dps = [dot_nt(dc, v_b[o][rows_of(o, p), c]) for dc, (c, p) in zip(dcs, group)]
            probs = softmaxes([(q, k, lengths[s][p]) for q, k, (_, p) in zip(qs, ks, group)])
            dvs = [dot_tn(prob.astype(BF16), dc) for prob, dc in zip(probs, dcs)]
            inner_sums = [jnp.sum(prob * dp, axis=-1, keepdims=True) for prob, dp in zip(probs, dps)]
            dss = [(prob * (dp - t)).astype(BF16) for prob, dp, t in zip(probs, dps, inner_sums)]
            dqs = [dot(ds, k) * SCALE for ds, k in zip(dss, ks)]
            dks = [dot_tn(ds, q) * SCALE for ds, q in zip(dss, qs)]
            for (c, p), dq, dk, dv in zip(group, dqs, dks, dvs):
                rq, rk = rows_of(s, p), rows_of(o, p)
                r_own[s][3][rq, c] = dq.astype(BF16)
                r_own[o][4][rk, c] = dk.astype(BF16)
                r_own[o][5][rk, c] = dv.astype(BF16)

        loop(HEADS // HEAD_GROUP, body, 1)
        send_right(s, 3)
        send_right(o, 4)
        send_right(o, 5)

    RB = 32

    def mean(v):
        return jnp.mean(v, axis=-1, keepdims=True)

    def sum8(v):
        return jnp.sum(v.reshape(v.shape[0] // 8, 8, v.shape[1]), axis=0)

    def norm_one(s):
        gain, shift = gain_ref[s][0:1, :], shift_ref[s][0:1, :]

        def body(i):
            r = at(i, RB)
            v = x_of[s][r, :].astype(F32) + acc[s][r, :]
            c = v - mean(v)
            iv = lax.rsqrt(mean(c * c) + EPS)
            n = c * iv
            n1[s][r, :] = n
            inv[s][r, :] = jnp.broadcast_to(iv, (RB, 128))
            low[s][r, :] = (n * gain + shift).astype(BF16)

        loop(m_of[s] // RB, body)
        send_left(s, 1, low[s])

    def norm_two(s, up_ref, res_ref):
        gain0, shift0 = gain_ref[s][0:1, :], shift_ref[s][0:1, :]
        gain, shift = gain_ref[s][1:2, :], shift_ref[s][1:2, :]

        def body(i):
            r = at(i, RB)
            v = n1[s][r, :] * gain0 + shift0 + acc[s][r, :]
            c = v - mean(v)
            iv = lax.rsqrt(mean(c * c) + EPS)
            n = c * iv
            up = up_ref[r, :].astype(F32)
            res_ref[r, :] = (n * gain + shift).astype(BF16)
            un = up * n
            sums[s][1] = sums[s][1] + sum8(un)
            sums[s][3] = sums[s][3] + sum8(up)
            u = up * gain
            d = iv * (u - mean(u) - n * mean(un * gain))
            acc[s][r, :] = d
            low[s][r, :] = d.astype(BF16)

        loop(m_of[s] // RB, body)
        send_left(s, 0, low[s])

    def norm_one_back(s):
        gain = gain_ref[s][0:1, :]

        def body(i):
            r = at(i, RB)
            g, n = acc[s][r, :], n1[s][r, :]
            gn = g * n
            sums[s][0] = sums[s][0] + sum8(gn)
            sums[s][2] = sums[s][2] + sum8(g)
            u = g * gain
            d = inv[s][r, 0:1] * (u - mean(u) - n * mean(gn * gain))
            acc[s][r, :] = d
            low[s][r, :] = d.astype(BF16)

        loop(m_of[s] // RB, body)
        send_left(s, 2, low[s])

    def out_project(s, w):
        m = m_of[s]

        def body(j):
            acc[s][pl.ds(0, m), at(j, TILE)] = dot(r_own[s][2][pl.ds(0, m), :], w[:, at(j, TILE)])

        loop(d_of[s] // TILE, body)

    def ffn(s, j, up_w, down_w):
        m, base = m_of[s], j * 1024

        def hidden(i):
            c = pl.ds(pl.multiple_of(base + i * TILE, TILE), TILE)
            v = dot(low[s][pl.ds(0, m), :], up_w[:, at(i, TILE)])
            half = 0.5 * (1.0 + lax.erf(v * (1.0 / math.sqrt(2.0))))
            r_own[s][0][pl.ds(0, m), c] = (v * half).astype(BF16)
            r_own[s][1][pl.ds(0, m), c] = (half + v * jnp.exp(-0.5 * v * v) * (1.0 / math.sqrt(2.0 * math.pi))).astype(BF16)

        loop(1024 // TILE, hidden)

        def second(i):
            part = dot(r_own[s][0][pl.ds(0, m), pl.ds(base, 1024)], down_w[:, at(i, TILE)])
            if j == 0:
                acc[s][pl.ds(0, m), at(i, TILE)] = part
            else:
                acc[s][pl.ds(0, m), at(i, TILE)] += part

        loop(d_of[s] // TILE, second)

    def slope_back(s, j, down_w):
        m, base = m_of[s], j * 1024

        def body(i):
            c = pl.ds(pl.multiple_of(base + i * TILE, TILE), TILE)
            g = dot_nt(low[s][pl.ds(0, m), :], down_w[at(i, TILE), :])
            r_own[s][1][pl.ds(0, m), c] = (g * r_own[s][1][pl.ds(0, m), c].astype(F32)).astype(BF16)

        loop(1024 // TILE, body)

    def back_add(s, src, cols, w):
        m = m_of[s]

        def body(i):
            acc[s][pl.ds(0, m), at(i, TILE)] += dot_nt(src[pl.ds(0, m), cols], w[at(i, TILE), :])

        loop(d_of[s] // TILE, body)

    def context_back(s, w):
        m = m_of[s]

        def body(i):
            dctx[s][pl.ds(0, m), at(i, TILE)] = dot_nt(low[s][pl.ds(0, m), :], w[at(i, TILE), :]).astype(BF16)

        loop(inner // TILE, body)

    def final(s, dst):
        def body(i):
            dst[at(i, RB), :] = acc[s][at(i, RB), :].astype(BF16)

        loop(m_of[s] // RB, body)

    def gather_rows(src, dst):
        for p in range(pairs_n):
            dst[p] = src[pl.ds(p * pad, regions), :]

    all_cols = pl.ds(0, 1024)

    def step(name):
        if name == "i_qkv":
            wait(in_copies[0])
            project(x_t, m_t, weight("tk"), k_b[T])
            release("tk")
            project(x_t, m_t, weight("tv"), v_b[T])
            release("tv")
            wait(in_copies[1])
            project(x_i, m_i, weight("iq"), q_b[I])
            release("iq")
        elif name == "i_attend":
            attend(I)
        elif name == "i_out":
            out_project(I, weight("io"))
            norm_one(I)
        elif name == "i_ffn":
            ffn(I, 0, weight("iu"), weight("id"))
            send_right(I, 0)
        elif name == "i_norm":
            wait(in_copies[3])
            norm_two(I, u_i, u_i)
            gather_rows(u_i, res_i)
        elif name == "i_slope":
            slope_back(I, 0, weight("id"))
            send_right(I, 1)
            release("id")
        elif name == "i_branch":
            back_add(I, r_own[I][1], all_cols, weight("iu"))
            release("iu")
            norm_one_back(I)
        elif name == "i_context":
            context_back(I, weight("io"))
            release("io")
            send_left(I, 3, x_i)
        elif name == "t_q":
            project(x_t, m_t, weight("tq"), q_b[T])
            release("tq")
            send_left(T, 3, x_t)
        elif name == "t_kv":
            project(x_i, m_i, weight("ik"), k_b[I])
            release("ik")
            project(x_i, m_i, weight("iv"), v_b[I])
            release("iv")
        elif name == "t_attend":
            attend(T)
        elif name == "t_out":
            out_project(T, weight("to"))
            release("to")
            norm_one(T)
        elif name.startswith("t_ffn"):
            j = int(name[-1])
            ffn(T, j, weight("tu%d" % j), weight("td%d" % j))
            if j == parts - 1:
                send_right(T, 0)
        elif name == "t_norm":
            wait(in_copies[2])
            norm_two(T, u_t, res_t)
        elif name.startswith("t_slope"):
            j = int(name[-1])
            slope_back(T, j, weight("td%d" % j))
            release("td%d" % j)
            if j == parts - 1:
                send_right(T, 1)
        elif name == "t_branch":
            for j in range(parts):
                back_add(T, r_own[T][1], pl.ds(j * 1024, 1024), weight("tu%d" % j))
                release("tu%d" % j)
            norm_one_back(T)
            small_fill()
        elif name == "t_context":
            context_back(T, weight("to"))
            release("to")
        elif name == "i_back":
            attend_back(I)
            back_add(I, r_own[I][3], all_cols, weight("iq"))
            release("iq")
            back_add(T, r_own[T][4], all_cols, weight("tk"))
            release("tk")
            back_add(T, r_own[T][5], all_cols, weight("tv"))
            release("tv")
        elif name == "t_back":
            attend_back(T)
        elif name == "i_final":
            back_add(I, r_own[I][4], all_cols, weight("ik"))
            release("ik")
            back_add(I, r_own[I][5], all_cols, weight("iv"))
            release("iv")
            final(I, u_i)
            gather_rows(u_i, sg_i)
        elif name == "t_final":
            back_add(T, r_own[T][3], all_cols, weight("tq"))
            release("tq")
            final(T, sg_t)

    def token(k):
        if k < 100:
            for c in (2 * k, 2 * k + 1):
                compute(c)
                s1(c).start()
            return
        p, lag = k // 100 - 1, k % 100
        stage(p, lag)
        if lag == nz and SMALL_FROM <= p < SMALL_FROM + 5:
            small_step(p - SMALL_FROM)

    small_copies = []

    def small_start(src, dst, i, who):
        c = remote(src, dst, sm_s.at[i], sm_r.at[i], who)
        c.start()
        small_copies.append(c)

    def small_fill():
        small[...] = jnp.zeros(small.shape, F32)
        for s in (T, I):
            for k in range(4):
                small[pl.ds(4 * s + k, 1), pl.ds(0, d_of[s])] = jnp.sum(sums[s][k], axis=0, keepdims=True)

    def small_step(i):
        if i == 0:
            small_start(small, sr.at[0], 0, partner)
        elif i == 1:
            small_copies[0].wait_recv()
            sv[0] = small[...] + sr[0]
            small_start(sv.at[0], sr.at[1], 1, nbr_x)
        elif i == 2:
            small_copies[1].wait_recv()
            sv[1] = sv[0] + sr[1]
            small_start(sv.at[1], sr.at[2], 2, nbr_y)
        elif i == 3:
            small_copies[2].wait_recv()
            sv[2] = sv[1] + sr[2]
            for off in range(1, nz):
                small_start(sv.at[2], sr.at[2 + off], 2 + off, dev(lax.rem(z + off, nz), y, x))
        elif i == 4:
            total = sv[2]
            for off in range(1, nz):
                small_copies[2 + off].wait_recv()
                total = total + sr[2 + off]
            wide = total.shape[1]
            me = b * 2 + h
            for s in (T, I):
                own = norm_out[2 * s].shape[1]
                mine = pltpu.roll(total, lax.rem(wide - me * own, wide), 1)
                norm_out[2 * s][...] = mine[4 * s : 4 * s + 2, :own]
                norm_out[2 * s + 1][...] = mine[4 * s + 2 : 4 * s + 4, :own]

    chunks = []
    for s, w in PRODUCED:
        for o in range(0, r_far[s][w].shape[1], CW):
            late = len(chunks) in LATE
            chunks.append((s, w, o, "xy"[len(chunks) % 2], len([1 for c in chunks if c[0] == s]), late))
    n = len(chunks)

    def bufs(c):
        rows = pl.ds(0, d_of[chunks[c][0]] // (nz * ny * nx))
        return (
            g_b.at[c % G_RING, :, :, :, rows], r1_b.at[c % R_RING, :, :, rows], r2_b.at[c % R_RING, :, rows],
            ru_b.at[c % Z_RING, :, :, rows], rd_b.at[c % Z_RING, :, :, rows],
        )

    def compute(c):
        s, w, o, way, _, _ = chunks[c]
        for copy, key in ((ex_left[s, LEFTS[w]], (0, s, LEFTS[w])), (ex_right[s, w], (1, s, w))):
            if key not in arrived:
                arrived.add(key)
                copy.wait_recv()
        blk = d_of[s] // (nz * ny * nx)
        size = ny * nx * blk
        half = r_far[s][w].shape[1]
        mine = pl.ds(pl.multiple_of(h * half + o, 128), CW)
        g = g_b.at[c % G_RING]

        def body(i):
            r = pl.ds(pl.multiple_of(i * size, 64), size)
            l = LEFTS[w]
            res = dot(lt[s][l, r, pl.ds(0, 256)], r_own[s][w][:, mine]) + dot(
                lt[s][l, r, pl.ds(256, 256)], r_far[s][w][:, pl.ds(o, CW)]
            )
            g[i, :, :, pl.ds(0, blk)] = res.astype(BF16).reshape(ny, nx, blk, CW)

        loop(nz, body)

    def add(dst, src):
        dst[...] = (dst[...].astype(F32) + src[...].astype(F32)).astype(BF16)

    def s1(c):
        g, r1 = bufs(c)[:2]
        if chunks[c][3] == "x":
            return remote(g.at[:, :, 1 - x], r1, st_s.at[0, c % G_RING], st_r.at[0, c % G_RING], nbr_x)
        return remote(g.at[:, 1 - y], r1, st_s.at[0, c % G_RING], st_r.at[0, c % G_RING], nbr_y)

    def s2(c):
        g, _, r2 = bufs(c)[:3]
        first, late = chunks[c][3] == "x", chunks[c][5]
        far = (1 - y, x) if first else (y, 1 - x)
        src, dst = (g.at[z, far[0], far[1]], r2.at[0]) if late else (g.at[:, far[0], far[1]], r2)
        return remote(src, dst, st_s.at[1, c % G_RING], st_r.at[1, c % G_RING], nbr_y if first else nbr_x)

    def blocks(c, t):
        g, _, _, ru, rd = bufs(c)
        if not chunks[c][5]:
            return [(g.at[t, y, x], ru.at[t, 0], rd.at[t, 0])]
        here = (lambda j: g.at[t, j, x]) if chunks[c][3] == "x" else (lambda j: g.at[t, y, j])
        return [(here(j), ru.at[t, j], rd.at[t, j]) for j in range(2)]

    def along(c, rest, buf):
        g = bufs(c)[0]
        if not chunks[c][5]:
            return g.at[rest, y, x], buf.at[rest, 0]
        return (g.at[rest, :, x] if chunks[c][3] == "x" else g.at[rest, y]), buf.at[rest]

    def up(c, k):
        src, dst = along(c, pl.ds(k + 1, nz - 1 - k), bufs(c)[3])
        return remote(src, dst, st_s.at[2, c % G_RING], st_r.at[2, c % G_RING], dev(k + 1, y, x))

    def down(c, k):
        src, dst = along(c, pl.ds(0, k), bufs(c)[4])
        return remote(src, dst, st_s.at[3, c % G_RING], st_r.at[3, c % G_RING], dev(k - 1, y, x))

    def swap(c):
        s, w, o, _, k, _ = chunks[c]
        out = w_out[s][w]
        half = out.shape[1] // 2
        return remote(
            f_b[s].at[k], out.at[:, pl.ds(pl.multiple_of(h * half + o, 128), CW)],
            sw_s.at[c], sw_r.at[c], partner,
        )

    def ends(c):
        @pl.when(z == 0)
        def _():
            up(c, 0).start()

        @pl.when(z == nz - 1)
        def _():
            down(c, nz - 1).start()

    def stage2(pair):
        for c in pair:
            s1(c).wait_recv()
        for c in pair:
            g, r1 = bufs(c)[:2]

            def body(i):
                for j in range(2):
                    add(g.at[i, j, x] if chunks[c][3] == "x" else g.at[i, y, j], r1.at[i, j])

            loop(nz, body)
            if chunks[c][5]:
                ends(c)
            else:
                s2(c).start()

    def stage3(pair):
        for c in pair:
            s2(c).wait_recv()
        for c in pair:
            g, _, r2 = bufs(c)[:3]
            loop(nz, lambda i: add(g.at[i, y, x], r2.at[i]))
            ends(c)

    def hop(pair, d):
        for c in pair:

            @pl.when(z == d)
            def _(c=c):
                up(c, d - 1).wait_recv()
                for t in range(d + 1, nz):
                    for here, below, _ in blocks(c, t):
                        add(here, below)
                up(c, d).start()

            @pl.when(z == nz - 1 - d)
            def _(c=c):
                down(c, nz - d).wait_recv()
                for t in range(0, nz - 1 - d):
                    for here, _, above in blocks(c, t):
                        add(here, above)
                down(c, nz - 1 - d).start()

    def last_hops(c, k):
        if k == nz - 1:
            up(c, k - 1).wait_recv()
        if k == 0:
            down(c, 1).wait_recv()

    def z_total(c, k, j):
        g, _, _, ru, rd = bufs(c)
        late, first = chunks[c][5], chunks[c][3] == "x"
        lane = j if late else 0
        row, col = (j, x) if late and first else (y, j) if late else (y, x)
        total = g[k, row, col].astype(F32)
        if k > 0:
            total = total + ru[k, lane].astype(F32)
        if k < nz - 1:
            total = total + rd[k, lane].astype(F32)
        return total

    def fold(pair):
        for c in pair:
            far = 1 - y if chunks[c][3] == "x" else 1 - x
            for k in range(nz):

                @pl.when(z == k)
                def _(c=c, k=k, far=far):
                    last_hops(c, k)
                    got = z_total(c, k, far).astype(BF16)
                    g = bufs(c)[0]
                    if chunks[c][3] == "x":
                        g[k, far, x] = got
                    else:
                        g[k, y, far] = got

            s2(c).start()

    def finish(pair):
        for c in pair:
            s, w, o, way, idx, late = chunks[c]
            out = w_out[s][w]
            r, half = out.shape[0], out.shape[1] // 2
            cols = pl.ds(pl.multiple_of(h * half + o, 128), CW)
            if late:
                s2(c).wait_recv()
            for k in range(nz):

                @pl.when(z == k)
                def _(k=k):
                    if not late:
                        last_hops(c, k)
                    total = z_total(c, k, y if way == "x" else x)
                    if late:
                        total = total + bufs(c)[2][0].astype(F32)
                    first, second = total[:r], total[r:]
                    out[:, cols] = jnp.where(h == 0, first, second)
                    f_b[s][idx] = jnp.where(h == 0, second, first)

            swap(c).start()
            s1(c).wait_send()
            s2(c).wait_send()
            for k in range(nz):

                @pl.when(z == k)
                def _(k=k):
                    if k < nz - 1:
                        up(c, k).wait_send()
                    if k > 0:
                        down(c, k).wait_send()


    def stage(p, lag):
        pair = (2 * p, 2 * p + 1)
        if lag == 0:
            return stage2(pair)
        if lag == nz:
            return finish(pair)
        for late in (True, False):
            part = [c for c in pair if chunks[c][5] == late]
            if late and lag == nz - 1:
                fold(part)
            elif not late and lag == 1:
                stage3(part)
            else:
                hop(part, lag if late else lag - 1)

    names = iter(STEPS)
    for k in SEQUENCE:
        if k < 0:
            step(next(names))
        else:
            token(k)

    for c in range(n):
        swap(c).wait_recv()
        swap(c).wait_send()
    for copy in (*ex_left.values(), *ex_right.values()):
        copy.wait_send()
    for copy in small_copies:
        copy.wait_send()


def hand_over(*refs):
    n = len(refs) // 2
    copies = [pltpu.make_async_copy(refs[i], refs[n + i], refs[-1].at[i]) for i in range(n)]
    for c in copies:
        c.start()
    for c in copies:
        c.wait()


def layer(dims, lengths, states, upstream, weights, gains, shifts):
    nz, ny, nx = dims
    chips = nz * ny * nx
    xt, xi = states
    pairs, cap, td = xt.shape
    regions, ti = xi.shape[1:]
    xt, ut = xt.reshape(pairs * cap, td), upstream[0].reshape(pairs * cap, td)
    mt = pairs * cap
    fixed = 256
    inner = weights[0][3].shape[1]
    d_of = (td, ti)
    cols = [[w.shape[0], weights[s][1].shape[1], inner, inner, inner, inner] for s, w in ((0, weights[0][0]), (1, weights[1][0]))]
    V, DMA = pltpu.VMEM, pltpu.SemaphoreType.DMA
    rows_of = (mt, fixed)
    ti_blk = ti // chips
    counts = [sum(c // 2 // CW for c in cols[s]) for s in range(2)]
    n = sum(counts)
    act = lambda dt, width: [V((rows_of[s], width[s]), dt) for s in range(2)]
    scratch = [
        V((SLOTS, 1024, 1024), BF16),
        V((mt, td), BF16), V((fixed, ti), BF16),
        *act(BF16, (inner, inner)), *act(BF16, (inner, inner)), *act(BF16, (inner, inner)),
        *act(F32, d_of), *act(F32, (128, 128)), *act(BF16, d_of),
        *act(F32, d_of), *act(BF16, (inner, inner)),
        *[V((4, 8, d), F32) for d in d_of],
        *[V((4, d, 512), BF16) for d in d_of],
        *[V((rows_of[s], c), BF16) for s in range(2) for c in cols[s]],
        *[V((rows_of[s], c // 2), BF16) for s in range(2) for c in cols[s]],
        V((G_RING, nz, ny, nx, ti_blk, CW), BF16),
        V((R_RING, nz, 2, ti_blk, CW), BF16),
        V((R_RING, nz, ti_blk, CW), BF16),
        V((Z_RING, nz, 2, ti_blk, CW), BF16),
        V((Z_RING, nz, 2, ti_blk, CW), BF16),
        *[V((counts[s], d_of[s] // chips // 2, CW), F32) for s in range(2)],
        V((8, max(d_of)), F32), V((3, 8, max(d_of)), F32), V((2 + nz, 8, max(d_of)), F32),
        DMA((2 + 2 * pairs,)), DMA((SLOTS,)), DMA((20,)), DMA((20,)), DMA((4, G_RING)), DMA((4, G_RING)), DMA((n,)), DMA((n,)), DMA((2 + nz,)), DMA((2 + nz,)),
    ]
    hbm = pl.BlockSpec(memory_space=pl.ANY)
    vm = pl.BlockSpec(memory_space=pltpu.VMEM)
    smem = pl.BlockSpec(memory_space=pltpu.SMEM)
    sds = jax.ShapeDtypeStruct
    outs = [
        sds((mt, td), BF16), sds((pairs, regions, ti), BF16), sds((mt, td), BF16), sds((pairs, regions, ti), BF16),
        *[sds((d_of[s] // chips // 2, c), F32) for s in range(2) for c in cols[s]],
        *[sds((2, d_of[s] // chips // 2), F32) for s in range(2) for _ in range(2)],
    ]
    got = pl.pallas_call(
        functools.partial(layer_kernel, dims),
        out_shape=outs,
        in_specs=[smem, smem, *[hbm] * 4, *[hbm] * 12, *[vm] * 4],
        out_specs=[vm] * len(outs),
        scratch_shapes=scratch,
        compiler_params=pltpu.CompilerParams(
            collective_id=0, has_side_effects=True, vmem_limit_bytes=67043328
        ),
        name="co_layer",
    )(*lengths, xt, xi, ut, upstream[1], *weights[0], *weights[1], *gains, *shifts)
    n = len(got)
    return pl.pallas_call(
        hand_over,
        out_shape=outs,
        in_specs=[vm] * n,
        out_specs=[hbm] * n,
        scratch_shapes=[DMA((n,))],
        name="hand_over",
    )(*got)


def matmul(row_values, weight):
    return jnp.dot(row_values, weight, preferred_element_type=F32)


def project_back(gradient, weight):
    return lax.dot_general(gradient, weight, (((1,), (1,)), ((), ())), preferred_element_type=F32)


def outer_sum(row_values, gradient):
    return lax.dot_general(row_values, gradient, (((0,), (0,)), ((), ())), preferred_element_type=F32)


def layer_norm(values, gain, shift):
    row_mean = jnp.mean(values, axis=-1, keepdims=True)
    centred = values - row_mean
    spread = jnp.mean(centred * centred, axis=-1, keepdims=True)
    inverse = lax.rsqrt(spread + EPS)
    normed = centred * inverse
    return (normed * gain + shift, normed, inverse)


def norm_back(gradient, normed, inverse, gain):
    scaled = gradient * gain
    first_mean = jnp.mean(scaled, axis=-1, keepdims=True)
    second_mean = jnp.mean(scaled * normed, axis=-1, keepdims=True)
    into = inverse * (scaled - first_mean - normed * second_mean)
    return (into, jnp.sum(gradient * normed, axis=0), jnp.sum(gradient, axis=0))


def gelu_value(values):
    return 0.5 * values * (1.0 + jax.scipy.special.erf(values / math.sqrt(2.0)))


def gelu_slope(values):
    return 0.5 * (1.0 + jax.scipy.special.erf(values / math.sqrt(2.0))) + values * jnp.exp(
        -0.5 * values * values
    ) / math.sqrt(2.0 * math.pi)


def attend(queries, key_rows, value_rows, lengths):
    score_scale = 1.0 / math.sqrt(queries.shape[-1])
    scores = jnp.einsum("bqhd,bkhd->bhqk", queries, key_rows, preferred_element_type=F32) * score_scale
    live_mask = lax.broadcasted_iota(jnp.int32, scores.shape, 3) < lengths[:, None, None, None]
    scores = jnp.where(live_mask, scores, NEG)
    weights = jnp.exp(scores - jnp.max(scores, axis=-1, keepdims=True))
    probability = weights / jnp.sum(weights, axis=-1, keepdims=True)
    context = jnp.einsum("bhqk,bkhd->bqhd", probability.astype(BF16), value_rows, preferred_element_type=F32)
    return context.astype(BF16), probability


def attend_back(queries, key_rows, value_rows, probability, context_grad):
    score_scale = 1.0 / math.sqrt(queries.shape[-1])
    value_grad = jnp.einsum(
        "bhqk,bqhd->bkhd", probability.astype(BF16), context_grad, preferred_element_type=F32
    )
    prob_grad = jnp.einsum("bqhd,bkhd->bhqk", context_grad, value_rows, preferred_element_type=F32)
    row_inner = jnp.sum(probability * prob_grad, axis=-1, keepdims=True)
    score_grad = (probability * (prob_grad - row_inner)).astype(BF16)
    query_grad = jnp.einsum("bhqk,bkhd->bqhd", score_grad, key_rows, preferred_element_type=F32) * score_scale
    key_grad = jnp.einsum("bhqk,bqhd->bkhd", score_grad, queries, preferred_element_type=F32) * score_scale
    return (query_grad.astype(BF16), key_grad.astype(BF16), value_grad.astype(BF16))


def stream_forward(row_values, context, out_weight, up_weight, down_weight, gains, shifts):
    attended = matmul(context, out_weight)
    first_out, normed_one, inverse_one = layer_norm(row_values.astype(F32) + attended, gains[0], shifts[0])
    first_low = first_out.astype(BF16)
    before = matmul(first_low, up_weight)
    active = gelu_value(before).astype(BF16)
    second_out, normed_two, inverse_two = layer_norm(
        first_out + matmul(active, down_weight), gains[1], shifts[1]
    )
    kept_state = (normed_one, inverse_one, first_low, before, active, normed_two, inverse_two)
    return (second_out.astype(BF16), kept_state)


def stream_back(upstream, kept_state, out_weight, up_weight, down_weight, gains):
    normed_one, inverse_one, first_low, before, active, normed_two, inverse_two = kept_state
    branch_grad, gain_two, shift_two = norm_back(upstream.astype(F32), normed_two, inverse_two, gains[1])
    branch_low = branch_grad.astype(BF16)
    active_grad = project_back(branch_low, down_weight)
    before_grad = (active_grad * gelu_slope(before)).astype(BF16)
    first_grad = project_back(before_grad, up_weight) + branch_grad
    sum_grad, gain_one, shift_one = norm_back(first_grad, normed_one, inverse_one, gains[0])
    sum_low = sum_grad.astype(BF16)
    context_grad = project_back(sum_low, out_weight).astype(BF16)
    return sum_grad, context_grad, branch_low, before_grad, sum_low, (gain_one, gain_two, shift_one, shift_two)


def make_local(mesh):
    devices = mesh.shape["batch"] * mesh.shape["heads"]

    def local(
        text_states, image_states, caption_lengths, region_counts,
        text_query, text_key, text_value, text_output, text_up, text_down, text_gains, text_shifts,
        image_query, image_key, image_value, image_output, image_up, image_down, image_gains, image_shifts,
        text_upstream, image_upstream,
    ):
        def parts(grads):
            down, up, out, query, key, value = grads
            return query, key, value, out.T, up, down.T

        if mesh.shape["batch"] == 16 and mesh.shape["heads"] == 2:
            text_weights = (text_down, text_up, text_output, text_query, text_key, text_value)
            image_weights = (image_down, image_up, image_output, image_query, image_key, image_value)
            got = layer(
                (4, 2, 2), (caption_lengths, region_counts), (text_states, image_states), (text_upstream, image_upstream),
                (text_weights, image_weights), (text_gains, image_gains), (text_shifts, image_shifts),
            )
            return (
                got[0].reshape(text_states.shape), got[1], got[2].reshape(text_states.shape), got[3],
                *parts(got[4:10]), got[16], got[17], *parts(got[10:16]), got[18], got[19],
            )
        pair_count, cap_len, text_width = text_states.shape
        region_len, image_width = image_states.shape[1:]
        text_rows = text_states.reshape(pair_count * cap_len, text_width)
        image_rows = image_states.reshape(pair_count * region_len, image_width)
        core = lax.axis_index("heads")
        captions = lax.dynamic_slice(caption_lengths, (core * pair_count,), (pair_count,))
        regions = lax.dynamic_slice(region_counts, (core * pair_count,), (pair_count,))

        def heads_of(row_values, weight, length):
            return matmul(row_values, weight).astype(BF16).reshape(pair_count, length, HEADS, HEAD)

        tq, tk, tv = (heads_of(text_rows, w, cap_len) for w in (text_query, text_key, text_value))
        iq, ik, iv = (heads_of(image_rows, w, region_len) for w in (image_query, image_key, image_value))
        text_context, text_prob = attend(tq, ik, iv, regions)
        image_context, image_prob = attend(iq, tk, tv, captions)
        flat = lambda v: v.reshape(v.shape[0] * v.shape[1], -1)
        text_result, text_kept = stream_forward(
            text_rows, flat(text_context), text_output, text_up, text_down, text_gains, text_shifts
        )
        image_result, image_kept = stream_forward(
            image_rows, flat(image_context), image_output, image_up, image_down, image_gains, image_shifts
        )
        t_sum, t_cgrad, t_branch, t_zgrad, t_slow, t_small = stream_back(
            text_upstream.reshape(text_rows.shape), text_kept, text_output, text_up, text_down, text_gains
        )
        i_sum, i_cgrad, i_branch, i_zgrad, i_slow, i_small = stream_back(
            image_upstream.reshape(image_rows.shape), image_kept, image_output, image_up, image_down, image_gains
        )
        g_tq, g_ik, g_iv = attend_back(tq, ik, iv, text_prob, t_cgrad.reshape(tq.shape))
        g_iq, g_tk, g_tv = attend_back(iq, tk, tv, image_prob, i_cgrad.reshape(iq.shape))
        g_tq, g_tk, g_tv, g_iq, g_ik, g_iv = (flat(v) for v in (g_tq, g_tk, g_tv, g_iq, g_ik, g_iv))
        text_in = t_sum + project_back(g_tq, text_query) + project_back(g_tk, text_key) + project_back(g_tv, text_value)
        image_in = (
            i_sum + project_back(g_iq, image_query) + project_back(g_ik, image_key) + project_back(g_iv, image_value)
        )
        tl = (t_branch, text_kept[2], t_slow, text_rows)
        tr = (text_kept[4], t_zgrad, flat(text_context), g_tq, g_tk, g_tv)
        il = (i_branch, image_kept[2], i_slow, image_rows)
        ir = (image_kept[4], i_zgrad, flat(image_context), g_iq, g_ik, g_iv)
        wide = max(text_width, image_width)
        small = jnp.stack([jnp.pad(v, (0, wide - v.shape[0])) for v in t_small + i_small])
        me = lax.axis_index("batch") * mesh.shape["heads"] + core

        scatter = lambda v: lax.psum_scatter(v, ("batch", "heads"), scatter_dimension=0, tiled=True)
        text_grads = [scatter(outer_sum(tl[l], r)) for l, r in zip(LEFTS, tr)]
        image_grads = [scatter(outer_sum(il[l], r)) for l, r in zip(LEFTS, ir)]
        total = lax.psum(small, ("batch", "heads"))
        t_own, i_own = text_width // devices, image_width // devices
        t_norm = lax.dynamic_slice(total, (0, me * t_own), (4, t_own))
        i_norm = lax.dynamic_slice(total, (4, me * i_own), (4, i_own))
        return (
            text_result.reshape(text_states.shape),
            image_result.reshape(image_states.shape),
            text_in.astype(BF16).reshape(text_states.shape),
            image_in.astype(BF16).reshape(image_states.shape),
            *parts(text_grads), t_norm[:2], t_norm[2:],
            *parts(image_grads), i_norm[:2], i_norm[2:],
        )

    return local


def solution(mesh):
    rows = P(("batch", "heads"), None, None)
    first, second = P(("batch", "heads"), None), P(None, ("batch", "heads"))
    grads = (first, first, first, second, first, second, second, second)
    return jax.shard_map(
        make_local(mesh),
        mesh=mesh,
        in_specs=(rows, rows, P("batch"), P("batch"), *[P()] * 16, rows, rows),
        out_specs=(rows, rows, rows, rows, *grads, *grads),
        check_vma=False,
    )
```

```python
import functools
import math

import jax
import jax.numpy as jnp
from jax import lax
from jax.experimental import pallas as pl
from jax.experimental.pallas import tpu as pltpu
from jax.sharding import PartitionSpec as P

MESH_ID = pl.DeviceIdType.MESH
F32 = jnp.float32
BF16 = jnp.bfloat16
EPS = 1e-05
NEG = -1000000000.0
HEADS = 8
HEAD = 128
SCALE = 1.0 / math.sqrt(HEAD)
TILE = 256
CW = 256
LEFTS = (0, 1, 2, 3, 3, 3)
NT_DIMS = (((1,), (1,)), ((), ()))
TN_DIMS = (((0,), (0,)), ((), ()))
SLOTS = 6
UNROLL = 2
HEAD_GROUP = 2
G_RING, R_RING, Z_RING = 12, 12, 12
LATE = (0, 6, 9, 10, 13, 15, 16, 19, 20, 22, 23, 24, 25, 26, 27)
PRODUCED = ((1, 0), (1, 1), (1, 2), (0, 0), (0, 1), (0, 2), (1, 3), (0, 4), (0, 5), (0, 3), (1, 4), (1, 5))
SMALL_FROM = 5
STEPS = (
    "i_qkv", "i_attend", "i_out", "i_ffn", "i_norm", "i_slope", "i_branch", "i_context", "t_q", "t_kv", "t_attend",
    "t_out", "t_ffn0", "t_ffn1", "t_ffn2", "t_norm", "t_slope0", "t_slope1", "t_slope2", "t_branch", "i_back",
    "t_context", "t_back", "i_final", "t_final",
)
SEQUENCE = (
    -1, -1, -1, -1, -1, 0, -1, 1, -1, -1, -1, -1, 2, -1, -1, 100, 200, -1, -1, 300, -1, 101, -1, 3, 201, -1, 102, 4,
    -1, 301, -1, 103, 400, 202, 5, -1, 302, 203, 104, 500, 401, 6, 204, 600, 7, 402, 501, 303, -1, 403, 700, 304, 502,
    601, 8, -1, 701, 800, 404, 503, 9, 602, 504, 900, 801, 603, 702, 10, 901, 802, 1000, 703, 604, 11, 803, 902, 704,
    12, 1100, 1001, -1, 903, 1002, 804, 1200, 13, 1101, 1003, 904, 14, 1201, 1300, 1004, 15, 1102, 1301, 1400, 1202,
    1500, -1, 1103, 1600, 1401, 1501, 1203, 1302, 1601, 1303, 1104, 1402, 1204, 1502, 1403, 1304, 1602, 1404, -1,
    1503, 1603, 1504, 1604,
)


def dot(a, b):
    return jnp.dot(a, b, preferred_element_type=F32)


def dot_nt(a, b):
    return lax.dot_general(a, b, NT_DIMS, preferred_element_type=F32)


def dot_tn(a, b):
    return lax.dot_general(a, b, TN_DIMS, preferred_element_type=F32)


def loop(n, body, unroll=None):
    u = min(n, unroll or UNROLL)

    def step(i, carry):
        for k in range(u):
            body(i * u + k)
        return carry

    if n == u:
        step(0, 0)
    else:
        lax.fori_loop(0, n // u, step, 0)
        for k in range(n - n % u, n):
            body(k)


def at(i, size):
    return pl.ds(i * size if isinstance(i, int) else pl.multiple_of(i * size, size), size)


def layer_kernel(dims, *refs):
    nz, ny, nx = dims
    refs = list(refs)

    def take(n):
        got = refs[:n]
        del refs[:n]
        return got

    cap_ref, reg_ref, xt_in, xi_in, ut_in, ui_in = take(6)
    w_in = [take(6), take(6)]
    gain_ref, shift_ref = take(2), take(2)
    res_t, res_i, sg_t, sg_i = take(4)
    w_out = [take(6), take(6)]
    norm_out = take(4)
    wbuf, x_t, x_i = take(3)
    q_b, k_b, v_b = take(2), take(2), take(2)
    n1, inv, low, acc, dctx, sums = take(2), take(2), take(2), take(2), take(2), take(2)
    lt = take(2)
    r_own, r_far = [take(6), take(6)], [take(6), take(6)]
    g_b, r1_b, r2_b, ru_b, rd_b = take(5)
    f_b = take(2)
    small, sv, sr = take(3)
    in_sem, w_sem, ex_s, ex_r, st_s, st_r, sw_s, sw_r, sm_s, sm_r = take(10)
    assert not refs
    u_t, u_i = dctx[0].at[:, pl.ds(0, x_t.shape[1])], dctx[1]

    b, h = lax.axis_index("batch"), lax.axis_index("heads")
    x, y, z = lax.rem(b, nx), lax.rem(lax.div(b, nx), ny), lax.div(b, nx * ny)

    def dev(zz, yy, xx):
        return ((zz * ny + yy) * nx + xx, h)

    partner, nbr_x, nbr_y = (b, 1 - h), dev(z, y, 1 - x), dev(z, 1 - y, x)
    barrier = pltpu.get_barrier_semaphore()
    for who in (partner, nbr_x, nbr_y):
        pl.semaphore_signal(barrier, inc=1, device_id=who, device_id_type=MESH_ID)
    for off in range(1, nz):
        pl.semaphore_signal(barrier, inc=1, device_id=dev(lax.rem(z + off, nz), y, x), device_id_type=MESH_ID)

    def remote(src, dst, ssem, rsem, who):
        return pltpu.make_async_remote_copy(
            src_ref=src, dst_ref=dst, send_sem=ssem, recv_sem=rsem, device_id=who, device_id_type=MESH_ID
        )

    T, I = 0, 1
    pieces = []

    def piece(name, ref, rows, cols):
        pieces.append((name, ref, rows, cols))

    td, ti = x_t.shape[1], x_i.shape[1]
    inner = q_b[0].shape[1]
    parts = w_in[T][1].shape[1] // 1024
    whole = lambda s, w: w_in[s][w]
    tu = lambda j: w_in[T][1].at[:, pl.ds(j * 1024, 1024)]
    tw = lambda j: w_in[T][0].at[pl.ds(j * 1024, 1024), :]
    piece("tk", whole(T, 4), td, inner)
    piece("tv", whole(T, 5), td, inner)
    piece("iq", whole(I, 3), ti, inner)
    piece("io", whole(I, 2), inner, ti)
    piece("iu", whole(I, 1), ti, ti)
    piece("id", whole(I, 0), ti, ti)
    piece("tq", whole(T, 3), td, inner)
    piece("ik", whole(I, 4), ti, inner)
    piece("iv", whole(I, 5), ti, inner)
    piece("to", whole(T, 2), inner, td)
    for j in range(parts):
        piece("tu%d" % j, tu(j), td, 1024)
        piece("td%d" % j, tw(j), 1024, td)
    piece("to", whole(T, 2), inner, td)
    for name, s, w in (("iq", I, 3), ("tk", T, 4), ("tv", T, 5), ("tq", T, 3), ("ik", I, 4), ("iv", I, 5)):
        rows = td if s == T else ti
        piece(name, whole(s, w), rows, inner)
    issued = [0]
    held = {}

    def weight_copy(k, slot):
        name, ref, rows, cols = pieces[k]
        return pltpu.make_async_copy(ref, wbuf.at[slot, pl.ds(0, rows), pl.ds(0, cols)], w_sem.at[slot])

    def issue(slot):
        if issued[0] < len(pieces):
            k = issued[0]
            issued[0] += 1
            weight_copy(k, slot).start()
            assert pieces[k][0] not in held
            held[pieces[k][0]] = [k, slot, False]

    def weight(name):
        k, slot, ready = held[name]
        if not ready:
            weight_copy(k, slot).wait()
            held[name][2] = True
        _, _, rows, cols = pieces[k]
        return wbuf.at[slot, pl.ds(0, rows), pl.ds(0, cols)]

    def release(name):
        k, slot, ready = held.pop(name)
        issue(slot)

    pairs_n, regions = xi_in.shape[:2]
    pad = 112

    def image_rows(src, dst, k):
        return [
            pltpu.make_async_copy(src.at[p], dst.at[pl.ds(p * pad, regions), :], in_sem.at[k + p]) for p in range(pairs_n)
        ]

    def start(copies):
        for c in copies:
            c.start()

    def wait(copies):
        for c in copies:
            c.wait()

    in_copies = [
        [pltpu.make_async_copy(xt_in, x_t, in_sem.at[0])], image_rows(xi_in, x_i, 2),
        [pltpu.make_async_copy(ut_in, u_t, in_sem.at[1])], image_rows(ui_in, u_i, 2 + pairs_n),
    ]
    start(in_copies[0])
    issue(0)
    start(in_copies[1])
    issue(1)
    issue(2)
    start(in_copies[3])
    start(in_copies[2])
    for slot in range(3, SLOTS):
        issue(slot)

    cap = x_t.shape[0] // pairs_n
    m_i, m_t = pairs_n * pad, x_t.shape[0]
    m_of, d_of = (m_t, m_i), (td, ti)
    x_of = (x_t, x_i)

    tail = pl.ds(m_i, x_i.shape[0] - m_i)
    for ref in (x_i, low[I], *r_own[I]):
        ref[tail, :] = jnp.zeros((x_i.shape[0] - m_i, ref.shape[1]), BF16)
    for ref in (*sums,):
        ref[...] = jnp.zeros(ref.shape, F32)

    for ref in (x_i, u_i):
        for p in range(pairs_n):
            ref[pl.ds(p * pad + regions, pad - regions), :] = jnp.zeros((pad - regions, ref.shape[1]), BF16)

    lengths = {
        T: [reg_ref[h * pairs_n + p] for p in range(pairs_n)],
        I: [cap_ref[h * pairs_n + p] for p in range(pairs_n)],
    }

    ex_left, ex_right = {}, {}
    n_left = max(LEFTS) + 1
    for s in (T, I):
        for l in range(n_left):
            k = s * n_left + l
            ex_left[s, l] = remote(
                lt[s].at[l, :, pl.ds(0, 256)], lt[s].at[l, :, pl.ds(256, 256)], ex_s.at[k], ex_r.at[k], partner
            )
        for w in range(6):
            k = 2 * n_left + s * 6 + w
            half = r_far[s][w].shape[1]
            ex_right[s, w] = remote(
                r_own[s][w].at[:, pl.ds(pl.multiple_of((1 - h) * half, 128), half)], r_far[s][w],
                ex_s.at[k], ex_r.at[k], partner,
            )
    arrived = set()
    entered = []

    def enter():
        if not entered:
            entered.append(1)
            pl.semaphore_wait(barrier, 3 + nz - 1)

    def send_left(s, l, src):
        def body(j):
            lt[s][l, at(j, TILE), pl.ds(0, 256)] = src[:, at(j, TILE)].T

        loop(d_of[s] // TILE, body)
        enter()
        ex_left[s, l].start()

    def send_right(s, w):
        enter()
        ex_right[s, w].start()

    def project(src, rows, w, dst):
        def body(j):
            dst[pl.ds(0, rows), at(j, TILE)] = dot(src[pl.ds(0, rows), :], w[:, at(j, TILE)]).astype(BF16)

        loop(w.shape[1] // TILE, body)

    def softmaxes(parts_of):
        scores = [dot_nt(q, k) * SCALE for q, k, _ in parts_of]
        scores = [
            jnp.where(lax.broadcasted_iota(jnp.int32, v.shape, 1) < live, v, NEG)
            for v, (_, _, live) in zip(scores, parts_of)
        ]
        tops = [jnp.max(v, axis=-1, keepdims=True) for v in scores]
        exps = [jnp.exp(v - t) for v, t in zip(scores, tops)]
        totals = [jnp.sum(e, axis=-1, keepdims=True) for e in exps]
        return [e / t for e, t in zip(exps, totals)]

    span = (cap, pad)

    def rows_of(s, p):
        return pl.ds(p * span[s], span[s])

    def units(i):
        return [(at(i * HEAD_GROUP + k, HEAD), p) for k in range(HEAD_GROUP) for p in range(pairs_n)]

    def attend(s):
        o = 1 - s

        def body(i):
            group = units(i)
            probs = softmaxes(
                [(q_b[s][rows_of(s, p), c], k_b[o][rows_of(o, p), c], lengths[s][p]) for c, p in group]
            )
            got = [dot(prob.astype(BF16), v_b[o][rows_of(o, p), c]) for prob, (c, p) in zip(probs, group)]
            for g, (c, p) in zip(got, group):
                r_own[s][2][rows_of(s, p), c] = g.astype(BF16)

        loop(HEADS // HEAD_GROUP, body, 1)
        send_right(s, 2)

    def attend_back(s):
        o = 1 - s

        def body(i):
            group = units(i)
            qs = [q_b[s][rows_of(s, p), c] for c, p in group]
            ks = [k_b[o][rows_of(o, p), c] for c, p in group]
            dcs = [dctx[s][rows_of(s, p), c] for c, p in group]
            dps = [dot_nt(dc, v_b[o][rows_of(o, p), c]) for dc, (c, p) in zip(dcs, group)]
            probs = softmaxes([(q, k, lengths[s][p]) for q, k, (_, p) in zip(qs, ks, group)])
            dvs = [dot_tn(prob.astype(BF16), dc) for prob, dc in zip(probs, dcs)]
            inner_sums = [jnp.sum(prob * dp, axis=-1, keepdims=True) for prob, dp in zip(probs, dps)]
            dss = [(prob * (dp - t)).astype(BF16) for prob, dp, t in zip(probs, dps, inner_sums)]
            dqs = [dot(ds, k) * SCALE for ds, k in zip(dss, ks)]
            dks = [dot_tn(ds, q) * SCALE for ds, q in zip(dss, qs)]
            for (c, p), dq, dk, dv in zip(group, dqs, dks, dvs):
                rq, rk = rows_of(s, p), rows_of(o, p)
                r_own[s][3][rq, c] = dq.astype(BF16)
                r_own[o][4][rk, c] = dk.astype(BF16)
                r_own[o][5][rk, c] = dv.astype(BF16)

        loop(HEADS // HEAD_GROUP, body, 1)
        send_right(s, 3)
        send_right(o, 4)
        send_right(o, 5)

    RB = 32

    def mean(v):
        return jnp.mean(v, axis=-1, keepdims=True)

    def sum8(v):
        return jnp.sum(v.reshape(v.shape[0] // 8, 8, v.shape[1]), axis=0)

    def norm_one(s):
        gain, shift = gain_ref[s][0:1, :], shift_ref[s][0:1, :]

        def body(i):
            r = at(i, RB)
            v = x_of[s][r, :].astype(F32) + acc[s][r, :]
            c = v - mean(v)
            iv = lax.rsqrt(mean(c * c) + EPS)
            n = c * iv
            n1[s][r, :] = n
            inv[s][r, :] = jnp.broadcast_to(iv, (RB, 128))
            low[s][r, :] = (n * gain + shift).astype(BF16)

        loop(m_of[s] // RB, body)
        send_left(s, 1, low[s])

    def norm_two(s, up_ref, res_ref):
        gain0, shift0 = gain_ref[s][0:1, :], shift_ref[s][0:1, :]
        gain, shift = gain_ref[s][1:2, :], shift_ref[s][1:2, :]

        def body(i):
            r = at(i, RB)
            v = n1[s][r, :] * gain0 + shift0 + acc[s][r, :]
            c = v - mean(v)
            iv = lax.rsqrt(mean(c * c) + EPS)
            n = c * iv
            up = up_ref[r, :].astype(F32)
            res_ref[r, :] = (n * gain + shift).astype(BF16)
            un = up * n
            sums[s][1] = sums[s][1] + sum8(un)
            sums[s][3] = sums[s][3] + sum8(up)
            u = up * gain
            d = iv * (u - mean(u) - n * mean(un * gain))
            acc[s][r, :] = d
            low[s][r, :] = d.astype(BF16)

        loop(m_of[s] // RB, body)
        send_left(s, 0, low[s])

    def norm_one_back(s):
        gain = gain_ref[s][0:1, :]

        def body(i):
            r = at(i, RB)
            g, n = acc[s][r, :], n1[s][r, :]
            gn = g * n
            sums[s][0] = sums[s][0] + sum8(gn)
            sums[s][2] = sums[s][2] + sum8(g)
            u = g * gain
            d = inv[s][r, 0:1] * (u - mean(u) - n * mean(gn * gain))
            acc[s][r, :] = d
            low[s][r, :] = d.astype(BF16)

        loop(m_of[s] // RB, body)
        send_left(s, 2, low[s])

    def out_project(s, w):
        m = m_of[s]

        def body(j):
            acc[s][pl.ds(0, m), at(j, TILE)] = dot(r_own[s][2][pl.ds(0, m), :], w[:, at(j, TILE)])

        loop(d_of[s] // TILE, body)

    def ffn(s, j, up_w, down_w):
        m, base = m_of[s], j * 1024

        def hidden(i):
            c = pl.ds(pl.multiple_of(base + i * TILE, TILE), TILE)
            v = dot(low[s][pl.ds(0, m), :], up_w[:, at(i, TILE)])
            half = 0.5 * (1.0 + lax.erf(v * (1.0 / math.sqrt(2.0))))
            r_own[s][0][pl.ds(0, m), c] = (v * half).astype(BF16)
            r_own[s][1][pl.ds(0, m), c] = (half + v * jnp.exp(-0.5 * v * v) * (1.0 / math.sqrt(2.0 * math.pi))).astype(BF16)

        loop(1024 // TILE, hidden)

        def second(i):
            part = dot(r_own[s][0][pl.ds(0, m), pl.ds(base, 1024)], down_w[:, at(i, TILE)])
            if j == 0:
                acc[s][pl.ds(0, m), at(i, TILE)] = part
            else:
                acc[s][pl.ds(0, m), at(i, TILE)] += part

        loop(d_of[s] // TILE, second)

    def slope_back(s, j, down_w):
        m, base = m_of[s], j * 1024

        def body(i):
            c = pl.ds(pl.multiple_of(base + i * TILE, TILE), TILE)
            g = dot_nt(low[s][pl.ds(0, m), :], down_w[at(i, TILE), :])
            r_own[s][1][pl.ds(0, m), c] = (g * r_own[s][1][pl.ds(0, m), c].astype(F32)).astype(BF16)

        loop(1024 // TILE, body)

    def back_add(s, src, cols, w):
        m = m_of[s]

        def body(i):
            acc[s][pl.ds(0, m), at(i, TILE)] += dot_nt(src[pl.ds(0, m), cols], w[at(i, TILE), :])

        loop(d_of[s] // TILE, body)

    def context_back(s, w):
        m = m_of[s]

        def body(i):
            dctx[s][pl.ds(0, m), at(i, TILE)] = dot_nt(low[s][pl.ds(0, m), :], w[at(i, TILE), :]).astype(BF16)

        loop(inner // TILE, body)

    def final(s, dst):
        def body(i):
            dst[at(i, RB), :] = acc[s][at(i, RB), :].astype(BF16)

        loop(m_of[s] // RB, body)

    def gather_rows(src, dst):
        for p in range(pairs_n):
            dst[p] = src[pl.ds(p * pad, regions), :]

    all_cols = pl.ds(0, 1024)

    def step(name):
        if name == "i_qkv":
            wait(in_copies[0])
            project(x_t, m_t, weight("tk"), k_b[T])
            release("tk")
            project(x_t, m_t, weight("tv"), v_b[T])
            release("tv")
            wait(in_copies[1])
            project(x_i, m_i, weight("iq"), q_b[I])
            release("iq")
        elif name == "i_attend":
            attend(I)
        elif name == "i_out":
            out_project(I, weight("io"))
            norm_one(I)
        elif name == "i_ffn":
            ffn(I, 0, weight("iu"), weight("id"))
            send_right(I, 0)
        elif name == "i_norm":
            wait(in_copies[3])
            norm_two(I, u_i, u_i)
            gather_rows(u_i, res_i)
        elif name == "i_slope":
            slope_back(I, 0, weight("id"))
            send_right(I, 1)
            release("id")
        elif name == "i_branch":
            back_add(I, r_own[I][1], all_cols, weight("iu"))
            release("iu")
            norm_one_back(I)
        elif name == "i_context":
            context_back(I, weight("io"))
            release("io")
            send_left(I, 3, x_i)
        elif name == "t_q":
            project(x_t, m_t, weight("tq"), q_b[T])
            release("tq")
            send_left(T, 3, x_t)
        elif name == "t_kv":
            project(x_i, m_i, weight("ik"), k_b[I])
            release("ik")
            project(x_i, m_i, weight("iv"), v_b[I])
            release("iv")
        elif name == "t_attend":
            attend(T)
        elif name == "t_out":
            out_project(T, weight("to"))
            release("to")
            norm_one(T)
        elif name.startswith("t_ffn"):
            j = int(name[-1])
            ffn(T, j, weight("tu%d" % j), weight("td%d" % j))
            if j == parts - 1:
                send_right(T, 0)
        elif name == "t_norm":
            wait(in_copies[2])
            norm_two(T, u_t, res_t)
        elif name.startswith("t_slope"):
            j = int(name[-1])
            slope_back(T, j, weight("td%d" % j))
            release("td%d" % j)
            if j == parts - 1:
                send_right(T, 1)
        elif name == "t_branch":
            for j in range(parts):
                back_add(T, r_own[T][1], pl.ds(j * 1024, 1024), weight("tu%d" % j))
                release("tu%d" % j)
            norm_one_back(T)
            small_fill()
        elif name == "t_context":
            context_back(T, weight("to"))
            release("to")
        elif name == "i_back":
            attend_back(I)
            back_add(I, r_own[I][3], all_cols, weight("iq"))
            release("iq")
            back_add(T, r_own[T][4], all_cols, weight("tk"))
            release("tk")
            back_add(T, r_own[T][5], all_cols, weight("tv"))
            release("tv")
        elif name == "t_back":
            attend_back(T)
        elif name == "i_final":
            back_add(I, r_own[I][4], all_cols, weight("ik"))
            release("ik")
            back_add(I, r_own[I][5], all_cols, weight("iv"))
            release("iv")
            final(I, u_i)
            gather_rows(u_i, sg_i)
        elif name == "t_final":
            back_add(T, r_own[T][3], all_cols, weight("tq"))
            release("tq")
            final(T, sg_t)

    def token(k):
        if k < 100:
            for c in (2 * k, 2 * k + 1):
                compute(c)
                s1(c).start()
            return
        p, lag = k // 100 - 1, k % 100
        stage(p, lag)
        if lag == nz and SMALL_FROM <= p < SMALL_FROM + 5:
            small_step(p - SMALL_FROM)

    small_copies = []

    def small_start(src, dst, i, who):
        c = remote(src, dst, sm_s.at[i], sm_r.at[i], who)
        c.start()
        small_copies.append(c)

    def small_fill():
        small[...] = jnp.zeros(small.shape, F32)
        for s in (T, I):
            for k in range(4):
                small[pl.ds(4 * s + k, 1), pl.ds(0, d_of[s])] = jnp.sum(sums[s][k], axis=0, keepdims=True)

    def small_step(i):
        if i == 0:
            small_start(small, sr.at[0], 0, partner)
        elif i == 1:
            small_copies[0].wait_recv()
            sv[0] = small[...] + sr[0]
            small_start(sv.at[0], sr.at[1], 1, nbr_x)
        elif i == 2:
            small_copies[1].wait_recv()
            sv[1] = sv[0] + sr[1]
            small_start(sv.at[1], sr.at[2], 2, nbr_y)
        elif i == 3:
            small_copies[2].wait_recv()
            sv[2] = sv[1] + sr[2]
            for off in range(1, nz):
                small_start(sv.at[2], sr.at[2 + off], 2 + off, dev(lax.rem(z + off, nz), y, x))
        elif i == 4:
            total = sv[2]
            for off in range(1, nz):
                small_copies[2 + off].wait_recv()
                total = total + sr[2 + off]
            wide = total.shape[1]
            me = b * 2 + h
            for s in (T, I):
                own = norm_out[2 * s].shape[1]
                mine = pltpu.roll(total, lax.rem(wide - me * own, wide), 1)
                norm_out[2 * s][...] = mine[4 * s : 4 * s + 2, :own]
                norm_out[2 * s + 1][...] = mine[4 * s + 2 : 4 * s + 4, :own]

    chunks = []
    for s, w in PRODUCED:
        for o in range(0, r_far[s][w].shape[1], CW):
            late = len(chunks) in LATE
            chunks.append((s, w, o, "xy"[len(chunks) % 2], len([1 for c in chunks if c[0] == s]), late))
    n = len(chunks)

    def bufs(c):
        rows = pl.ds(0, d_of[chunks[c][0]] // (nz * ny * nx))
        return (
            g_b.at[c % G_RING, :, :, :, rows], r1_b.at[c % R_RING, :, :, rows], r2_b.at[c % R_RING, :, rows],
            ru_b.at[c % Z_RING, :, :, rows], rd_b.at[c % Z_RING, :, :, rows],
        )

    def compute(c):
        s, w, o, way, _, _ = chunks[c]
        for copy, key in ((ex_left[s, LEFTS[w]], (0, s, LEFTS[w])), (ex_right[s, w], (1, s, w))):
            if key not in arrived:
                arrived.add(key)
                copy.wait_recv()
        blk = d_of[s] // (nz * ny * nx)
        size = ny * nx * blk
        half = r_far[s][w].shape[1]
        mine = pl.ds(pl.multiple_of(h * half + o, 128), CW)
        g = g_b.at[c % G_RING]

        def body(i):
            r = pl.ds(pl.multiple_of(i * size, 64), size)
            l = LEFTS[w]
            res = dot(lt[s][l, r, pl.ds(0, 256)], r_own[s][w][:, mine]) + dot(
                lt[s][l, r, pl.ds(256, 256)], r_far[s][w][:, pl.ds(o, CW)]
            )
            g[i, :, :, pl.ds(0, blk)] = res.astype(BF16).reshape(ny, nx, blk, CW)

        loop(nz, body)

    def add(dst, src):
        dst[...] = (dst[...].astype(F32) + src[...].astype(F32)).astype(BF16)

    def s1(c):
        g, r1 = bufs(c)[:2]
        if chunks[c][3] == "x":
            return remote(g.at[:, :, 1 - x], r1, st_s.at[0, c % G_RING], st_r.at[0, c % G_RING], nbr_x)
        return remote(g.at[:, 1 - y], r1, st_s.at[0, c % G_RING], st_r.at[0, c % G_RING], nbr_y)

    def s2(c):
        g, _, r2 = bufs(c)[:3]
        first, late = chunks[c][3] == "x", chunks[c][5]
        far = (1 - y, x) if first else (y, 1 - x)
        src, dst = (g.at[z, far[0], far[1]], r2.at[0]) if late else (g.at[:, far[0], far[1]], r2)
        return remote(src, dst, st_s.at[1, c % G_RING], st_r.at[1, c % G_RING], nbr_y if first else nbr_x)

    def blocks(c, t):
        g, _, _, ru, rd = bufs(c)
        if not chunks[c][5]:
            return [(g.at[t, y, x], ru.at[t, 0], rd.at[t, 0])]
        here = (lambda j: g.at[t, j, x]) if chunks[c][3] == "x" else (lambda j: g.at[t, y, j])
        return [(here(j), ru.at[t, j], rd.at[t, j]) for j in range(2)]

    def along(c, rest, buf):
        g = bufs(c)[0]
        if not chunks[c][5]:
            return g.at[rest, y, x], buf.at[rest, 0]
        return (g.at[rest, :, x] if chunks[c][3] == "x" else g.at[rest, y]), buf.at[rest]

    def up(c, k):
        src, dst = along(c, pl.ds(k + 1, nz - 1 - k), bufs(c)[3])
        return remote(src, dst, st_s.at[2, c % G_RING], st_r.at[2, c % G_RING], dev(k + 1, y, x))

    def down(c, k):
        src, dst = along(c, pl.ds(0, k), bufs(c)[4])
        return remote(src, dst, st_s.at[3, c % G_RING], st_r.at[3, c % G_RING], dev(k - 1, y, x))

    def swap(c):
        s, w, o, _, k, _ = chunks[c]
        out = w_out[s][w]
        half = out.shape[1] // 2
        return remote(
            f_b[s].at[k], out.at[:, pl.ds(pl.multiple_of(h * half + o, 128), CW)],
            sw_s.at[c], sw_r.at[c], partner,
        )

    def ends(c):
        @pl.when(z == 0)
        def _():
            up(c, 0).start()

        @pl.when(z == nz - 1)
        def _():
            down(c, nz - 1).start()

    def stage2(pair):
        for c in pair:
            s1(c).wait_recv()
        for c in pair:
            g, r1 = bufs(c)[:2]

            def body(i):
                for j in range(2):
                    add(g.at[i, j, x] if chunks[c][3] == "x" else g.at[i, y, j], r1.at[i, j])

            loop(nz, body)
            if chunks[c][5]:
                ends(c)
            else:
                s2(c).start()

    def stage3(pair):
        for c in pair:
            s2(c).wait_recv()
        for c in pair:
            g, _, r2 = bufs(c)[:3]
            loop(nz, lambda i: add(g.at[i, y, x], r2.at[i]))
            ends(c)

    def hop(pair, d):
        for c in pair:

            @pl.when(z == d)
            def _(c=c):
                up(c, d - 1).wait_recv()
                for t in range(d + 1, nz):
                    for here, below, _ in blocks(c, t):
                        add(here, below)
                up(c, d).start()

            @pl.when(z == nz - 1 - d)
            def _(c=c):
                down(c, nz - d).wait_recv()
                for t in range(0, nz - 1 - d):
                    for here, _, above in blocks(c, t):
                        add(here, above)
                down(c, nz - 1 - d).start()

    def last_hops(c, k):
        if k == nz - 1:
            up(c, k - 1).wait_recv()
        if k == 0:
            down(c, 1).wait_recv()

    def z_total(c, k, j):
        g, _, _, ru, rd = bufs(c)
        late, first = chunks[c][5], chunks[c][3] == "x"
        lane = j if late else 0
        row, col = (j, x) if late and first else (y, j) if late else (y, x)
        total = g[k, row, col].astype(F32)
        if k > 0:
            total = total + ru[k, lane].astype(F32)
        if k < nz - 1:
            total = total + rd[k, lane].astype(F32)
        return total

    def fold(pair):
        for c in pair:
            far = 1 - y if chunks[c][3] == "x" else 1 - x
            for k in range(nz):

                @pl.when(z == k)
                def _(c=c, k=k, far=far):
                    last_hops(c, k)
                    got = z_total(c, k, far).astype(BF16)
                    g = bufs(c)[0]
                    if chunks[c][3] == "x":
                        g[k, far, x] = got
                    else:
                        g[k, y, far] = got

            s2(c).start()

    def finish(pair):
        for c in pair:
            s, w, o, way, idx, late = chunks[c]
            out = w_out[s][w]
            r, half = out.shape[0], out.shape[1] // 2
            cols = pl.ds(pl.multiple_of(h * half + o, 128), CW)
            if late:
                s2(c).wait_recv()
            for k in range(nz):

                @pl.when(z == k)
                def _(k=k):
                    if not late:
                        last_hops(c, k)
                    total = z_total(c, k, y if way == "x" else x)
                    if late:
                        total = total + bufs(c)[2][0].astype(F32)
                    first, second = total[:r], total[r:]
                    out[:, cols] = jnp.where(h == 0, first, second)
                    f_b[s][idx] = jnp.where(h == 0, second, first)

            swap(c).start()
            s1(c).wait_send()
            s2(c).wait_send()
            for k in range(nz):

                @pl.when(z == k)
                def _(k=k):
                    if k < nz - 1:
                        up(c, k).wait_send()
                    if k > 0:
                        down(c, k).wait_send()


    def stage(p, lag):
        pair = (2 * p, 2 * p + 1)
        if lag == 0:
            return stage2(pair)
        if lag == nz:
            return finish(pair)
        for late in (True, False):
            part = [c for c in pair if chunks[c][5] == late]
            if late and lag == nz - 1:
                fold(part)
            elif not late and lag == 1:
                stage3(part)
            else:
                hop(part, lag if late else lag - 1)

    names = iter(STEPS)
    for k in SEQUENCE:
        if k < 0:
            step(next(names))
        else:
            token(k)

    for c in range(n):
        swap(c).wait_recv()
        swap(c).wait_send()
    for copy in (*ex_left.values(), *ex_right.values()):
        copy.wait_send()
    for copy in small_copies:
        copy.wait_send()


def hand_over(*refs):
    n = len(refs) // 2
    copies = [pltpu.make_async_copy(refs[i], refs[n + i], refs[-1].at[i]) for i in range(n)]
    for c in copies:
        c.start()
    for c in copies:
        c.wait()


def layer(dims, lengths, states, upstream, weights, gains, shifts):
    nz, ny, nx = dims
    chips = nz * ny * nx
    xt, xi = states
    pairs, cap, td = xt.shape
    regions, ti = xi.shape[1:]
    xt, ut = xt.reshape(pairs * cap, td), upstream[0].reshape(pairs * cap, td)
    mt = pairs * cap
    fixed = 256
    inner = weights[0][3].shape[1]
    d_of = (td, ti)
    cols = [[w.shape[0], weights[s][1].shape[1], inner, inner, inner, inner] for s, w in ((0, weights[0][0]), (1, weights[1][0]))]
    V, DMA = pltpu.VMEM, pltpu.SemaphoreType.DMA
    rows_of = (mt, fixed)
    ti_blk = ti // chips
    counts = [sum(c // 2 // CW for c in cols[s]) for s in range(2)]
    n = sum(counts)
    act = lambda dt, width: [V((rows_of[s], width[s]), dt) for s in range(2)]
    scratch = [
        V((SLOTS, 1024, 1024), BF16),
        V((mt, td), BF16), V((fixed, ti), BF16),
        *act(BF16, (inner, inner)), *act(BF16, (inner, inner)), *act(BF16, (inner, inner)),
        *act(F32, d_of), *act(F32, (128, 128)), *act(BF16, d_of),
        *act(F32, d_of), *act(BF16, (inner, inner)),
        *[V((4, 8, d), F32) for d in d_of],
        *[V((4, d, 512), BF16) for d in d_of],
        *[V((rows_of[s], c), BF16) for s in range(2) for c in cols[s]],
        *[V((rows_of[s], c // 2), BF16) for s in range(2) for c in cols[s]],
        V((G_RING, nz, ny, nx, ti_blk, CW), BF16),
        V((R_RING, nz, 2, ti_blk, CW), BF16),
        V((R_RING, nz, ti_blk, CW), BF16),
        V((Z_RING, nz, 2, ti_blk, CW), BF16),
        V((Z_RING, nz, 2, ti_blk, CW), BF16),
        *[V((counts[s], d_of[s] // chips // 2, CW), F32) for s in range(2)],
        V((8, max(d_of)), F32), V((3, 8, max(d_of)), F32), V((2 + nz, 8, max(d_of)), F32),
        DMA((2 + 2 * pairs,)), DMA((SLOTS,)), DMA((20,)), DMA((20,)), DMA((4, G_RING)), DMA((4, G_RING)), DMA((n,)), DMA((n,)), DMA((2 + nz,)), DMA((2 + nz,)),
    ]
    hbm = pl.BlockSpec(memory_space=pl.ANY)
    vm = pl.BlockSpec(memory_space=pltpu.VMEM)
    smem = pl.BlockSpec(memory_space=pltpu.SMEM)
    sds = jax.ShapeDtypeStruct
    outs = [
        sds((mt, td), BF16), sds((pairs, regions, ti), BF16), sds((mt, td), BF16), sds((pairs, regions, ti), BF16),
        *[sds((d_of[s] // chips // 2, c), F32) for s in range(2) for c in cols[s]],
        *[sds((2, d_of[s] // chips // 2), F32) for s in range(2) for _ in range(2)],
    ]
    got = pl.pallas_call(
        functools.partial(layer_kernel, dims),
        out_shape=outs,
        in_specs=[smem, smem, *[hbm] * 4, *[hbm] * 12, *[vm] * 4],
        out_specs=[vm] * len(outs),
        scratch_shapes=scratch,
        compiler_params=pltpu.CompilerParams(
            collective_id=0, has_side_effects=True, vmem_limit_bytes=67043328
        ),
        name="co_layer",
    )(*lengths, xt, xi, ut, upstream[1], *weights[0], *weights[1], *gains, *shifts)
    n = len(got)
    return pl.pallas_call(
        hand_over,
        out_shape=outs,
        in_specs=[vm] * n,
        out_specs=[hbm] * n,
        scratch_shapes=[DMA((n,))],
        name="hand_over",
    )(*got)


def matmul(row_values, weight):
    return jnp.dot(row_values, weight, preferred_element_type=F32)


def project_back(gradient, weight):
    return lax.dot_general(gradient, weight, (((1,), (1,)), ((), ())), preferred_element_type=F32)


def outer_sum(row_values, gradient):
    return lax.dot_general(row_values, gradient, (((0,), (0,)), ((), ())), preferred_element_type=F32)


def layer_norm(values, gain, shift):
    row_mean = jnp.mean(values, axis=-1, keepdims=True)
    centred = values - row_mean
    spread = jnp.mean(centred * centred, axis=-1, keepdims=True)
    inverse = lax.rsqrt(spread + EPS)
    normed = centred * inverse
    return (normed * gain + shift, normed, inverse)


def norm_back(gradient, normed, inverse, gain):
    scaled = gradient * gain
    first_mean = jnp.mean(scaled, axis=-1, keepdims=True)
    second_mean = jnp.mean(scaled * normed, axis=-1, keepdims=True)
    into = inverse * (scaled - first_mean - normed * second_mean)
    return (into, jnp.sum(gradient * normed, axis=0), jnp.sum(gradient, axis=0))


def gelu_value(values):
    return 0.5 * values * (1.0 + jax.scipy.special.erf(values / math.sqrt(2.0)))


def gelu_slope(values):
    return 0.5 * (1.0 + jax.scipy.special.erf(values / math.sqrt(2.0))) + values * jnp.exp(
        -0.5 * values * values
    ) / math.sqrt(2.0 * math.pi)


def attend(queries, key_rows, value_rows, lengths):
    score_scale = 1.0 / math.sqrt(queries.shape[-1])
    scores = jnp.einsum("bqhd,bkhd->bhqk", queries, key_rows, preferred_element_type=F32) * score_scale
    live_mask = lax.broadcasted_iota(jnp.int32, scores.shape, 3) < lengths[:, None, None, None]
    scores = jnp.where(live_mask, scores, NEG)
    weights = jnp.exp(scores - jnp.max(scores, axis=-1, keepdims=True))
    probability = weights / jnp.sum(weights, axis=-1, keepdims=True)
    context = jnp.einsum("bhqk,bkhd->bqhd", probability.astype(BF16), value_rows, preferred_element_type=F32)
    return context.astype(BF16), probability


def attend_back(queries, key_rows, value_rows, probability, context_grad):
    score_scale = 1.0 / math.sqrt(queries.shape[-1])
    value_grad = jnp.einsum(
        "bhqk,bqhd->bkhd", probability.astype(BF16), context_grad, preferred_element_type=F32
    )
    prob_grad = jnp.einsum("bqhd,bkhd->bhqk", context_grad, value_rows, preferred_element_type=F32)
    row_inner = jnp.sum(probability * prob_grad, axis=-1, keepdims=True)
    score_grad = (probability * (prob_grad - row_inner)).astype(BF16)
    query_grad = jnp.einsum("bhqk,bkhd->bqhd", score_grad, key_rows, preferred_element_type=F32) * score_scale
    key_grad = jnp.einsum("bhqk,bqhd->bkhd", score_grad, queries, preferred_element_type=F32) * score_scale
    return (query_grad.astype(BF16), key_grad.astype(BF16), value_grad.astype(BF16))


def stream_forward(row_values, context, out_weight, up_weight, down_weight, gains, shifts):
    attended = matmul(context, out_weight)
    first_out, normed_one, inverse_one = layer_norm(row_values.astype(F32) + attended, gains[0], shifts[0])
    first_low = first_out.astype(BF16)
    before = matmul(first_low, up_weight)
    active = gelu_value(before).astype(BF16)
    second_out, normed_two, inverse_two = layer_norm(
        first_out + matmul(active, down_weight), gains[1], shifts[1]
    )
    kept_state = (normed_one, inverse_one, first_low, before, active, normed_two, inverse_two)
    return (second_out.astype(BF16), kept_state)


def stream_back(upstream, kept_state, out_weight, up_weight, down_weight, gains):
    normed_one, inverse_one, first_low, before, active, normed_two, inverse_two = kept_state
    branch_grad, gain_two, shift_two = norm_back(upstream.astype(F32), normed_two, inverse_two, gains[1])
    branch_low = branch_grad.astype(BF16)
    active_grad = project_back(branch_low, down_weight)
    before_grad = (active_grad * gelu_slope(before)).astype(BF16)
    first_grad = project_back(before_grad, up_weight) + branch_grad
    sum_grad, gain_one, shift_one = norm_back(first_grad, normed_one, inverse_one, gains[0])
    sum_low = sum_grad.astype(BF16)
    context_grad = project_back(sum_low, out_weight).astype(BF16)
    return sum_grad, context_grad, branch_low, before_grad, sum_low, (gain_one, gain_two, shift_one, shift_two)


def make_local(mesh):
    devices = mesh.shape["batch"] * mesh.shape["heads"]

    def local(
        text_states, image_states, caption_lengths, region_counts,
        text_query, text_key, text_value, text_output, text_up, text_down, text_gains, text_shifts,
        image_query, image_key, image_value, image_output, image_up, image_down, image_gains, image_shifts,
        text_upstream, image_upstream,
    ):
        def parts(grads):
            down, up, out, query, key, value = grads
            return query, key, value, out.T, up, down.T

        if mesh.shape["batch"] == 16 and mesh.shape["heads"] == 2:
            text_weights = (text_down, text_up, text_output, text_query, text_key, text_value)
            image_weights = (image_down, image_up, image_output, image_query, image_key, image_value)
            got = layer(
                (4, 2, 2), (caption_lengths, region_counts), (text_states, image_states), (text_upstream, image_upstream),
                (text_weights, image_weights), (text_gains, image_gains), (text_shifts, image_shifts),
            )
            return (
                got[0].reshape(text_states.shape), got[1], got[2].reshape(text_states.shape), got[3],
                *parts(got[4:10]), got[16], got[17], *parts(got[10:16]), got[18], got[19],
            )
        pair_count, cap_len, text_width = text_states.shape
        region_len, image_width = image_states.shape[1:]
        text_rows = text_states.reshape(pair_count * cap_len, text_width)
        image_rows = image_states.reshape(pair_count * region_len, image_width)
        core = lax.axis_index("heads")
        captions = lax.dynamic_slice(caption_lengths, (core * pair_count,), (pair_count,))
        regions = lax.dynamic_slice(region_counts, (core * pair_count,), (pair_count,))

        def heads_of(row_values, weight, length):
            return matmul(row_values, weight).astype(BF16).reshape(pair_count, length, HEADS, HEAD)

        tq, tk, tv = (heads_of(text_rows, w, cap_len) for w in (text_query, text_key, text_value))
        iq, ik, iv = (heads_of(image_rows, w, region_len) for w in (image_query, image_key, image_value))
        text_context, text_prob = attend(tq, ik, iv, regions)
        image_context, image_prob = attend(iq, tk, tv, captions)
        flat = lambda v: v.reshape(v.shape[0] * v.shape[1], -1)
        text_result, text_kept = stream_forward(
            text_rows, flat(text_context), text_output, text_up, text_down, text_gains, text_shifts
        )
        image_result, image_kept = stream_forward(
            image_rows, flat(image_context), image_output, image_up, image_down, image_gains, image_shifts
        )
        t_sum, t_cgrad, t_branch, t_zgrad, t_slow, t_small = stream_back(
            text_upstream.reshape(text_rows.shape), text_kept, text_output, text_up, text_down, text_gains
        )
        i_sum, i_cgrad, i_branch, i_zgrad, i_slow, i_small = stream_back(
            image_upstream.reshape(image_rows.shape), image_kept, image_output, image_up, image_down, image_gains
        )
        g_tq, g_ik, g_iv = attend_back(tq, ik, iv, text_prob, t_cgrad.reshape(tq.shape))
        g_iq, g_tk, g_tv = attend_back(iq, tk, tv, image_prob, i_cgrad.reshape(iq.shape))
        g_tq, g_tk, g_tv, g_iq, g_ik, g_iv = (flat(v) for v in (g_tq, g_tk, g_tv, g_iq, g_ik, g_iv))
        text_in = t_sum + project_back(g_tq, text_query) + project_back(g_tk, text_key) + project_back(g_tv, text_value)
        image_in = (
            i_sum + project_back(g_iq, image_query) + project_back(g_ik, image_key) + project_back(g_iv, image_value)
        )
        tl = (t_branch, text_kept[2], t_slow, text_rows)
        tr = (text_kept[4], t_zgrad, flat(text_context), g_tq, g_tk, g_tv)
        il = (i_branch, image_kept[2], i_slow, image_rows)
        ir = (image_kept[4], i_zgrad, flat(image_context), g_iq, g_ik, g_iv)
        wide = max(text_width, image_width)
        small = jnp.stack([jnp.pad(v, (0, wide - v.shape[0])) for v in t_small + i_small])
        me = lax.axis_index("batch") * mesh.shape["heads"] + core

        scatter = lambda v: lax.psum_scatter(v, ("batch", "heads"), scatter_dimension=0, tiled=True)
        text_grads = [scatter(outer_sum(tl[l], r)) for l, r in zip(LEFTS, tr)]
        image_grads = [scatter(outer_sum(il[l], r)) for l, r in zip(LEFTS, ir)]
        total = lax.psum(small, ("batch", "heads"))
        t_own, i_own = text_width // devices, image_width // devices
        t_norm = lax.dynamic_slice(total, (0, me * t_own), (4, t_own))
        i_norm = lax.dynamic_slice(total, (4, me * i_own), (4, i_own))
        return (
            text_result.reshape(text_states.shape),
            image_result.reshape(image_states.shape),
            text_in.astype(BF16).reshape(text_states.shape),
            image_in.astype(BF16).reshape(image_states.shape),
            *parts(text_grads), t_norm[:2], t_norm[2:],
            *parts(image_grads), i_norm[:2], i_norm[2:],
        )

    return local


def solution(mesh):
    rows = P(("batch", "heads"), None, None)
    first, second = P(("batch", "heads"), None), P(None, ("batch", "heads"))
    grads = (first, first, first, second, first, second, second, second)
    return jax.shard_map(
        make_local(mesh),
        mesh=mesh,
        in_specs=(rows, rows, P("batch"), P("batch"), *[P()] * 16, rows, rows),
        out_specs=(rows, rows, rows, rows, *grads, *grads),
        check_vma=False,
    )
```
